512 devices in a mesh: gx: 16 (over x, z_hi, core), gy: 32 (over z_lo, y).
Axes of the slice: x: 4, y: 4, z: 16 (z_hi: 2, z_lo: 8; z = z_hi * 8 + z_lo), core: 2. Of those that a mesh axis runs over, the one named last changes fastest.
Arguments:
- damage: float32 [256, 256, 512], P('gx', 'gy'), may hold values from 0 to 0.9
- strain: float32 [3, 256, 256, 512], P(None, 'gx', 'gy'), may hold values from -3 to 3
- seed_damage: float32 [256, 256, 512], P('gx', 'gy'), may hold values from -6 to 6
- seed_disp: float32 [3, 256, 256, 512], P(None, 'gx', 'gy'), may hold values from -6 to 6
- brick_work: int32 [16, 32], P('gx', 'gy'), may hold values from 1 to 4, as said below
Outputs:
- adjoint_damage: float32 [256, 256, 512], P('gx', 'gy')
- adjoint_disp: float32 [3, 256, 256, 512], P(None, 'gx', 'gy')
The draws below stay inside these ranges and needn't reach their ends.
Inputs may be any that keep to these rules, and one draw needn't show every extreme that they name: brick_work is 1 on ordinary bricks and 2 to 4 on crack-band bricks. In every row of bricks (one gx index) the crack-band bricks form one run of 8 neighbouring bricks, all with gy index below 16. Some brick has weight 4.
All inputs are finite; a program needn't handle non-finite values.
Results may differ from the reference program's by a relative error of at most 0.0001.
Values sent between devices are 32-bit elements; how exact they have to be, the bound alone decides.
A program may use at most 64 MiB of HBM per device.

```python
import jax
import jax.numpy as jnp
from jax import lax

CX = 16
CY = 8
SWEEPS = 3
WORK_MAX = 4
RELAX_INNER = 8
NX = 256
NY = 256
NZ = 512
BRICKS_X = 16
BRICKS_Y = 32


def draw_brick_work(key, part):
    start_key = jax.random.fold_in(key, 11)
    load_key = jax.random.fold_in(key, 23)
    band = BRICKS_Y // 4
    starts = jax.random.randint(start_key, (BRICKS_X,), 0, band + 1)
    columns = jnp.arange(BRICKS_Y)[None, :]
    inside = (columns >= starts[:, None]) & (columns < starts[:, None] + band)
    loads = jax.random.randint(load_key, (BRICKS_X, BRICKS_Y), 2, WORK_MAX + 1)
    first_row = jnp.arange(BRICKS_X)[:, None] == 0
    loads = jnp.where(first_row & (columns == starts[0]), WORK_MAX, loads)
    return jnp.where(inside, loads, 1).astype(jnp.int32)


def levels(key, shape, split, smallest, largest):
    factor_of = 1.0
    for position, blocks in split:
        steps = jax.random.uniform(jax.random.fold_in(jax.random.fold_in(key, 6), position), (blocks,), jnp.float32, smallest / len(split), largest / len(split))
        factor_of = factor_of * jnp.repeat(jnp.exp(steps), shape[position] // blocks).reshape((-1,) + (1,) * (len(shape) - 1 - position))
    return factor_of


def bell_draw(own_key, shape, scale, bound, cuts=(), held_as=jnp.bfloat16):
    drawn = jax.random.normal(own_key, shape, jnp.float32) * scale
    if len(cuts) > 0:
        drawn = levels(own_key, shape, cuts, -0.22, 0.18) * drawn
    return jnp.clip(drawn, min=-bound, max=bound).astype(held_as)


def setup_inputs(seed: int = 0) -> dict:
    seeds = jax.random.split(jax.random.key(seed), 6)
    return {
        "damage": jnp.clip(0.9 * jax.random.uniform(seeds[0], (NX, NY, NZ), jnp.float32) ** levels(seeds[0], (NX, NY, NZ), ((0, 16), (1, 32)), -0.2, 0.2), 0.0, 0.9),
        "strain": bell_draw(seeds[1], (3, NX, NY, NZ), 0.5, 3.0, ((1, 16), (2, 32)), jnp.float32),
        "seed_damage": bell_draw(seeds[2], (NX, NY, NZ), 1.0, 6.0, ((0, 16), (1, 32)), jnp.float32),
        "seed_disp": bell_draw(seeds[3], (3, NX, NY, NZ), 1.0, 6.0, ((1, 16), (2, 32)), jnp.float32),
        "brick_work": draw_brick_work(jax.random.fold_in(seeds[5], 71), 0),
    }


RESIDUAL_STIFFNESS = 0.001
TOUGH_OVER_LENGTH = 0.5
TOUGH_TIMES_LENGTH = 0.25
MASS_SHIFT = 0.5
STIFF_SCALE = 0.25
CENTER_VALUE = 1.0
HALF_WIDTH = 0.75
NORMAL_WEIGHT = 1.5
RELAX_STEP = 0.5
NORMAL_FLOOR = 0.05

def shifted(field):
    center = field[..., 1:-1, 1:-1, :]
    widths = [(0, 0)] * (center.ndim - 1) + [(1, 1)]
    padded = jnp.pad(center, widths)
    sides = [field[..., 2:, 1:-1, :], field[..., :-2, 1:-1, :], field[..., 1:-1, 2:, :], field[..., 1:-1, :-2, :], padded[..., 2:], padded[..., :-2]]
    return (center, sides)

def prepare(framed_damage, framed_strain):
    center, sides = shifted(framed_damage)
    soft_center = (1.0 - center) ** 2 + RESIDUAL_STIFFNESS
    faces = jnp.stack([0.5 * (soft_center + (1.0 - side) ** 2 + RESIDUAL_STIFFNESS) for side in sides])
    energy = 0.5 * lax.optimization_barrier(jnp.sum(framed_strain[:, 1:-1, 1:-1, :] ** 2, axis=0))
    coupling = 2.0 * (framed_damage - 1.0)[None] * framed_strain
    inverse_damage = 1.0 / (TOUGH_OVER_LENGTH + 2.0 * energy + 6.0 * TOUGH_TIMES_LENGTH)
    inverse_disp = 1.0 / (MASS_SHIFT + STIFF_SCALE * lax.optimization_barrier(jnp.sum(faces, axis=0)))
    inverse = jnp.stack([inverse_damage, inverse_disp, inverse_disp, inverse_disp])
    return (faces, energy, coupling, inverse)

def operate(faces, energy, coupling, state):
    mu_center, mu_sides = shifted(state[0])
    damage_part = (TOUGH_OVER_LENGTH + 2.0 * energy) * mu_center + TOUGH_TIMES_LENGTH * sum((mu_center - side for side in mu_sides))
    lam_center, lam_sides = shifted(state[1:])
    disp_part = MASS_SHIFT * lam_center + STIFF_SCALE * sum((faces[slot] * (lam_center - lam_sides[slot]) for slot in range(6)))
    weighted = coupling * state[0][None]
    along_x = 0.5 * (weighted[0, :-2, 1:-1, :] - weighted[0, 2:, 1:-1, :])
    along_y = 0.5 * (weighted[1, 1:-1, :-2, :] - weighted[1, 1:-1, 2:, :])
    padded = jnp.pad(weighted[2, 1:-1, 1:-1, :], ((0, 0), (0, 0), (1, 1)))
    along_z = 0.5 * (padded[..., :-2] - padded[..., 2:])
    transfer = jnp.stack([along_x, along_y, along_z])
    return jnp.concatenate([damage_part[None], disp_part + transfer], axis=0)

def chebyshev(faces, energy, coupling, inverse, source, widen, keep):
    ratio = CENTER_VALUE / HALF_WIDTH
    rho = 1.0 / ratio
    update = inverse * source / CENTER_VALUE
    state = keep(update)
    for sweep in range(SWEEPS):
        residual = source - operate(faces, energy, coupling, widen(state))
        rho_next = 1.0 / (2.0 * ratio - rho)
        update = rho_next * rho * update + 2.0 * rho_next / HALF_WIDTH * inverse * residual
        state = keep(state + update)
        rho = rho_next
    return state

def crack_normal(framed_damage):
    center, sides = shifted(framed_damage)
    grad = jnp.stack([0.5 * (sides[0] - sides[1]), 0.5 * (sides[2] - sides[3]), 0.5 * (sides[4] - sides[5])])
    length = jnp.sqrt(jnp.maximum(lax.optimization_barrier(jnp.sum(grad * grad, axis=0, keepdims=True)), NORMAL_FLOOR))
    return grad / length

def relax_once(target, normal, relaxed):
    along = lax.optimization_barrier(jnp.sum(normal * relaxed, axis=0, keepdims=True))
    return relaxed + RELAX_STEP / RELAX_INNER * (target - relaxed - NORMAL_WEIGHT * along * normal)

def widen_zero(state):
    return jnp.pad(state, ((0, 0), (1, 1), (1, 1), (0, 0)))

def unchanged(state):
    return state

def reference(damage, strain, seed_damage, seed_disp, brick_work):
    framed_damage = jnp.pad(damage, ((1, 1), (1, 1), (0, 0)))
    framed_strain = jnp.pad(strain, ((0, 0), (1, 1), (1, 1), (0, 0)))
    faces, energy, coupling, inverse = prepare(framed_damage, framed_strain)
    source = jnp.concatenate([seed_damage[None], seed_disp], axis=0)
    state = chebyshev(faces, energy, coupling, inverse, source, widen_zero, unchanged)
    normal = crack_normal(framed_damage)
    counts = jnp.repeat(jnp.repeat(brick_work * RELAX_INNER, CX, axis=0), CY, axis=1)[:, :, None]
    target = state[1:]

    def advance(level, relaxed):
        moved = relax_once(target, normal, relaxed)
        return jnp.where(level < counts, moved, relaxed)
    relaxed = lax.fori_loop(0, WORK_MAX * RELAX_INNER, advance, target)
    return (state[0], relaxed)
```

```python
import jax
import jax.numpy as jnp
from jax import lax
from jax.sharding import PartitionSpec as P

SWEEPS = 3
RELAX_INNER = 8


RESIDUAL_STIFFNESS = 0.001
TOUGH_OVER_LENGTH = 0.5
TOUGH_TIMES_LENGTH = 0.25
MASS_SHIFT = 0.5
STIFF_SCALE = 0.25
CENTER_VALUE = 1.0
HALF_WIDTH = 0.75
NORMAL_WEIGHT = 1.5
RELAX_STEP = 0.5
NORMAL_FLOOR = 0.05


def neighbours(block, axis, dim):
    count = lax.axis_size(axis)
    forward = [(i, i + 1) for i in range(count - 1)]
    backward = [(target, source) for source, target in forward]
    width = block.shape[dim]
    low = lax.ppermute(lax.slice_in_dim(block, width - 1, None, axis=dim), axis, forward)
    high = lax.ppermute(lax.slice_in_dim(block, 0, 1, axis=dim), axis, backward)
    return low, high


def frame(block, xs, ys):
    lead = block.ndim - 3
    xlo, xhi = xs
    ylo, yhi = ys
    mid = jnp.concatenate([xlo, block, xhi], axis=lead)
    widths = [(0, 0)] * lead + [(1, 1), (0, 0), (0, 0)]
    ylo = jnp.pad(ylo, widths)
    yhi = jnp.pad(yhi, widths)
    return jnp.concatenate([ylo, mid, yhi], axis=lead + 1)


def framed_state(state):
    xs = neighbours(state, "gx", 1)
    ys = neighbours(state, "gy", 2)
    return frame(state, xs, ys)


def shifted(field):
    center = field[..., 1:-1, 1:-1, :]
    widths = [(0, 0)] * (center.ndim - 1) + [(1, 1)]
    padded = jnp.pad(center, widths)
    sides = [
        field[..., 2:, 1:-1, :],
        field[..., :-2, 1:-1, :],
        field[..., 1:-1, 2:, :],
        field[..., 1:-1, :-2, :],
        padded[..., 2:],
        padded[..., :-2],
    ]
    return (center, sides)


def prepare(framed_damage, framed_strain):
    center, sides = shifted(framed_damage)
    soft_center = (1.0 - center) ** 2 + RESIDUAL_STIFFNESS
    faces = jnp.stack(
        [0.5 * (soft_center + (1.0 - side) ** 2 + RESIDUAL_STIFFNESS) for side in sides]
    )
    energy = 0.5 * jnp.sum(framed_strain[:, 1:-1, 1:-1, :] ** 2, axis=0)
    coupling = 2.0 * (framed_damage - 1.0)[None] * framed_strain
    inverse_damage = 1.0 / (TOUGH_OVER_LENGTH + 2.0 * energy + 6.0 * TOUGH_TIMES_LENGTH)
    inverse_disp = 1.0 / (MASS_SHIFT + STIFF_SCALE * jnp.sum(faces, axis=0))
    inverse = jnp.stack([inverse_damage, inverse_disp, inverse_disp, inverse_disp])
    return (faces, energy, coupling, inverse)


def operate(faces, energy, coupling, state):
    mu_center, mu_sides = shifted(state[0])
    damage_part = (TOUGH_OVER_LENGTH + 2.0 * energy) * mu_center + TOUGH_TIMES_LENGTH * sum(
        (mu_center - side for side in mu_sides)
    )
    lam_center, lam_sides = shifted(state[1:])
    disp_part = MASS_SHIFT * lam_center + STIFF_SCALE * sum(
        (faces[slot] * (lam_center - lam_sides[slot]) for slot in range(6))
    )
    weighted = coupling * state[0][None]
    along_x = 0.5 * (weighted[0, :-2, 1:-1, :] - weighted[0, 2:, 1:-1, :])
    along_y = 0.5 * (weighted[1, 1:-1, :-2, :] - weighted[1, 1:-1, 2:, :])
    padded = jnp.pad(weighted[2, 1:-1, 1:-1, :], ((0, 0), (0, 0), (1, 1)))
    along_z = 0.5 * (padded[..., :-2] - padded[..., 2:])
    transfer = jnp.stack([along_x, along_y, along_z])
    return jnp.concatenate([damage_part[None], disp_part + transfer], axis=0)


def chebyshev(faces, energy, coupling, inverse, source, widen):
    ratio = CENTER_VALUE / HALF_WIDTH
    rho = 1.0 / ratio
    update = inverse * source / CENTER_VALUE
    state = update
    for sweep in range(SWEEPS):
        residual = source - operate(faces, energy, coupling, widen(state))
        rho_next = 1.0 / (2.0 * ratio - rho)
        update = rho_next * rho * update + 2.0 * rho_next / HALF_WIDTH * inverse * residual
        state = state + update
        rho = rho_next
    return state


def crack_normal(framed_damage):
    center, sides = shifted(framed_damage)
    grad = jnp.stack(
        [0.5 * (sides[0] - sides[1]), 0.5 * (sides[2] - sides[3]), 0.5 * (sides[4] - sides[5])]
    )
    length = jnp.sqrt(jnp.maximum(jnp.sum(grad * grad, axis=0, keepdims=True), NORMAL_FLOOR))
    return grad / length


def relax(target, normal, count):
    step = RELAX_STEP / RELAX_INNER
    size = jnp.sum(normal * normal, axis=0, keepdims=True)
    along = jnp.sum(normal * target, axis=0, keepdims=True)
    factor = 1.0 - step * (1.0 + NORMAL_WEIGHT * size)
    power = factor
    for _ in range(3):
        power = power * power
    base = power
    total = power
    for level in range(2, 5):
        total = jnp.where(count >= level, total * base, total)
    gain = NORMAL_WEIGHT * (1.0 - total) / (1.0 + NORMAL_WEIGHT * size)
    return target - (gain * along) * normal


def body(damage, strain, seed_damage, seed_disp, brick_work):
    pair_x = jnp.stack([damage, strain[0]])
    pair_y = jnp.stack([damage, strain[1]])
    xlo, xhi = neighbours(pair_x, "gx", 1)
    ylo, yhi = neighbours(pair_y, "gy", 2)
    framed_damage = frame(damage, (xlo[0], xhi[0]), (ylo[0], yhi[0]))
    zero_x = jnp.zeros_like(xlo[1])
    zero_y = jnp.zeros_like(ylo[1])
    strain_x = frame(strain[0], (xlo[1], xhi[1]), (zero_y, zero_y))
    strain_y = frame(strain[1], (zero_x, zero_x), (ylo[1], yhi[1]))
    strain_z = jnp.pad(strain[2], ((1, 1), (1, 1), (0, 0)))
    framed_strain = jnp.stack([strain_x, strain_y, strain_z])
    faces, energy, coupling, inverse = prepare(framed_damage, framed_strain)
    source = jnp.concatenate([seed_damage[None], seed_disp], axis=0)
    state = chebyshev(faces, energy, coupling, inverse, source, framed_state)
    normal = crack_normal(framed_damage)
    corrected = relax(state[1:], normal, brick_work[0, 0])
    return (state[0], corrected)


def solution(mesh):
    placed = (
        P("gx", "gy", None),
        P(None, "gx", "gy", None),
        P("gx", "gy", None),
        P(None, "gx", "gy", None),
        P("gx", "gy"),
    )
    return jax.shard_map(
        body,
        mesh=mesh,
        in_specs=placed,
        out_specs=(P("gx", "gy", None), P(None, "gx", "gy", None)),
        check_vma=False,
    )
```

```python
import functools

import jax
import jax.numpy as jnp
from jax import lax
from jax.experimental import pallas as pl
from jax.experimental.pallas import tpu as pltpu
from jax.sharding import PartitionSpec as P

SWEEPS = 3
RELAX_INNER = 8

RESIDUAL_STIFFNESS = 0.001
TOUGH_OVER_LENGTH = 0.5
TOUGH_TIMES_LENGTH = 0.25
MASS_SHIFT = 0.5
STIFF_SCALE = 0.25
CENTER_VALUE = 1.0
HALF_WIDTH = 0.75
NORMAL_WEIGHT = 1.5
RELAX_STEP = 0.5
NORMAL_FLOOR = 0.05

MESH = pl.DeviceIdType.MESH


def soft_of(d):
    return (1.0 - d) ** 2


def kernel(
    nx, ny,
    bw_ref, dmg_ref, strain_ref, sd_ref, sdisp_ref,
    out_mu_ref, out_disp_ref,
    dfr, dyl, dyh, sfr, syl, syh, faces, upd, invs, send_sem, recv_sem,
):
    X, Y, Z = dmg_ref.shape
    bx = lax.axis_index("gx")
    by = lax.axis_index("gy")
    has = (bx < nx - 1, bx > 0, by < ny - 1, by > 0)
    peers = ((bx + 1, by), (bx - 1, by), (bx, by + 1), (bx, by - 1))

    @pl.when(bx == 0)
    def _():
        dfr[:, 0] = jnp.zeros((2, Y, Z), jnp.float32)
        sfr[:, :, 0] = jnp.zeros((SWEEPS, 4, Y, Z), jnp.float32)

    @pl.when(bx == nx - 1)
    def _():
        dfr[:, X + 1] = jnp.zeros((2, Y, Z), jnp.float32)
        sfr[:, :, X + 1] = jnp.zeros((SWEEPS, 4, Y, Z), jnp.float32)

    @pl.when(by == 0)
    def _():
        dyl[...] = jnp.zeros(dyl.shape, jnp.float32)
        syl[...] = jnp.zeros(syl.shape, jnp.float32)

    @pl.when(by == ny - 1)
    def _():
        dyh[...] = jnp.zeros(dyh.shape, jnp.float32)
        syh[...] = jnp.zeros(syh.shape, jnp.float32)

    barrier = pltpu.get_barrier_semaphore()
    count = jnp.int32(0)
    for d in range(4):
        @pl.when(has[d])
        def _():
            pl.semaphore_signal(barrier, inc=1, device_id=peers[d], device_id_type=MESH)
        count = count + has[d].astype(jnp.int32)
    pl.semaphore_wait(barrier, count)

    def exchange(slot, routes):
        copies = []
        for d in range(4):
            src, dst = routes[d]
            copies.append(
                pltpu.make_async_remote_copy(
                    src_ref=src, dst_ref=dst,
                    send_sem=send_sem.at[slot, d], recv_sem=recv_sem.at[slot, d],
                    device_id=peers[d], device_id_type=MESH,
                )
            )
        for d in range(4):
            @pl.when(has[d])
            def _():
                copies[d].start()
        return copies

    def finish(copies):
        opposite = (1, 0, 3, 2)
        for d in range(4):
            @pl.when(has[d])
            def _():
                copies[d].wait_send()

            @pl.when(has[opposite[d]])
            def _():
                copies[d].wait_recv()

    c_dmg = exchange(0, (
        (dmg_ref.at[X - 1:X], dfr.at[0, 0:1]),
        (dmg_ref.at[0:1], dfr.at[0, X + 1:X + 2]),
        (dmg_ref.at[:, Y - 1:Y], dyl.at[0]),
        (dmg_ref.at[:, 0:1], dyh.at[0]),
    ))
    c_str = exchange(1, (
        (strain_ref.at[0, X - 1:X], dfr.at[1, 0:1]),
        (strain_ref.at[0, 0:1], dfr.at[1, X + 1:X + 2]),
        (strain_ref.at[1, :, Y - 1:Y], dyl.at[1]),
        (strain_ref.at[1, :, 0:1], dyh.at[1]),
    ))
    dfr[0, 1:X + 1] = dmg_ref[...]
    dfr[1, 1:X + 1] = strain_ref[0]
    finish(c_dmg)
    finish(c_str)

    rows = lax.broadcasted_iota(jnp.int32, (Y, Z), 0)
    lanes = lax.broadcasted_iota(jnp.int32, (Y, Z), 1)

    def sides(center, nxp, nxm, lo, hi):
        yp = jnp.where(rows == Y - 1, hi, pltpu.roll(center, Y - 1, 0))
        ym = jnp.where(rows == 0, lo, pltpu.roll(center, 1, 0))
        zp = jnp.where(lanes == Z - 1, 0.0, pltpu.roll(center, Z - 1, 1))
        zm = jnp.where(lanes == 0, 0.0, pltpu.roll(center, 1, 1))
        return [nxp, nxm, yp, ym, zp, zm]

    def damage_sides(i):
        d = dfr[0, i + 1]
        return d, sides(d, dfr[0, i + 2], dfr[0, i], dyl[0, i], dyh[0, i])

    def prep(i, carry):
        d, ds = damage_sides(i)
        soft_center = soft_of(d) + RESIDUAL_STIFFNESS
        fs = [0.5 * (soft_center + soft_of(s) + RESIDUAL_STIFFNESS) for s in ds]
        total = fs[0]
        for k in range(6):
            faces[k, i] = fs[k]
            if k:
                total = total + fs[k]
        sx = strain_ref[0, i]
        sy = strain_ref[1, i]
        sz = strain_ref[2, i]
        energy = 0.5 * (sx * sx + sy * sy + sz * sz)
        inv_mu = 1.0 / (TOUGH_OVER_LENGTH + 2.0 * energy + 6.0 * TOUGH_TIMES_LENGTH)
        inv_lam = 1.0 / (MASS_SHIFT + STIFF_SCALE * total)
        invs[0, i] = inv_mu
        invs[1, i] = inv_lam
        invs[2, i] = TOUGH_OVER_LENGTH + 2.0 * energy
        mu0 = inv_mu * sd_ref[i] / CENTER_VALUE
        upd[0, i] = mu0
        sfr[0, 0, i + 1] = mu0
        for c in range(3):
            lam0 = inv_lam * sdisp_ref[c, i] / CENTER_VALUE
            upd[1 + c, i] = lam0
            sfr[0, 1 + c, i + 1] = lam0
        return carry

    lax.fori_loop(0, X, prep, 0)

    def state_routes(r):
        return (
            (sfr.at[r, :, X:X + 1], sfr.at[r, :, 0:1]),
            (sfr.at[r, :, 1:2], sfr.at[r, :, X + 1:X + 2]),
            (sfr.at[r, :, 1:X + 1, Y - 1:Y], syl.at[r]),
            (sfr.at[r, :, 1:X + 1, 0:1], syh.at[r]),
        )

    ratio = CENTER_VALUE / HALF_WIDTH
    rho = 1.0 / ratio
    for sweep in range(SWEEPS):
        r = sweep
        copies = exchange(2 + r, state_routes(r))
        finish(copies)
        rho_next = 1.0 / (2.0 * ratio - rho)
        keep = rho_next * rho
        gain = 2.0 * rho_next / HALF_WIDTH
        rho = rho_next
        last = sweep == SWEEPS - 1

        def step(i, carry, r=r, keep=keep, gain=gain, last=last):
            mu = sfr[r, 0, i + 1]
            mus = sides(mu, sfr[r, 0, i + 2], sfr[r, 0, i], syl[r, 0, i], syh[r, 0, i])
            energy_diag = invs[2, i]
            damage_part = energy_diag * mu + TOUGH_TIMES_LENGTH * sum(mu - s for s in mus)
            fs = [faces[k, i] for k in range(6)]
            wxm = 2.0 * (dfr[0, i] - 1.0) * dfr[1, i] * mus[1]
            wxp = 2.0 * (dfr[0, i + 2] - 1.0) * dfr[1, i + 2] * mus[0]
            d = dfr[0, i + 1]
            wy = 2.0 * (d - 1.0) * strain_ref[1, i] * mu
            wy_lo = 2.0 * (dyl[0, i] - 1.0) * dyl[1, i] * syl[r, 0, i]
            wy_hi = 2.0 * (dyh[0, i] - 1.0) * dyh[1, i] * syh[r, 0, i]
            wy_p = jnp.where(rows == Y - 1, wy_hi, pltpu.roll(wy, Y - 1, 0))
            wy_m = jnp.where(rows == 0, wy_lo, pltpu.roll(wy, 1, 0))
            wz = 2.0 * (d - 1.0) * strain_ref[2, i] * mu
            wz_p = jnp.where(lanes == Z - 1, 0.0, pltpu.roll(wz, Z - 1, 1))
            wz_m = jnp.where(lanes == 0, 0.0, pltpu.roll(wz, 1, 1))
            transfer = (
                0.5 * (wxm - wxp),
                0.5 * (wy_m - wy_p),
                0.5 * (wz_m - wz_p),
            )
            inv_mu = invs[0, i]
            inv_lam = invs[1, i]
            residual_mu = sd_ref[i] - damage_part
            new_upd = keep * upd[0, i] + gain * inv_mu * residual_mu
            new_mu = mu + new_upd
            upd[0, i] = new_upd
            lams = []
            for c in range(3):
                lam = sfr[r, 1 + c, i + 1]
                ls = sides(lam, sfr[r, 1 + c, i + 2], sfr[r, 1 + c, i],
                           syl[r, 1 + c, i], syh[r, 1 + c, i])
                disp = MASS_SHIFT * lam + STIFF_SCALE * sum(
                    fs[k] * (lam - ls[k]) for k in range(6))
                residual = sdisp_ref[c, i] - (disp + transfer[c])
                nu = keep * upd[1 + c, i] + gain * inv_lam * residual
                upd[1 + c, i] = nu
                lams.append(lam + nu)
            if not last:
                sfr[r + 1, 0, i + 1] = new_mu
                for c in range(3):
                    sfr[r + 1, 1 + c, i + 1] = lams[c]
            else:
                out_mu_ref[i] = new_mu
                _, ds = damage_sides(i)
                grad = [0.5 * (ds[0] - ds[1]), 0.5 * (ds[2] - ds[3]), 0.5 * (ds[4] - ds[5])]
                length = jnp.sqrt(jnp.maximum(
                    grad[0] * grad[0] + grad[1] * grad[1] + grad[2] * grad[2], NORMAL_FLOOR))
                normal = [g / length for g in grad]
                size = normal[0] * normal[0] + normal[1] * normal[1] + normal[2] * normal[2]
                along = normal[0] * lams[0] + normal[1] * lams[1] + normal[2] * lams[2]
                a = RELAX_STEP / RELAX_INNER
                factor = 1.0 - a * (1.0 + NORMAL_WEIGHT * size)
                power = factor
                for _ in range(3):
                    power = power * power
                total = power
                work = bw_ref[0, 0]
                for level in range(2, 5):
                    total = jnp.where(work >= level, total * power, total)
                pull = NORMAL_WEIGHT * (1.0 - total) / (1.0 + NORMAL_WEIGHT * size)
                for c in range(3):
                    out_disp_ref[c, i] = lams[c] - (pull * along) * normal[c]
            return carry

        lax.fori_loop(0, X, step, 0)


def body(damage, strain, seed_damage, seed_disp, brick_work, nx, ny):
    X, Y, Z = damage.shape
    f32 = jnp.float32
    vmem = pl.BlockSpec(memory_space=pltpu.VMEM)
    return pl.pallas_call(
        functools.partial(kernel, nx, ny),
        out_shape=(
            jax.ShapeDtypeStruct((X, Y, Z), f32),
            jax.ShapeDtypeStruct((3, X, Y, Z), f32),
        ),
        in_specs=[pl.BlockSpec(memory_space=pltpu.SMEM), vmem, vmem, vmem, vmem],
        out_specs=(vmem, vmem),
        scratch_shapes=[
            pltpu.VMEM((2, X + 2, Y, Z), f32),
            pltpu.VMEM((2, X, 1, Z), f32),
            pltpu.VMEM((2, X, 1, Z), f32),
            pltpu.VMEM((SWEEPS, 4, X + 2, Y, Z), f32),
            pltpu.VMEM((SWEEPS, 4, X, 1, Z), f32),
            pltpu.VMEM((SWEEPS, 4, X, 1, Z), f32),
            pltpu.VMEM((6, X, Y, Z), f32),
            pltpu.VMEM((4, X, Y, Z), f32),
            pltpu.VMEM((3, X, Y, Z), f32),
            pltpu.SemaphoreType.DMA((2 + SWEEPS, 4)),
            pltpu.SemaphoreType.DMA((2 + SWEEPS, 4)),
        ],
        compiler_params=pltpu.CompilerParams(
            collective_id=0, has_side_effects=True, vmem_limit_bytes=60 * 1024 * 1024
        ),
    )(brick_work, damage, strain, seed_damage, seed_disp)


def solution(mesh):
    nx = mesh.shape["gx"]
    ny = mesh.shape["gy"]
    placed = (
        P("gx", "gy", None),
        P(None, "gx", "gy", None),
        P("gx", "gy", None),
        P(None, "gx", "gy", None),
        P("gx", "gy"),
    )
    return jax.shard_map(
        functools.partial(body, nx=nx, ny=ny),
        mesh=mesh,
        in_specs=placed,
        out_specs=(P("gx", "gy", None), P(None, "gx", "gy", None)),
        check_vma=False,
    )
```

```python
import functools

import jax
import jax.numpy as jnp
from jax import lax
from jax.experimental import pallas as pl
from jax.experimental.pallas import tpu as pltpu
from jax.sharding import PartitionSpec as P

SWEEPS = 3
RELAX_INNER = 8

RESIDUAL_STIFFNESS = 0.001
TOUGH_OVER_LENGTH = 0.5
TOUGH_TIMES_LENGTH = 0.25
MASS_SHIFT = 0.5
STIFF_SCALE = 0.25
CENTER_VALUE = 1.0
HALF_WIDTH = 0.75
NORMAL_WEIGHT = 1.5
RELAX_STEP = 0.5
NORMAL_FLOOR = 0.05

MESH = pl.DeviceIdType.MESH


def soft_of(d):
    return (1.0 - d) ** 2


def kernel(
    nx, ny,
    bw_ref, dmg_ref, strain_ref, sd_ref, sdisp_ref,
    out_mu_ref, out_disp_ref,
    dfr, dyl, dyh, sfr, syl, syh, faces, upd, invs, send_sem, recv_sem,
):
    X, Y, Z = dmg_ref.shape
    bx = lax.axis_index("gx")
    by = lax.axis_index("gy")
    has = (bx < nx - 1, bx > 0, by < ny - 1, by > 0)
    peers = ((bx + 1, by), (bx - 1, by), (bx, by + 1), (bx, by - 1))

    @pl.when(bx == 0)
    def _():
        dfr[:, 0] = jnp.zeros((2, Y, Z), jnp.float32)
        sfr[:, :, 0] = jnp.zeros((SWEEPS, 4, Y, Z), jnp.float32)

    @pl.when(bx == nx - 1)
    def _():
        dfr[:, X + 1] = jnp.zeros((2, Y, Z), jnp.float32)
        sfr[:, :, X + 1] = jnp.zeros((SWEEPS, 4, Y, Z), jnp.float32)

    @pl.when(by == 0)
    def _():
        dyl[...] = jnp.zeros(dyl.shape, jnp.float32)
        syl[...] = jnp.zeros(syl.shape, jnp.float32)

    @pl.when(by == ny - 1)
    def _():
        dyh[...] = jnp.zeros(dyh.shape, jnp.float32)
        syh[...] = jnp.zeros(syh.shape, jnp.float32)

    barrier = pltpu.get_barrier_semaphore()
    count = jnp.int32(0)
    for d in range(4):
        @pl.when(has[d])
        def _():
            pl.semaphore_signal(barrier, inc=1, device_id=peers[d], device_id_type=MESH)
        count = count + has[d].astype(jnp.int32)
    pl.semaphore_wait(barrier, count)

    def exchange(slot, routes):
        copies = []
        for d in range(4):
            src, dst = routes[d]
            copies.append(
                pltpu.make_async_remote_copy(
                    src_ref=src, dst_ref=dst,
                    send_sem=send_sem.at[slot, d], recv_sem=recv_sem.at[slot, d],
                    device_id=peers[d], device_id_type=MESH,
                )
            )
        for d in range(4):
            @pl.when(has[d])
            def _():
                copies[d].start()
        return copies

    def arrive(copies, dirs):
        opposite = (1, 0, 3, 2)
        for d in dirs:
            @pl.when(has[opposite[d]])
            def _():
                copies[d].wait_recv()

    def sent(copies):
        for d in range(4):
            @pl.when(has[d])
            def _():
                copies[d].wait_send()

    c_dmg = exchange(0, (
        (dmg_ref.at[X - 1:X], dfr.at[0, 0:1]),
        (dmg_ref.at[0:1], dfr.at[0, X + 1:X + 2]),
        (dmg_ref.at[:, Y - 1:Y], dyl.at[0]),
        (dmg_ref.at[:, 0:1], dyh.at[0]),
    ))
    c_str = exchange(1, (
        (strain_ref.at[0, X - 1:X], dfr.at[1, 0:1]),
        (strain_ref.at[0, 0:1], dfr.at[1, X + 1:X + 2]),
        (strain_ref.at[1, :, Y - 1:Y], dyl.at[1]),
        (strain_ref.at[1, :, 0:1], dyh.at[1]),
    ))
    dfr[0, 1:X + 1] = dmg_ref[...]
    dfr[1, 1:X + 1] = strain_ref[0]
    arrive(c_dmg, (2, 3))
    arrive(c_str, (2, 3))
    pending = [c_dmg, c_str]

    rows = lax.broadcasted_iota(jnp.int32, (Y, Z), 0)
    lanes = lax.broadcasted_iota(jnp.int32, (Y, Z), 1)

    def sides(center, nxp, nxm, lo, hi):
        yp = jnp.where(rows == Y - 1, hi, pltpu.roll(center, Y - 1, 0))
        ym = jnp.where(rows == 0, lo, pltpu.roll(center, 1, 0))
        zp = jnp.where(lanes == Z - 1, 0.0, pltpu.roll(center, Z - 1, 1))
        zm = jnp.where(lanes == 0, 0.0, pltpu.roll(center, 1, 1))
        return [nxp, nxm, yp, ym, zp, zm]

    def damage_sides(i):
        d = dfr[0, i + 1]
        return d, sides(d, dfr[0, i + 2], dfr[0, i], dyl[0, i], dyh[0, i])

    def prep(i, carry):
        d, ds = damage_sides(i)
        soft_center = soft_of(d) + RESIDUAL_STIFFNESS
        fs = [0.5 * (soft_center + soft_of(s) + RESIDUAL_STIFFNESS) for s in ds]
        total = fs[0]
        for k in range(6):
            faces[k, i] = fs[k]
            if k:
                total = total + fs[k]
        sx = strain_ref[0, i]
        sy = strain_ref[1, i]
        sz = strain_ref[2, i]
        energy = 0.5 * (sx * sx + sy * sy + sz * sz)
        inv_mu = 1.0 / (TOUGH_OVER_LENGTH + 2.0 * energy + 6.0 * TOUGH_TIMES_LENGTH)
        inv_lam = 1.0 / (MASS_SHIFT + STIFF_SCALE * total)
        invs[0, i] = inv_mu
        invs[1, i] = inv_lam
        invs[2, i] = TOUGH_OVER_LENGTH + 2.0 * energy
        mu0 = inv_mu * sd_ref[i] / CENTER_VALUE
        upd[0, i] = mu0
        sfr[0, 0, i + 1] = mu0
        for c in range(3):
            lam0 = inv_lam * sdisp_ref[c, i] / CENTER_VALUE
            upd[1 + c, i] = lam0
            sfr[0, 1 + c, i + 1] = lam0
        return carry

    lax.fori_loop(1, X - 1, prep, 0)
    arrive(c_dmg, (0, 1))
    arrive(c_str, (0, 1))
    for i in (0, X - 1):
        prep(i, 0)

    def state_routes(r):
        return (
            (sfr.at[r, :, X:X + 1], sfr.at[r, :, 0:1]),
            (sfr.at[r, :, 1:2], sfr.at[r, :, X + 1:X + 2]),
            (sfr.at[r, :, 1:X + 1, Y - 1:Y], syl.at[r]),
            (sfr.at[r, :, 1:X + 1, 0:1], syh.at[r]),
        )

    ratio = CENTER_VALUE / HALF_WIDTH
    rho = 1.0 / ratio
    for sweep in range(SWEEPS):
        r = sweep
        copies = exchange(2 + r, state_routes(r))
        pending.append(copies)
        arrive(copies, (2, 3))
        rho_next = 1.0 / (2.0 * ratio - rho)
        keep = rho_next * rho
        gain = 2.0 * rho_next / HALF_WIDTH
        rho = rho_next
        last = sweep == SWEEPS - 1

        def step(i, carry, r=r, keep=keep, gain=gain, last=last):
            mu = sfr[r, 0, i + 1]
            mus = sides(mu, sfr[r, 0, i + 2], sfr[r, 0, i], syl[r, 0, i], syh[r, 0, i])
            energy_diag = invs[2, i]
            damage_part = energy_diag * mu + TOUGH_TIMES_LENGTH * sum(mu - s for s in mus)
            fs = [faces[k, i] for k in range(6)]
            wxm = 2.0 * (dfr[0, i] - 1.0) * dfr[1, i] * mus[1]
            wxp = 2.0 * (dfr[0, i + 2] - 1.0) * dfr[1, i + 2] * mus[0]
            d = dfr[0, i + 1]
            wy = 2.0 * (d - 1.0) * strain_ref[1, i] * mu
            wy_lo = 2.0 * (dyl[0, i] - 1.0) * dyl[1, i] * syl[r, 0, i]
            wy_hi = 2.0 * (dyh[0, i] - 1.0) * dyh[1, i] * syh[r, 0, i]
            wy_p = jnp.where(rows == Y - 1, wy_hi, pltpu.roll(wy, Y - 1, 0))
            wy_m = jnp.where(rows == 0, wy_lo, pltpu.roll(wy, 1, 0))
            wz = 2.0 * (d - 1.0) * strain_ref[2, i] * mu
            wz_p = jnp.where(lanes == Z - 1, 0.0, pltpu.roll(wz, Z - 1, 1))
            wz_m = jnp.where(lanes == 0, 0.0, pltpu.roll(wz, 1, 1))
            transfer = (
                0.5 * (wxm - wxp),
                0.5 * (wy_m - wy_p),
                0.5 * (wz_m - wz_p),
            )
            inv_mu = invs[0, i]
            inv_lam = invs[1, i]
            residual_mu = sd_ref[i] - damage_part
            new_upd = keep * upd[0, i] + gain * inv_mu * residual_mu
            new_mu = mu + new_upd
            upd[0, i] = new_upd
            lams = []
            for c in range(3):
                lam = sfr[r, 1 + c, i + 1]
                ls = sides(lam, sfr[r, 1 + c, i + 2], sfr[r, 1 + c, i],
                           syl[r, 1 + c, i], syh[r, 1 + c, i])
                disp = MASS_SHIFT * lam + STIFF_SCALE * sum(
                    fs[k] * (lam - ls[k]) for k in range(6))
                residual = sdisp_ref[c, i] - (disp + transfer[c])
                nu = keep * upd[1 + c, i] + gain * inv_lam * residual
                upd[1 + c, i] = nu
                lams.append(lam + nu)
            if not last:
                sfr[r + 1, 0, i + 1] = new_mu
                for c in range(3):
                    sfr[r + 1, 1 + c, i + 1] = lams[c]
            else:
                out_mu_ref[i] = new_mu
                _, ds = damage_sides(i)
                grad = [0.5 * (ds[0] - ds[1]), 0.5 * (ds[2] - ds[3]), 0.5 * (ds[4] - ds[5])]
                length = jnp.sqrt(jnp.maximum(
                    grad[0] * grad[0] + grad[1] * grad[1] + grad[2] * grad[2], NORMAL_FLOOR))
                normal = [g / length for g in grad]
                size = normal[0] * normal[0] + normal[1] * normal[1] + normal[2] * normal[2]
                along = normal[0] * lams[0] + normal[1] * lams[1] + normal[2] * lams[2]
                a = RELAX_STEP / RELAX_INNER
                factor = 1.0 - a * (1.0 + NORMAL_WEIGHT * size)
                power = factor
                for _ in range(3):
                    power = power * power
                total = power
                work = bw_ref[0, 0]
                for level in range(2, 5):
                    total = jnp.where(work >= level, total * power, total)
                pull = NORMAL_WEIGHT * (1.0 - total) / (1.0 + NORMAL_WEIGHT * size)
                for c in range(3):
                    out_disp_ref[c, i] = lams[c] - (pull * along) * normal[c]
            return carry

        lax.fori_loop(1, X - 1, step, 0)
        arrive(copies, (0, 1))
        for i in (0, X - 1):
            step(i, 0)

    for copies in pending:
        sent(copies)


def body(damage, strain, seed_damage, seed_disp, brick_work, nx, ny):
    X, Y, Z = damage.shape
    f32 = jnp.float32
    vmem = pl.BlockSpec(memory_space=pltpu.VMEM)
    return pl.pallas_call(
        functools.partial(kernel, nx, ny),
        out_shape=(
            jax.ShapeDtypeStruct((X, Y, Z), f32),
            jax.ShapeDtypeStruct((3, X, Y, Z), f32),
        ),
        in_specs=[pl.BlockSpec(memory_space=pltpu.SMEM), vmem, vmem, vmem, vmem],
        out_specs=(vmem, vmem),
        scratch_shapes=[
            pltpu.VMEM((2, X + 2, Y, Z), f32),
            pltpu.VMEM((2, X, 1, Z), f32),
            pltpu.VMEM((2, X, 1, Z), f32),
            pltpu.VMEM((SWEEPS, 4, X + 2, Y, Z), f32),
            pltpu.VMEM((SWEEPS, 4, X, 1, Z), f32),
            pltpu.VMEM((SWEEPS, 4, X, 1, Z), f32),
            pltpu.VMEM((6, X, Y, Z), f32),
            pltpu.VMEM((4, X, Y, Z), f32),
            pltpu.VMEM((3, X, Y, Z), f32),
            pltpu.SemaphoreType.DMA((2 + SWEEPS, 4)),
            pltpu.SemaphoreType.DMA((2 + SWEEPS, 4)),
        ],
        compiler_params=pltpu.CompilerParams(
            collective_id=0, has_side_effects=True, vmem_limit_bytes=60 * 1024 * 1024
        ),
    )(brick_work, damage, strain, seed_damage, seed_disp)


def solution(mesh):
    nx = mesh.shape["gx"]
    ny = mesh.shape["gy"]
    placed = (
        P("gx", "gy", None),
        P(None, "gx", "gy", None),
        P("gx", "gy", None),
        P(None, "gx", "gy", None),
        P("gx", "gy"),
    )
    return jax.shard_map(
        functools.partial(body, nx=nx, ny=ny),
        mesh=mesh,
        in_specs=placed,
        out_specs=(P("gx", "gy", None), P(None, "gx", "gy", None)),
        check_vma=False,
    )
```

```python
import functools

import jax
import jax.numpy as jnp
from jax import lax
from jax.experimental import pallas as pl
from jax.experimental.pallas import tpu as pltpu
from jax.sharding import PartitionSpec as P

SWEEPS = 3
RELAX_INNER = 8

RESIDUAL_STIFFNESS = 0.001
TOUGH_OVER_LENGTH = 0.5
TOUGH_TIMES_LENGTH = 0.25
MASS_SHIFT = 0.5
STIFF_SCALE = 0.25
CENTER_VALUE = 1.0
HALF_WIDTH = 0.75
NORMAL_WEIGHT = 1.5
RELAX_STEP = 0.5
NORMAL_FLOOR = 0.05

MESH = pl.DeviceIdType.MESH

S_DMG, S_STR, S_SEED, S_MU, S_STATE = 0, 1, 2, 3, 4


def soft_of(d):
    return (1.0 - d) ** 2


def inverse_disp(d, sides):
    soft_center = soft_of(d) + RESIDUAL_STIFFNESS
    fs = [0.5 * (soft_center + soft_of(s) + RESIDUAL_STIFFNESS) for s in sides]
    total = fs[0]
    for k in range(1, 6):
        total = total + fs[k]
    return fs, 1.0 / (MASS_SHIFT + STIFF_SCALE * total)


def kernel(
    nx, ny,
    bw_ref, dmg_ref, strain_ref, sd_ref, sdisp_ref,
    out_mu_ref, out_disp_ref,
    dxf, ydl, ydh, strl, strh, sdxl, sdxh, sdyl, sdyh, cor,
    sfr, syl, syh, faces, upd, invs,
    send_sem, recv_sem, csend_sem, crecv_sem,
):
    X, Y, Z = dmg_ref.shape
    bx = lax.axis_index("gx")
    by = lax.axis_index("gy")
    has = (bx < nx - 1, bx > 0, by < ny - 1, by > 0)
    peers = ((bx + 1, by), (bx - 1, by), (bx, by + 1), (bx, by - 1))
    diag = ((bx + 1, by + 1), (bx + 1, by - 1), (bx - 1, by + 1), (bx - 1, by - 1))
    diag_has = (has[0] & has[2], has[0] & has[3], has[1] & has[2], has[1] & has[3])
    f32 = jnp.float32

    @pl.when(bx == 0)
    def _():
        dxf[:, 0:2] = jnp.zeros((2, 2, Y, Z), f32)
        sdxl[...] = jnp.zeros(sdxl.shape, f32)
        sfr[:, :, 0] = jnp.zeros((SWEEPS, 4, Y, Z), f32)

    @pl.when(bx == nx - 1)
    def _():
        dxf[:, X + 2:X + 4] = jnp.zeros((2, 2, Y, Z), f32)
        sdxh[...] = jnp.zeros(sdxh.shape, f32)
        sfr[:, :, X + 1] = jnp.zeros((SWEEPS, 4, Y, Z), f32)

    @pl.when(by == 0)
    def _():
        ydl[...] = jnp.zeros(ydl.shape, f32)
        strl[...] = jnp.zeros(strl.shape, f32)
        sdyl[...] = jnp.zeros(sdyl.shape, f32)
        syl[...] = jnp.zeros(syl.shape, f32)

    @pl.when(by == ny - 1)
    def _():
        ydh[...] = jnp.zeros(ydh.shape, f32)
        strh[...] = jnp.zeros(strh.shape, f32)
        sdyh[...] = jnp.zeros(sdyh.shape, f32)
        syh[...] = jnp.zeros(syh.shape, f32)

    for k in range(4):
        @pl.when(jnp.logical_not(diag_has[k]))
        def _():
            cor[k] = jnp.zeros((1, 1, Z), f32)

    barrier = pltpu.get_barrier_semaphore()
    count = jnp.int32(0)
    for peer, ok in zip(peers + diag, has + diag_has):
        @pl.when(ok)
        def _():
            pl.semaphore_signal(barrier, inc=1, device_id=peer, device_id_type=MESH)
        count = count + ok.astype(jnp.int32)

    dxf[0, 2:X + 2] = dmg_ref[...]
    dxf[1, 2:X + 2] = strain_ref[0]

    def local(i, carry):
        sx = strain_ref[0, i]
        sy = strain_ref[1, i]
        sz = strain_ref[2, i]
        energy = 0.5 * (sx * sx + sy * sy + sz * sz)
        inv_mu = 1.0 / (TOUGH_OVER_LENGTH + 2.0 * energy + 6.0 * TOUGH_TIMES_LENGTH)
        invs[0, i] = inv_mu
        invs[2, i] = TOUGH_OVER_LENGTH + 2.0 * energy
        mu0 = inv_mu * sd_ref[i] / CENTER_VALUE
        upd[0, i] = mu0
        sfr[0, 0, i + 1] = mu0
        return carry

    lax.fori_loop(0, X, local, 0)

    pl.semaphore_wait(barrier, count)

    def exchange(slot, routes, dirs):
        copies = {}
        for d in dirs:
            src, dst = routes[d]
            copies[d] = pltpu.make_async_remote_copy(
                src_ref=src, dst_ref=dst,
                send_sem=send_sem.at[slot, d], recv_sem=recv_sem.at[slot, d],
                device_id=peers[d], device_id_type=MESH,
            )
            @pl.when(has[d])
            def _():
                copies[d].start()
        return copies

    opposite = (1, 0, 3, 2)
    pending = []

    def arrive(copies):
        for d, copy in copies.items():
            @pl.when(has[opposite[d]])
            def _():
                copy.wait_recv()

    x_dirs, y_dirs = (0, 1), (2, 3)
    round0 = [
        (S_DMG, (
            (dmg_ref.at[X - 2:X], dxf.at[0, 0:2]),
            (dmg_ref.at[0:2], dxf.at[0, X + 2:X + 4]),
            (dmg_ref.at[:, Y - 2:Y], ydl),
            (dmg_ref.at[:, 0:2], ydh),
        )),
        (S_STR, (
            (strain_ref.at[0, X - 1:X], dxf.at[1, 1:2]),
            (strain_ref.at[0, 0:1], dxf.at[1, X + 2:X + 3]),
            (strain_ref.at[1, :, Y - 1:Y], strl),
            (strain_ref.at[1, :, 0:1], strh),
        )),
        (S_SEED, (
            (sdisp_ref.at[:, X - 1:X], sdxl),
            (sdisp_ref.at[:, 0:1], sdxh),
            (sdisp_ref.at[:, :, Y - 1:Y], sdyl),
            (sdisp_ref.at[:, :, 0:1], sdyh),
        )),
        (S_MU, (
            (sfr.at[0, 0:1, X:X + 1], sfr.at[0, 0:1, 0:1]),
            (sfr.at[0, 0:1, 1:2], sfr.at[0, 0:1, X + 1:X + 2]),
            (sfr.at[0, 0:1, 1:X + 1, Y - 1:Y], syl.at[0, 0:1]),
            (sfr.at[0, 0:1, 1:X + 1, 0:1], syh.at[0, 0:1]),
        )),
    ]
    x0 = [exchange(slot, routes, x_dirs) for slot, routes in round0]
    y0 = [exchange(slot, routes, y_dirs) for slot, routes in round0]
    corner_src = (
        dmg_ref.at[0:1, 0:1],
        dmg_ref.at[0:1, Y - 1:Y],
        dmg_ref.at[X - 1:X, 0:1],
        dmg_ref.at[X - 1:X, Y - 1:Y],
    )
    send_to = ((bx - 1, by - 1), (bx - 1, by + 1), (bx + 1, by - 1), (bx + 1, by + 1))
    send_has = (diag_has[3], diag_has[2], diag_has[1], diag_has[0])
    corners = []
    for k in range(4):
        copy = pltpu.make_async_remote_copy(
            src_ref=corner_src[k], dst_ref=cor.at[k],
            send_sem=csend_sem.at[k], recv_sem=crecv_sem.at[k],
            device_id=send_to[k], device_id_type=MESH,
        )
        corners.append(copy)

        @pl.when(send_has[k])
        def _():
            copy.start()
    pending += x0 + y0

    rows = lax.broadcasted_iota(jnp.int32, (Y, Z), 0)
    lanes = lax.broadcasted_iota(jnp.int32, (Y, Z), 1)
    lanes1 = lax.broadcasted_iota(jnp.int32, (1, Z), 1)

    def zsides(v, ln):
        n = v.shape[-1]
        zp = jnp.where(ln == n - 1, 0.0, pltpu.roll(v, n - 1, v.ndim - 1))
        zm = jnp.where(ln == 0, 0.0, pltpu.roll(v, 1, v.ndim - 1))
        return zp, zm

    def sides(center, nxp, nxm, lo, hi):
        yp = jnp.where(rows == Y - 1, hi, pltpu.roll(center, Y - 1, 0))
        ym = jnp.where(rows == 0, lo, pltpu.roll(center, 1, 0))
        zp, zm = zsides(center, lanes)
        return [nxp, nxm, yp, ym, zp, zm]

    def damage_sides(i):
        d = dxf[0, i + 2]
        return d, sides(d, dxf[0, i + 3], dxf[0, i + 1], ydl[i, 1:2], ydh[i, 0:1])

    for k in range(4):
        @pl.when(diag_has[k])
        def _():
            corners[k].wait_recv()
    arrive_y0 = [arrive(c) for c in y0]

    def y_row_lam(i, carry):
        for hi in (False, True):
            buf = ydh if hi else ydl
            near = 0 if hi else 1
            far = 1 if hi else 0
            d = buf[i, near:near + 1]
            right = cor[0 if hi else 1, 0]
            left = cor[2 if hi else 3, 0]
            nxp = jnp.where(i == X - 1, right, buf[(i + 1) % X, near:near + 1])
            nxm = jnp.where(i == 0, left, buf[(i + X - 1) % X, near:near + 1])
            own = dmg_ref[i, Y - 1:Y] if hi else dmg_ref[i, 0:1]
            beyond = buf[i, far:far + 1]
            yp, ym = (beyond, own) if hi else (own, beyond)
            zp, zm = zsides(d, lanes1)
            _, inv = inverse_disp(d, [nxp, nxm, yp, ym, zp, zm])
            seeds = sdyh if hi else sdyl
            target = syh if hi else syl
            for c in range(3):
                target[0, 1 + c, i] = inv * seeds[c, i] / CENTER_VALUE
        return carry

    lax.fori_loop(0, X, y_row_lam, 0)

    def prep(i, carry):
        d, ds = damage_sides(i)
        fs, inv_lam = inverse_disp(d, ds)
        for k in range(6):
            faces[k, i] = fs[k]
        invs[1, i] = inv_lam
        for c in range(3):
            lam0 = inv_lam * sdisp_ref[c, i] / CENTER_VALUE
            upd[1 + c, i] = lam0
            sfr[0, 1 + c, i + 1] = lam0
        return carry

    lax.fori_loop(1, X - 1, prep, 0)
    for c in x0:
        arrive(c)
    for i in (0, X - 1):
        prep(i, 0)

    for hi in (False, True):
        j = X + 2 if hi else 1
        d = dxf[0, j]
        nxp = dxf[0, j + 1]
        nxm = dxf[0, j - 1]
        up = cor[0 if hi else 2]
        down = cor[1 if hi else 3]
        yp = jnp.where(rows == Y - 1, up[0], pltpu.roll(d, Y - 1, 0))
        ym = jnp.where(rows == 0, down[0], pltpu.roll(d, 1, 0))
        zp, zm = zsides(d, lanes)
        _, inv = inverse_disp(d, [nxp, nxm, yp, ym, zp, zm])
        seeds = sdxh if hi else sdxl
        plane = X + 1 if hi else 0
        for c in range(3):
            sfr[0, 1 + c, plane] = inv * seeds[c, 0] / CENTER_VALUE

    def state_routes(r):
        return (
            (sfr.at[r, :, X:X + 1], sfr.at[r, :, 0:1]),
            (sfr.at[r, :, 1:2], sfr.at[r, :, X + 1:X + 2]),
            (sfr.at[r, :, 1:X + 1, Y - 1:Y], syl.at[r]),
            (sfr.at[r, :, 1:X + 1, 0:1], syh.at[r]),
        )

    ratio = CENTER_VALUE / HALF_WIDTH
    rho = 1.0 / ratio
    for sweep in range(SWEEPS):
        r = sweep
        rho_next = 1.0 / (2.0 * ratio - rho)
        keep = rho_next * rho
        gain = 2.0 * rho_next / HALF_WIDTH
        rho = rho_next
        last = sweep == SWEEPS - 1

        def step(i, carry, r=r, keep=keep, gain=gain, last=last):
            mu = sfr[r, 0, i + 1]
            mus = sides(mu, sfr[r, 0, i + 2], sfr[r, 0, i], syl[r, 0, i], syh[r, 0, i])
            damage_part = invs[2, i] * mu + TOUGH_TIMES_LENGTH * sum(mu - s for s in mus)
            fs = [faces[k, i] for k in range(6)]
            wxm = 2.0 * (dxf[0, i + 1] - 1.0) * dxf[1, i + 1] * mus[1]
            wxp = 2.0 * (dxf[0, i + 3] - 1.0) * dxf[1, i + 3] * mus[0]
            d = dxf[0, i + 2]
            wy = 2.0 * (d - 1.0) * strain_ref[1, i] * mu
            wy_lo = 2.0 * (ydl[i, 1:2] - 1.0) * strl[i] * syl[r, 0, i]
            wy_hi = 2.0 * (ydh[i, 0:1] - 1.0) * strh[i] * syh[r, 0, i]
            wy_p = jnp.where(rows == Y - 1, wy_hi, pltpu.roll(wy, Y - 1, 0))
            wy_m = jnp.where(rows == 0, wy_lo, pltpu.roll(wy, 1, 0))
            wz = 2.0 * (d - 1.0) * strain_ref[2, i] * mu
            wz_p, wz_m = zsides(wz, lanes)
            transfer = (
                0.5 * (wxm - wxp),
                0.5 * (wy_m - wy_p),
                0.5 * (wz_m - wz_p),
            )
            inv_mu = invs[0, i]
            inv_lam = invs[1, i]
            residual_mu = sd_ref[i] - damage_part
            new_upd = keep * upd[0, i] + gain * inv_mu * residual_mu
            new_mu = mu + new_upd
            upd[0, i] = new_upd
            lams = []
            for c in range(3):
                lam = sfr[r, 1 + c, i + 1]
                ls = sides(lam, sfr[r, 1 + c, i + 2], sfr[r, 1 + c, i],
                           syl[r, 1 + c, i], syh[r, 1 + c, i])
                disp = MASS_SHIFT * lam + STIFF_SCALE * sum(
                    fs[k] * (lam - ls[k]) for k in range(6))
                residual = sdisp_ref[c, i] - (disp + transfer[c])
                nu = keep * upd[1 + c, i] + gain * inv_lam * residual
                upd[1 + c, i] = nu
                lams.append(lam + nu)
            if not last:
                sfr[r + 1, 0, i + 1] = new_mu
                for c in range(3):
                    sfr[r + 1, 1 + c, i + 1] = lams[c]
            else:
                out_mu_ref[i] = new_mu
                _, ds = damage_sides(i)
                grad = [0.5 * (ds[0] - ds[1]), 0.5 * (ds[2] - ds[3]), 0.5 * (ds[4] - ds[5])]
                length = jnp.sqrt(jnp.maximum(
                    grad[0] * grad[0] + grad[1] * grad[1] + grad[2] * grad[2], NORMAL_FLOOR))
                normal = [g / length for g in grad]
                size = normal[0] * normal[0] + normal[1] * normal[1] + normal[2] * normal[2]
                along = normal[0] * lams[0] + normal[1] * lams[1] + normal[2] * lams[2]
                a = RELAX_STEP / RELAX_INNER
                factor = 1.0 - a * (1.0 + NORMAL_WEIGHT * size)
                power = factor
                for _ in range(3):
                    power = power * power
                total = power
                work = bw_ref[0, 0]
                for level in range(2, 5):
                    total = jnp.where(work >= level, total * power, total)
                pull = NORMAL_WEIGHT * (1.0 - total) / (1.0 + NORMAL_WEIGHT * size)
                for c in range(3):
                    out_disp_ref[c, i] = lams[c] - (pull * along) * normal[c]
            return carry

        if r == 0:
            for i in (0, X - 1):
                step(i, 0)
            nxt = exchange(S_STATE, state_routes(1), x_dirs)
            lax.fori_loop(1, X - 1, step, 0)
            nyt = exchange(S_STATE, state_routes(1), y_dirs)
        else:
            arrive(nyt)
            lax.fori_loop(1, X - 1, step, 0)
            arrive(nxt)
            for i in (0, X - 1):
                step(i, 0)
            pending += [nxt, nyt]
            if not last:
                nxt = exchange(S_STATE + r, state_routes(r + 1), x_dirs)
                nyt = exchange(S_STATE + r, state_routes(r + 1), y_dirs)

    for copies in pending:
        for d, copy in copies.items():
            @pl.when(has[d])
            def _():
                copy.wait_send()
    for k in range(4):
        @pl.when(send_has[k])
        def _():
            corners[k].wait_send()


def body(damage, strain, seed_damage, seed_disp, brick_work, nx, ny):
    X, Y, Z = damage.shape
    f32 = jnp.float32
    vmem = pl.BlockSpec(memory_space=pltpu.VMEM)
    return pl.pallas_call(
        functools.partial(kernel, nx, ny),
        out_shape=(
            jax.ShapeDtypeStruct((X, Y, Z), f32),
            jax.ShapeDtypeStruct((3, X, Y, Z), f32),
        ),
        in_specs=[pl.BlockSpec(memory_space=pltpu.SMEM), vmem, vmem, vmem, vmem],
        out_specs=(vmem, vmem),
        scratch_shapes=[
            pltpu.VMEM((2, X + 4, Y, Z), f32),
            pltpu.VMEM((X, 2, Z), f32),
            pltpu.VMEM((X, 2, Z), f32),
            pltpu.VMEM((X, 1, Z), f32),
            pltpu.VMEM((X, 1, Z), f32),
            pltpu.VMEM((3, 1, Y, Z), f32),
            pltpu.VMEM((3, 1, Y, Z), f32),
            pltpu.VMEM((3, X, 1, Z), f32),
            pltpu.VMEM((3, X, 1, Z), f32),
            pltpu.VMEM((4, 1, 1, Z), f32),
            pltpu.VMEM((SWEEPS, 4, X + 2, Y, Z), f32),
            pltpu.VMEM((SWEEPS, 4, X, 1, Z), f32),
            pltpu.VMEM((SWEEPS, 4, X, 1, Z), f32),
            pltpu.VMEM((6, X, Y, Z), f32),
            pltpu.VMEM((4, X, Y, Z), f32),
            pltpu.VMEM((3, X, Y, Z), f32),
            pltpu.SemaphoreType.DMA((S_STATE + SWEEPS - 1, 4)),
            pltpu.SemaphoreType.DMA((S_STATE + SWEEPS - 1, 4)),
            pltpu.SemaphoreType.DMA((4,)),
            pltpu.SemaphoreType.DMA((4,)),
        ],
        compiler_params=pltpu.CompilerParams(
            collective_id=0, has_side_effects=True, vmem_limit_bytes=60 * 1024 * 1024
        ),
    )(brick_work, damage, strain, seed_damage, seed_disp)


def solution(mesh):
    nx = mesh.shape["gx"]
    ny = mesh.shape["gy"]
    placed = (
        P("gx", "gy", None),
        P(None, "gx", "gy", None),
        P("gx", "gy", None),
        P(None, "gx", "gy", None),
        P("gx", "gy"),
    )
    return jax.shard_map(
        functools.partial(body, nx=nx, ny=ny),
        mesh=mesh,
        in_specs=placed,
        out_specs=(P("gx", "gy", None), P(None, "gx", "gy", None)),
        check_vma=False,
    )
```

```python
import functools

import jax
import jax.numpy as jnp
from jax import lax
from jax.experimental import pallas as pl
from jax.experimental.pallas import tpu as pltpu
from jax.sharding import PartitionSpec as P

SWEEPS = 3
RELAX_INNER = 8

RESIDUAL_STIFFNESS = 0.001
TOUGH_OVER_LENGTH = 0.5
TOUGH_TIMES_LENGTH = 0.25
MASS_SHIFT = 0.5
STIFF_SCALE = 0.25
CENTER_VALUE = 1.0
HALF_WIDTH = 0.75
NORMAL_WEIGHT = 1.5
RELAX_STEP = 0.5
NORMAL_FLOOR = 0.05

MESH = pl.DeviceIdType.MESH

S_DMG, S_STR, S_SEED, S_MU, S_STATE = 0, 1, 2, 3, 4


def soft_of(d):
    return (1.0 - d) ** 2


def inverse_disp(d, sides):
    soft_center = soft_of(d) + RESIDUAL_STIFFNESS
    fs = [0.5 * (soft_center + soft_of(s) + RESIDUAL_STIFFNESS) for s in sides]
    total = fs[0]
    for k in range(1, 6):
        total = total + fs[k]
    return fs, 1.0 / (MASS_SHIFT + STIFF_SCALE * total)


def kernel(
    nx, ny,
    bw_ref, dmg_ref, strain_ref, sd_ref, sdisp_ref,
    out_mu_ref, out_disp_ref,
    dxf, ydl, ydh, strl, strh, sdxl, sdxh, sdyl, sdyh, cor,
    sfr, syl, syh, faces, upd, invs,
    send_sem, recv_sem, csend_sem, crecv_sem, edge_send, edge_recv,
):
    X, Y, Z = dmg_ref.shape
    bx = lax.axis_index("gx")
    by = lax.axis_index("gy")
    has = (bx < nx - 1, bx > 0, by < ny - 1, by > 0)
    peers = ((bx + 1, by), (bx - 1, by), (bx, by + 1), (bx, by - 1))
    diag = ((bx + 1, by + 1), (bx + 1, by - 1), (bx - 1, by + 1), (bx - 1, by - 1))
    diag_has = (has[0] & has[2], has[0] & has[3], has[1] & has[2], has[1] & has[3])
    f32 = jnp.float32

    @pl.when(bx == 0)
    def _():
        dxf[:, 0:2] = jnp.zeros((2, 2, Y, Z), f32)
        sdxl[...] = jnp.zeros(sdxl.shape, f32)
        sfr[:, :, 0] = jnp.zeros((SWEEPS, 4, Y, Z), f32)

    @pl.when(bx == nx - 1)
    def _():
        dxf[:, X + 2:X + 4] = jnp.zeros((2, 2, Y, Z), f32)
        sdxh[...] = jnp.zeros(sdxh.shape, f32)
        sfr[:, :, X + 1] = jnp.zeros((SWEEPS, 4, Y, Z), f32)

    @pl.when(by == 0)
    def _():
        ydl[...] = jnp.zeros(ydl.shape, f32)
        strl[...] = jnp.zeros(strl.shape, f32)
        sdyl[...] = jnp.zeros(sdyl.shape, f32)
        syl[...] = jnp.zeros(syl.shape, f32)

    @pl.when(by == ny - 1)
    def _():
        ydh[...] = jnp.zeros(ydh.shape, f32)
        strh[...] = jnp.zeros(strh.shape, f32)
        sdyh[...] = jnp.zeros(sdyh.shape, f32)
        syh[...] = jnp.zeros(syh.shape, f32)

    for k in range(4):
        @pl.when(jnp.logical_not(diag_has[k]))
        def _():
            cor[k] = jnp.zeros((1, 1, Z), f32)

    barrier = pltpu.get_barrier_semaphore()
    count = jnp.int32(0)
    for peer, ok in zip(peers + diag, has + diag_has):
        @pl.when(ok)
        def _():
            pl.semaphore_signal(barrier, inc=1, device_id=peer, device_id_type=MESH)
        count = count + ok.astype(jnp.int32)

    dxf[0, 2:X + 2] = dmg_ref[...]
    dxf[1, 2:X + 2] = strain_ref[0]

    def local(i, carry):
        sx = strain_ref[0, i]
        sy = strain_ref[1, i]
        sz = strain_ref[2, i]
        energy = 0.5 * (sx * sx + sy * sy + sz * sz)
        inv_mu = 1.0 / (TOUGH_OVER_LENGTH + 2.0 * energy + 6.0 * TOUGH_TIMES_LENGTH)
        invs[0, i] = inv_mu
        invs[2, i] = TOUGH_OVER_LENGTH + 2.0 * energy
        mu0 = inv_mu * sd_ref[i] / CENTER_VALUE
        upd[0, i] = mu0
        sfr[0, 0, i + 1] = mu0
        return carry

    lax.fori_loop(0, X, local, 0)

    pl.semaphore_wait(barrier, count)

    def exchange(slot, routes, dirs, sems=None):
        ssem, rsem = sems if sems is not None else (send_sem, recv_sem)
        copies = {}
        for d in dirs:
            src, dst = routes[d]
            copies[d] = pltpu.make_async_remote_copy(
                src_ref=src, dst_ref=dst,
                send_sem=ssem.at[slot, d], recv_sem=rsem.at[slot, d],
                device_id=peers[d], device_id_type=MESH,
            )
            @pl.when(has[d])
            def _():
                copies[d].start()
        return copies

    opposite = (1, 0, 3, 2)
    pending = []

    def arrive(copies):
        for d, copy in copies.items():
            @pl.when(has[opposite[d]])
            def _():
                copy.wait_recv()

    x_dirs, y_dirs = (0, 1), (2, 3)
    round0 = [
        (S_DMG, (
            (dmg_ref.at[X - 2:X], dxf.at[0, 0:2]),
            (dmg_ref.at[0:2], dxf.at[0, X + 2:X + 4]),
            (dmg_ref.at[:, Y - 2:Y], ydl),
            (dmg_ref.at[:, 0:2], ydh),
        )),
        (S_STR, (
            (strain_ref.at[0, X - 1:X], dxf.at[1, 1:2]),
            (strain_ref.at[0, 0:1], dxf.at[1, X + 2:X + 3]),
            (strain_ref.at[1, :, Y - 1:Y], strl),
            (strain_ref.at[1, :, 0:1], strh),
        )),
        (S_SEED, (
            (sdisp_ref.at[:, X - 1:X], sdxl),
            (sdisp_ref.at[:, 0:1], sdxh),
            (sdisp_ref.at[:, :, Y - 1:Y], sdyl),
            (sdisp_ref.at[:, :, 0:1], sdyh),
        )),
        (S_MU, (
            (sfr.at[0, 0:1, X:X + 1], sfr.at[0, 0:1, 0:1]),
            (sfr.at[0, 0:1, 1:2], sfr.at[0, 0:1, X + 1:X + 2]),
            (sfr.at[0, 0:1, 1:X + 1, Y - 1:Y], syl.at[0, 0:1]),
            (sfr.at[0, 0:1, 1:X + 1, 0:1], syh.at[0, 0:1]),
        )),
    ]
    x0 = [exchange(slot, routes, x_dirs) for slot, routes in round0]
    y0 = [exchange(slot, routes, y_dirs) for slot, routes in round0]
    corner_src = (
        dmg_ref.at[0:1, 0:1],
        dmg_ref.at[0:1, Y - 1:Y],
        dmg_ref.at[X - 1:X, 0:1],
        dmg_ref.at[X - 1:X, Y - 1:Y],
    )
    send_to = ((bx - 1, by - 1), (bx - 1, by + 1), (bx + 1, by - 1), (bx + 1, by + 1))
    send_has = (diag_has[3], diag_has[2], diag_has[1], diag_has[0])
    corners = []
    for k in range(4):
        copy = pltpu.make_async_remote_copy(
            src_ref=corner_src[k], dst_ref=cor.at[k],
            send_sem=csend_sem.at[k], recv_sem=crecv_sem.at[k],
            device_id=send_to[k], device_id_type=MESH,
        )
        corners.append(copy)

        @pl.when(send_has[k])
        def _():
            copy.start()
    pending += x0 + y0

    rows = lax.broadcasted_iota(jnp.int32, (Y, Z), 0)
    lanes = lax.broadcasted_iota(jnp.int32, (Y, Z), 1)
    lanes1 = lax.broadcasted_iota(jnp.int32, (1, Z), 1)

    def zsides(v, ln):
        n = v.shape[-1]
        zp = jnp.where(ln == n - 1, 0.0, pltpu.roll(v, n - 1, v.ndim - 1))
        zm = jnp.where(ln == 0, 0.0, pltpu.roll(v, 1, v.ndim - 1))
        return zp, zm

    def sides(center, nxp, nxm, lo, hi):
        yp = jnp.where(rows == Y - 1, hi, pltpu.roll(center, Y - 1, 0))
        ym = jnp.where(rows == 0, lo, pltpu.roll(center, 1, 0))
        zp, zm = zsides(center, lanes)
        return [nxp, nxm, yp, ym, zp, zm]

    def damage_sides(i):
        d = dxf[0, i + 2]
        return d, sides(d, dxf[0, i + 3], dxf[0, i + 1], ydl[i, 1:2], ydh[i, 0:1])

    for k in range(4):
        @pl.when(diag_has[k])
        def _():
            corners[k].wait_recv()
    arrive_y0 = [arrive(c) for c in y0]

    def y_row_lam(i, carry):
        for hi in (False, True):
            buf = ydh if hi else ydl
            near = 0 if hi else 1
            far = 1 if hi else 0
            d = buf[i, near:near + 1]
            right = cor[0 if hi else 1, 0]
            left = cor[2 if hi else 3, 0]
            nxp = jnp.where(i == X - 1, right, buf[(i + 1) % X, near:near + 1])
            nxm = jnp.where(i == 0, left, buf[(i + X - 1) % X, near:near + 1])
            own = dmg_ref[i, Y - 1:Y] if hi else dmg_ref[i, 0:1]
            beyond = buf[i, far:far + 1]
            yp, ym = (beyond, own) if hi else (own, beyond)
            zp, zm = zsides(d, lanes1)
            _, inv = inverse_disp(d, [nxp, nxm, yp, ym, zp, zm])
            seeds = sdyh if hi else sdyl
            target = syh if hi else syl
            for c in range(3):
                target[0, 1 + c, i] = inv * seeds[c, i] / CENTER_VALUE
        return carry

    lax.fori_loop(0, X, y_row_lam, 0)

    def prep(i, carry):
        d, ds = damage_sides(i)
        fs, inv_lam = inverse_disp(d, ds)
        for k in range(6):
            faces[k, i] = fs[k]
        invs[1, i] = inv_lam
        for c in range(3):
            lam0 = inv_lam * sdisp_ref[c, i] / CENTER_VALUE
            upd[1 + c, i] = lam0
            sfr[0, 1 + c, i + 1] = lam0
        return carry

    lax.fori_loop(1, X - 1, prep, 0)
    for c in x0:
        arrive(c)
    for i in (0, X - 1):
        prep(i, 0)

    for hi in (False, True):
        j = X + 2 if hi else 1
        d = dxf[0, j]
        nxp = dxf[0, j + 1]
        nxm = dxf[0, j - 1]
        up = cor[0 if hi else 2]
        down = cor[1 if hi else 3]
        yp = jnp.where(rows == Y - 1, up[0], pltpu.roll(d, Y - 1, 0))
        ym = jnp.where(rows == 0, down[0], pltpu.roll(d, 1, 0))
        zp, zm = zsides(d, lanes)
        _, inv = inverse_disp(d, [nxp, nxm, yp, ym, zp, zm])
        seeds = sdxh if hi else sdxl
        plane = X + 1 if hi else 0
        for c in range(3):
            sfr[0, 1 + c, plane] = inv * seeds[c, 0] / CENTER_VALUE

    def state_routes(r, part):
        if part == "x":
            return (
                (sfr.at[r, :, X:X + 1], sfr.at[r, :, 0:1]),
                (sfr.at[r, :, 1:2], sfr.at[r, :, X + 1:X + 2]),
            )
        lo, hi = {"ya": (1, X - 1), "y0": (0, 1), "y1": (X - 1, X)}[part]
        return (None, None,
                (sfr.at[r, :, lo + 1:hi + 1, Y - 1:Y], syl.at[r, :, lo:hi]),
                (sfr.at[r, :, lo + 1:hi + 1, 0:1], syh.at[r, :, lo:hi]))

    def send_state(r, part):
        routes = state_routes(r, part)
        if part == "x":
            return exchange(S_STATE + r - 1, routes + (None, None), x_dirs)
        if part == "ya":
            return exchange(S_STATE + r - 1, routes, y_dirs)
        k = 0 if part == "y0" else 1
        return exchange(r - 1, routes, y_dirs, (edge_send.at[k], edge_recv.at[k]))

    ratio = CENTER_VALUE / HALF_WIDTH
    rho = 1.0 / ratio
    for sweep in range(SWEEPS):
        r = sweep
        rho_next = 1.0 / (2.0 * ratio - rho)
        keep = rho_next * rho
        gain = 2.0 * rho_next / HALF_WIDTH
        rho = rho_next
        last = sweep == SWEEPS - 1

        def step(i, carry, r=r, keep=keep, gain=gain, last=last):
            mu = sfr[r, 0, i + 1]
            mus = sides(mu, sfr[r, 0, i + 2], sfr[r, 0, i], syl[r, 0, i], syh[r, 0, i])
            damage_part = invs[2, i] * mu + TOUGH_TIMES_LENGTH * sum(mu - s for s in mus)
            fs = [faces[k, i] for k in range(6)]
            wxm = 2.0 * (dxf[0, i + 1] - 1.0) * dxf[1, i + 1] * mus[1]
            wxp = 2.0 * (dxf[0, i + 3] - 1.0) * dxf[1, i + 3] * mus[0]
            d = dxf[0, i + 2]
            wy = 2.0 * (d - 1.0) * strain_ref[1, i] * mu
            wy_lo = 2.0 * (ydl[i, 1:2] - 1.0) * strl[i] * syl[r, 0, i]
            wy_hi = 2.0 * (ydh[i, 0:1] - 1.0) * strh[i] * syh[r, 0, i]
            wy_p = jnp.where(rows == Y - 1, wy_hi, pltpu.roll(wy, Y - 1, 0))
            wy_m = jnp.where(rows == 0, wy_lo, pltpu.roll(wy, 1, 0))
            wz = 2.0 * (d - 1.0) * strain_ref[2, i] * mu
            wz_p, wz_m = zsides(wz, lanes)
            transfer = (
                0.5 * (wxm - wxp),
                0.5 * (wy_m - wy_p),
                0.5 * (wz_m - wz_p),
            )
            inv_mu = invs[0, i]
            inv_lam = invs[1, i]
            residual_mu = sd_ref[i] - damage_part
            new_upd = keep * upd[0, i] + gain * inv_mu * residual_mu
            new_mu = mu + new_upd
            upd[0, i] = new_upd
            lams = []
            for c in range(3):
                lam = sfr[r, 1 + c, i + 1]
                ls = sides(lam, sfr[r, 1 + c, i + 2], sfr[r, 1 + c, i],
                           syl[r, 1 + c, i], syh[r, 1 + c, i])
                disp = MASS_SHIFT * lam + STIFF_SCALE * sum(
                    fs[k] * (lam - ls[k]) for k in range(6))
                residual = sdisp_ref[c, i] - (disp + transfer[c])
                nu = keep * upd[1 + c, i] + gain * inv_lam * residual
                upd[1 + c, i] = nu
                lams.append(lam + nu)
            if not last:
                sfr[r + 1, 0, i + 1] = new_mu
                for c in range(3):
                    sfr[r + 1, 1 + c, i + 1] = lams[c]
            else:
                out_mu_ref[i] = new_mu
                _, ds = damage_sides(i)
                grad = [0.5 * (ds[0] - ds[1]), 0.5 * (ds[2] - ds[3]), 0.5 * (ds[4] - ds[5])]
                length = jnp.sqrt(jnp.maximum(
                    grad[0] * grad[0] + grad[1] * grad[1] + grad[2] * grad[2], NORMAL_FLOOR))
                normal = [g / length for g in grad]
                size = normal[0] * normal[0] + normal[1] * normal[1] + normal[2] * normal[2]
                along = normal[0] * lams[0] + normal[1] * lams[1] + normal[2] * lams[2]
                a = RELAX_STEP / RELAX_INNER
                factor = 1.0 - a * (1.0 + NORMAL_WEIGHT * size)
                power = factor
                for _ in range(3):
                    power = power * power
                total = power
                work = bw_ref[0, 0]
                for level in range(2, 5):
                    total = jnp.where(work >= level, total * power, total)
                pull = NORMAL_WEIGHT * (1.0 - total) / (1.0 + NORMAL_WEIGHT * size)
                for c in range(3):
                    out_disp_ref[c, i] = lams[c] - (pull * along) * normal[c]
            return carry

        if r == 0:
            for i in (0, X - 1):
                step(i, 0)
            edge_copies = [send_state(1, p) for p in ("x", "y0", "y1")]
            lax.fori_loop(1, X - 1, step, 0)
            inner_copies = send_state(1, "ya")
        else:
            arrive(inner_copies)
            lax.fori_loop(1, X - 1, step, 0)
            pending.append(inner_copies)
            if not last:
                inner_copies = send_state(r + 1, "ya")
            for c in edge_copies:
                arrive(c)
            for i in (0, X - 1):
                step(i, 0)
            pending += edge_copies
            if not last:
                edge_copies = [send_state(r + 1, p) for p in ("x", "y0", "y1")]

    for copies in pending:
        for d, copy in copies.items():
            @pl.when(has[d])
            def _():
                copy.wait_send()
    for k in range(4):
        @pl.when(send_has[k])
        def _():
            corners[k].wait_send()


def body(damage, strain, seed_damage, seed_disp, brick_work, nx, ny):
    X, Y, Z = damage.shape
    f32 = jnp.float32
    vmem = pl.BlockSpec(memory_space=pltpu.VMEM)
    return pl.pallas_call(
        functools.partial(kernel, nx, ny),
        out_shape=(
            jax.ShapeDtypeStruct((X, Y, Z), f32),
            jax.ShapeDtypeStruct((3, X, Y, Z), f32),
        ),
        in_specs=[pl.BlockSpec(memory_space=pltpu.SMEM), vmem, vmem, vmem, vmem],
        out_specs=(vmem, vmem),
        scratch_shapes=[
            pltpu.VMEM((2, X + 4, Y, Z), f32),
            pltpu.VMEM((X, 2, Z), f32),
            pltpu.VMEM((X, 2, Z), f32),
            pltpu.VMEM((X, 1, Z), f32),
            pltpu.VMEM((X, 1, Z), f32),
            pltpu.VMEM((3, 1, Y, Z), f32),
            pltpu.VMEM((3, 1, Y, Z), f32),
            pltpu.VMEM((3, X, 1, Z), f32),
            pltpu.VMEM((3, X, 1, Z), f32),
            pltpu.VMEM((4, 1, 1, Z), f32),
            pltpu.VMEM((SWEEPS, 4, X + 2, Y, Z), f32),
            pltpu.VMEM((SWEEPS, 4, X, 1, Z), f32),
            pltpu.VMEM((SWEEPS, 4, X, 1, Z), f32),
            pltpu.VMEM((6, X, Y, Z), f32),
            pltpu.VMEM((4, X, Y, Z), f32),
            pltpu.VMEM((3, X, Y, Z), f32),
            pltpu.SemaphoreType.DMA((S_STATE + SWEEPS - 1, 4)),
            pltpu.SemaphoreType.DMA((S_STATE + SWEEPS - 1, 4)),
            pltpu.SemaphoreType.DMA((4,)),
            pltpu.SemaphoreType.DMA((4,)),
            pltpu.SemaphoreType.DMA((2, SWEEPS - 1, 4)),
            pltpu.SemaphoreType.DMA((2, SWEEPS - 1, 4)),
        ],
        compiler_params=pltpu.CompilerParams(
            collective_id=0, has_side_effects=True, vmem_limit_bytes=60 * 1024 * 1024
        ),
    )(brick_work, damage, strain, seed_damage, seed_disp)


def solution(mesh):
    nx = mesh.shape["gx"]
    ny = mesh.shape["gy"]
    placed = (
        P("gx", "gy", None),
        P(None, "gx", "gy", None),
        P("gx", "gy", None),
        P(None, "gx", "gy", None),
        P("gx", "gy"),
    )
    return jax.shard_map(
        functools.partial(body, nx=nx, ny=ny),
        mesh=mesh,
        in_specs=placed,
        out_specs=(P("gx", "gy", None), P(None, "gx", "gy", None)),
        check_vma=False,
    )
```

```python
import functools

import jax
import jax.numpy as jnp
from jax import lax
from jax.experimental import pallas as pl
from jax.experimental.pallas import tpu as pltpu
from jax.sharding import PartitionSpec as P

SWEEPS = 3
RELAX_INNER = 8

RESIDUAL_STIFFNESS = 0.001
TOUGH_OVER_LENGTH = 0.5
TOUGH_TIMES_LENGTH = 0.25
MASS_SHIFT = 0.5
STIFF_SCALE = 0.25
CENTER_VALUE = 1.0
HALF_WIDTH = 0.75
NORMAL_WEIGHT = 1.5
RELAX_STEP = 0.5
NORMAL_FLOOR = 0.05

MESH = pl.DeviceIdType.MESH


def soft_of(d):
    return (1.0 - d) ** 2


def kernel(
    nx, ny,
    bw_ref, dmg_ref, strain_ref, sd_ref, sdisp_ref,
    out_mu_ref, out_step_ref, out_disp_ref, out_corr_ref,
    dfr, dyl, dyh, sfr, syl, syh, faces, upd, invs, send_sem, recv_sem,
):
    X, Y, Z = dmg_ref.shape
    bx = lax.axis_index("gx")
    by = lax.axis_index("gy")
    has = (bx < nx - 1, bx > 0, by < ny - 1, by > 0)
    peers = ((bx + 1, by), (bx - 1, by), (bx, by + 1), (bx, by - 1))

    @pl.when(bx == 0)
    def _():
        dfr[:, 0] = jnp.zeros((2, Y, Z), jnp.float32)
        sfr[:, :, 0] = jnp.zeros((SWEEPS, 4, Y, Z), jnp.float32)

    @pl.when(bx == nx - 1)
    def _():
        dfr[:, X + 1] = jnp.zeros((2, Y, Z), jnp.float32)
        sfr[:, :, X + 1] = jnp.zeros((SWEEPS, 4, Y, Z), jnp.float32)

    @pl.when(by == 0)
    def _():
        dyl[...] = jnp.zeros(dyl.shape, jnp.float32)
        syl[...] = jnp.zeros(syl.shape, jnp.float32)

    @pl.when(by == ny - 1)
    def _():
        dyh[...] = jnp.zeros(dyh.shape, jnp.float32)
        syh[...] = jnp.zeros(syh.shape, jnp.float32)

    barrier = pltpu.get_barrier_semaphore()
    count = jnp.int32(0)
    for d in range(4):
        @pl.when(has[d])
        def _():
            pl.semaphore_signal(barrier, inc=1, device_id=peers[d], device_id_type=MESH)
        count = count + has[d].astype(jnp.int32)
    pl.semaphore_wait(barrier, count)

    def exchange(slot, routes):
        copies = []
        for d in range(4):
            src, dst = routes[d]
            copies.append(
                pltpu.make_async_remote_copy(
                    src_ref=src, dst_ref=dst,
                    send_sem=send_sem.at[slot, d], recv_sem=recv_sem.at[slot, d],
                    device_id=peers[d], device_id_type=MESH,
                )
            )
        for d in range(4):
            @pl.when(has[d])
            def _():
                copies[d].start()
        return copies

    def arrive(copies, dirs):
        opposite = (1, 0, 3, 2)
        for d in dirs:
            @pl.when(has[opposite[d]])
            def _():
                copies[d].wait_recv()

    def sent(copies):
        for d in range(4):
            @pl.when(has[d])
            def _():
                copies[d].wait_send()

    c_dmg = exchange(0, (
        (dmg_ref.at[X - 1:X], dfr.at[0, 0:1]),
        (dmg_ref.at[0:1], dfr.at[0, X + 1:X + 2]),
        (dmg_ref.at[:, Y - 1:Y], dyl.at[0]),
        (dmg_ref.at[:, 0:1], dyh.at[0]),
    ))
    c_str = exchange(1, (
        (strain_ref.at[0, X - 1:X], dfr.at[1, 0:1]),
        (strain_ref.at[0, 0:1], dfr.at[1, X + 1:X + 2]),
        (strain_ref.at[1, :, Y - 1:Y], dyl.at[1]),
        (strain_ref.at[1, :, 0:1], dyh.at[1]),
    ))
    dfr[0, 1:X + 1] = dmg_ref[...]
    dfr[1, 1:X + 1] = strain_ref[0]
    arrive(c_dmg, (2, 3))
    arrive(c_str, (2, 3))
    pending = [c_dmg, c_str]

    rows = lax.broadcasted_iota(jnp.int32, (Y, Z), 0)
    lanes = lax.broadcasted_iota(jnp.int32, (Y, Z), 1)

    def sides(center, nxp, nxm, lo, hi):
        yp = jnp.where(rows == Y - 1, hi, pltpu.roll(center, Y - 1, 0))
        ym = jnp.where(rows == 0, lo, pltpu.roll(center, 1, 0))
        zp = jnp.where(lanes == Z - 1, 0.0, pltpu.roll(center, Z - 1, 1))
        zm = jnp.where(lanes == 0, 0.0, pltpu.roll(center, 1, 1))
        return [nxp, nxm, yp, ym, zp, zm]

    def damage_sides(i):
        d = dfr[0, i + 1]
        return d, sides(d, dfr[0, i + 2], dfr[0, i], dyl[0, i], dyh[0, i])

    def prep(i, carry):
        d, ds = damage_sides(i)
        soft_center = soft_of(d) + RESIDUAL_STIFFNESS
        fs = [0.5 * (soft_center + soft_of(s) + RESIDUAL_STIFFNESS) for s in ds]
        total = fs[0]
        for k in range(6):
            faces[k, i] = fs[k]
            if k:
                total = total + fs[k]
        sx = strain_ref[0, i]
        sy = strain_ref[1, i]
        sz = strain_ref[2, i]
        energy = 0.5 * (sx * sx + sy * sy + sz * sz)
        inv_mu = 1.0 / (TOUGH_OVER_LENGTH + 2.0 * energy + 6.0 * TOUGH_TIMES_LENGTH)
        inv_lam = 1.0 / (MASS_SHIFT + STIFF_SCALE * total)
        invs[0, i] = inv_mu
        invs[1, i] = inv_lam
        invs[2, i] = TOUGH_OVER_LENGTH + 2.0 * energy
        mu0 = inv_mu * sd_ref[i] / CENTER_VALUE
        upd[0, i] = mu0
        sfr[0, 0, i + 1] = mu0
        for c in range(3):
            lam0 = inv_lam * sdisp_ref[c, i] / CENTER_VALUE
            upd[1 + c, i] = lam0
            sfr[0, 1 + c, i + 1] = lam0
        return carry

    lax.fori_loop(1, X - 1, prep, 0)
    arrive(c_dmg, (0, 1))
    arrive(c_str, (0, 1))
    for i in (0, X - 1):
        prep(i, 0)

    def state_routes(r):
        return (
            (sfr.at[r, :, X:X + 1], sfr.at[r, :, 0:1]),
            (sfr.at[r, :, 1:2], sfr.at[r, :, X + 1:X + 2]),
            (sfr.at[r, :, 1:X + 1, Y - 1:Y], syl.at[r]),
            (sfr.at[r, :, 1:X + 1, 0:1], syh.at[r]),
        )

    ratio = CENTER_VALUE / HALF_WIDTH
    rho = 1.0 / ratio
    for sweep in range(SWEEPS):
        r = sweep
        copies = exchange(2 + r, state_routes(r))
        pending.append(copies)
        arrive(copies, (2, 3))
        rho_next = 1.0 / (2.0 * ratio - rho)
        keep = rho_next * rho
        gain = 2.0 * rho_next / HALF_WIDTH
        rho = rho_next
        last = sweep == SWEEPS - 1

        def step(i, carry, r=r, keep=keep, gain=gain, last=last):
            mu = sfr[r, 0, i + 1]
            mus = sides(mu, sfr[r, 0, i + 2], sfr[r, 0, i], syl[r, 0, i], syh[r, 0, i])
            energy_diag = invs[2, i]
            damage_part = energy_diag * mu + TOUGH_TIMES_LENGTH * sum(mu - s for s in mus)
            fs = [faces[k, i] for k in range(6)]
            wxm = 2.0 * (dfr[0, i] - 1.0) * dfr[1, i] * mus[1]
            wxp = 2.0 * (dfr[0, i + 2] - 1.0) * dfr[1, i + 2] * mus[0]
            d = dfr[0, i + 1]
            wy = 2.0 * (d - 1.0) * strain_ref[1, i] * mu
            wy_lo = 2.0 * (dyl[0, i] - 1.0) * dyl[1, i] * syl[r, 0, i]
            wy_hi = 2.0 * (dyh[0, i] - 1.0) * dyh[1, i] * syh[r, 0, i]
            wy_p = jnp.where(rows == Y - 1, wy_hi, pltpu.roll(wy, Y - 1, 0))
            wy_m = jnp.where(rows == 0, wy_lo, pltpu.roll(wy, 1, 0))
            wz = 2.0 * (d - 1.0) * strain_ref[2, i] * mu
            wz_p = jnp.where(lanes == Z - 1, 0.0, pltpu.roll(wz, Z - 1, 1))
            wz_m = jnp.where(lanes == 0, 0.0, pltpu.roll(wz, 1, 1))
            transfer = (
                0.5 * (wxm - wxp),
                0.5 * (wy_m - wy_p),
                0.5 * (wz_m - wz_p),
            )
            inv_mu = invs[0, i]
            inv_lam = invs[1, i]
            residual_mu = sd_ref[i] - damage_part
            new_upd = keep * upd[0, i] + gain * inv_mu * residual_mu
            new_mu = mu + new_upd
            upd[0, i] = new_upd
            lams = []
            for c in range(3):
                lam = sfr[r, 1 + c, i + 1]
                ls = sides(lam, sfr[r, 1 + c, i + 2], sfr[r, 1 + c, i],
                           syl[r, 1 + c, i], syh[r, 1 + c, i])
                disp = MASS_SHIFT * lam + STIFF_SCALE * sum(
                    fs[k] * (lam - ls[k]) for k in range(6))
                residual = sdisp_ref[c, i] - (disp + transfer[c])
                nu = keep * upd[1 + c, i] + gain * inv_lam * residual
                upd[1 + c, i] = nu
                lams.append(lam + nu)
            if not last:
                sfr[r + 1, 0, i + 1] = new_mu
                for c in range(3):
                    sfr[r + 1, 1 + c, i + 1] = lams[c]
            else:
                out_mu_ref[i] = mu
                out_step_ref[i] = new_upd
                _, ds = damage_sides(i)
                grad = [0.5 * (ds[0] - ds[1]), 0.5 * (ds[2] - ds[3]), 0.5 * (ds[4] - ds[5])]
                length = jnp.sqrt(jnp.maximum(
                    grad[0] * grad[0] + grad[1] * grad[1] + grad[2] * grad[2], NORMAL_FLOOR))
                normal = [g / length for g in grad]
                size = normal[0] * normal[0] + normal[1] * normal[1] + normal[2] * normal[2]
                along = normal[0] * lams[0] + normal[1] * lams[1] + normal[2] * lams[2]
                a = RELAX_STEP / RELAX_INNER
                factor = 1.0 - a * (1.0 + NORMAL_WEIGHT * size)
                power = factor
                for _ in range(3):
                    power = power * power
                total = power
                work = bw_ref[0, 0]
                for level in range(2, 5):
                    total = jnp.where(work >= level, total * power, total)
                pull = NORMAL_WEIGHT * (1.0 - total) / (1.0 + NORMAL_WEIGHT * size)
                for c in range(3):
                    out_disp_ref[c, i] = lams[c]
                    out_corr_ref[c, i] = (pull * along) * normal[c]
            return carry

        lax.fori_loop(1, X - 1, step, 0)
        arrive(copies, (0, 1))
        for i in (0, X - 1):
            step(i, 0)

    for copies in pending:
        sent(copies)


def body(damage, strain, seed_damage, seed_disp, brick_work, nx, ny):
    X, Y, Z = damage.shape
    f32 = jnp.float32
    vmem = pl.BlockSpec(memory_space=pltpu.VMEM)
    state = pl.pallas_call(
        functools.partial(kernel, nx, ny),
        out_shape=(
            jax.ShapeDtypeStruct((X, Y, Z), f32),
            jax.ShapeDtypeStruct((X, Y, Z), f32),
            jax.ShapeDtypeStruct((3, X, Y, Z), f32),
            jax.ShapeDtypeStruct((3, X, Y, Z), f32),
        ),
        in_specs=[pl.BlockSpec(memory_space=pltpu.SMEM), vmem, vmem, vmem, vmem],
        out_specs=(vmem, vmem, vmem, vmem),
        scratch_shapes=[
            pltpu.VMEM((2, X + 2, Y, Z), f32),
            pltpu.VMEM((2, X, 1, Z), f32),
            pltpu.VMEM((2, X, 1, Z), f32),
            pltpu.VMEM((SWEEPS, 4, X + 2, Y, Z), f32),
            pltpu.VMEM((SWEEPS, 4, X, 1, Z), f32),
            pltpu.VMEM((SWEEPS, 4, X, 1, Z), f32),
            pltpu.VMEM((6, X, Y, Z), f32),
            pltpu.VMEM((4, X, Y, Z), f32),
            pltpu.VMEM((3, X, Y, Z), f32),
            pltpu.SemaphoreType.DMA((2 + SWEEPS, 4)),
            pltpu.SemaphoreType.DMA((2 + SWEEPS, 4)),
        ],
        compiler_params=pltpu.CompilerParams(
            collective_id=0, has_side_effects=True, vmem_limit_bytes=60 * 1024 * 1024
        ),
    )(brick_work, damage, strain, seed_damage, seed_disp)
    mu, step, lam, corr = state
    return mu + step, lam - corr


def solution(mesh):
    nx = mesh.shape["gx"]
    ny = mesh.shape["gy"]
    placed = (
        P("gx", "gy", None),
        P(None, "gx", "gy", None),
        P("gx", "gy", None),
        P(None, "gx", "gy", None),
        P("gx", "gy"),
    )
    return jax.shard_map(
        functools.partial(body, nx=nx, ny=ny),
        mesh=mesh,
        in_specs=placed,
        out_specs=(P("gx", "gy", None), P(None, "gx", "gy", None)),
        check_vma=False,
    )
```

```python
import functools

import jax
import jax.numpy as jnp
from jax import lax
from jax.experimental import pallas as pl
from jax.experimental.pallas import tpu as pltpu
from jax.sharding import PartitionSpec as P

SWEEPS = 3
RELAX_INNER = 8

RESIDUAL_STIFFNESS = 0.001
TOUGH_OVER_LENGTH = 0.5
TOUGH_TIMES_LENGTH = 0.25
MASS_SHIFT = 0.5
STIFF_SCALE = 0.25
CENTER_VALUE = 1.0
HALF_WIDTH = 0.75
NORMAL_WEIGHT = 1.5
RELAX_STEP = 0.5
NORMAL_FLOOR = 0.05

MESH = pl.DeviceIdType.MESH


def soft_of(d):
    return (1.0 - d) ** 2


def kernel(
    nx, ny,
    bw_ref, dmg_ref, strain_ref, sd_ref, sdisp_ref,
    out_mu_ref, out_step_ref, out_disp_ref, out_corr_ref,
    dfr, dyl, dyh, sfr, syl, syh, faces, upd, invs, send_sem, recv_sem,
):
    X, Y, Z = dmg_ref.shape
    bx = lax.axis_index("gx")
    by = lax.axis_index("gy")
    has = (bx < nx - 1, bx > 0, by < ny - 1, by > 0)
    peers = ((bx + 1, by), (bx - 1, by), (bx, by + 1), (bx, by - 1))

    @pl.when(bx == 0)
    def _():
        dfr[:, 0] = jnp.zeros((2, Y, Z), jnp.float32)
        sfr[:, :, 0] = jnp.zeros((SWEEPS, 4, Y, Z), jnp.float32)

    @pl.when(bx == nx - 1)
    def _():
        dfr[:, X + 1] = jnp.zeros((2, Y, Z), jnp.float32)
        sfr[:, :, X + 1] = jnp.zeros((SWEEPS, 4, Y, Z), jnp.float32)

    @pl.when(by == 0)
    def _():
        dyl[...] = jnp.zeros(dyl.shape, jnp.float32)
        syl[...] = jnp.zeros(syl.shape, jnp.float32)

    @pl.when(by == ny - 1)
    def _():
        dyh[...] = jnp.zeros(dyh.shape, jnp.float32)
        syh[...] = jnp.zeros(syh.shape, jnp.float32)

    barrier = pltpu.get_barrier_semaphore()
    count = jnp.int32(0)
    for d in range(4):
        @pl.when(has[d])
        def _():
            pl.semaphore_signal(barrier, inc=1, device_id=peers[d], device_id_type=MESH)
        count = count + has[d].astype(jnp.int32)
    pl.semaphore_wait(barrier, count)

    def exchange(slot, routes):
        copies = []
        for d in range(4):
            src, dst = routes[d]
            copies.append(
                pltpu.make_async_remote_copy(
                    src_ref=src, dst_ref=dst,
                    send_sem=send_sem.at[slot, d], recv_sem=recv_sem.at[slot, d],
                    device_id=peers[d], device_id_type=MESH,
                )
            )
        for d in range(4):
            @pl.when(has[d])
            def _():
                copies[d].start()
        return copies

    def arrive(copies, dirs):
        opposite = (1, 0, 3, 2)
        for d in dirs:
            @pl.when(has[opposite[d]])
            def _():
                copies[d].wait_recv()

    def sent(copies):
        for d in range(4):
            @pl.when(has[d])
            def _():
                copies[d].wait_send()

    c_dmg = exchange(0, (
        (dmg_ref.at[X - 1:X], dfr.at[0, 0:1]),
        (dmg_ref.at[0:1], dfr.at[0, X + 1:X + 2]),
        (dmg_ref.at[:, Y - 1:Y], dyl.at[0]),
        (dmg_ref.at[:, 0:1], dyh.at[0]),
    ))
    c_str = exchange(1, (
        (strain_ref.at[0, X - 1:X], dfr.at[1, 0:1]),
        (strain_ref.at[0, 0:1], dfr.at[1, X + 1:X + 2]),
        (strain_ref.at[1, :, Y - 1:Y], dyl.at[1]),
        (strain_ref.at[1, :, 0:1], dyh.at[1]),
    ))
    dfr[0, 1:X + 1] = dmg_ref[...]
    dfr[1, 1:X + 1] = strain_ref[0]
    arrive(c_dmg, (2, 3))
    arrive(c_str, (2, 3))
    pending = [c_dmg, c_str]

    rows = lax.broadcasted_iota(jnp.int32, (Y, Z), 0)
    lanes = lax.broadcasted_iota(jnp.int32, (Y, Z), 1)

    def sides(center, nxp, nxm, lo, hi):
        yp = jnp.where(rows == Y - 1, hi, pltpu.roll(center, Y - 1, 0))
        ym = jnp.where(rows == 0, lo, pltpu.roll(center, 1, 0))
        zp = jnp.where(lanes == Z - 1, 0.0, pltpu.roll(center, Z - 1, 1))
        zm = jnp.where(lanes == 0, 0.0, pltpu.roll(center, 1, 1))
        return [nxp, nxm, yp, ym, zp, zm]

    def damage_sides(i):
        d = dfr[0, i + 1]
        return d, sides(d, dfr[0, i + 2], dfr[0, i], dyl[0, i], dyh[0, i])

    def prep(i, carry):
        d, ds = damage_sides(i)
        soft_center = soft_of(d) + RESIDUAL_STIFFNESS
        fs = [0.5 * (soft_center + soft_of(s) + RESIDUAL_STIFFNESS) for s in ds]
        total = fs[0]
        for k in range(6):
            faces[k, i] = fs[k]
            if k:
                total = total + fs[k]
        sx = strain_ref[0, i]
        sy = strain_ref[1, i]
        sz = strain_ref[2, i]
        energy = 0.5 * (sx * sx + sy * sy + sz * sz)
        inv_mu = 1.0 / (TOUGH_OVER_LENGTH + 2.0 * energy + 6.0 * TOUGH_TIMES_LENGTH)
        inv_lam = 1.0 / (MASS_SHIFT + STIFF_SCALE * total)
        invs[0, i] = inv_mu
        invs[1, i] = inv_lam
        invs[2, i] = TOUGH_OVER_LENGTH + 2.0 * energy
        mu0 = inv_mu * sd_ref[i] / CENTER_VALUE
        upd[0, i] = mu0
        sfr[0, 0, i + 1] = mu0
        for c in range(3):
            lam0 = inv_lam * sdisp_ref[c, i] / CENTER_VALUE
            upd[1 + c, i] = lam0
            sfr[0, 1 + c, i + 1] = lam0
        return carry

    lax.fori_loop(1, X - 1, prep, 0)
    arrive(c_dmg, (0, 1))
    arrive(c_str, (0, 1))
    for i in (0, X - 1):
        prep(i, 0)

    def state_routes(r):
        return (
            (sfr.at[r, :, X:X + 1], sfr.at[r, :, 0:1]),
            (sfr.at[r, :, 1:2], sfr.at[r, :, X + 1:X + 2]),
            (sfr.at[r, :, 1:X + 1, Y - 1:Y], syl.at[r]),
            (sfr.at[r, :, 1:X + 1, 0:1], syh.at[r]),
        )

    ratio = CENTER_VALUE / HALF_WIDTH
    rho = 1.0 / ratio
    for sweep in range(SWEEPS):
        r = sweep
        copies = exchange(2 + r, state_routes(r))
        pending.append(copies)
        arrive(copies, (2, 3))
        rho_next = 1.0 / (2.0 * ratio - rho)
        keep = rho_next * rho
        gain = 2.0 * rho_next / HALF_WIDTH
        rho = rho_next
        last = sweep == SWEEPS - 1

        def step(i, carry, r=r, keep=keep, gain=gain, last=last):
            mu = sfr[r, 0, i + 1]
            mus = sides(mu, sfr[r, 0, i + 2], sfr[r, 0, i], syl[r, 0, i], syh[r, 0, i])
            energy_diag = invs[2, i]
            damage_part = energy_diag * mu + TOUGH_TIMES_LENGTH * sum(mu - s for s in mus)
            fs = [faces[k, i] for k in range(6)]
            wxm = 2.0 * (dfr[0, i] - 1.0) * dfr[1, i] * mus[1]
            wxp = 2.0 * (dfr[0, i + 2] - 1.0) * dfr[1, i + 2] * mus[0]
            d = dfr[0, i + 1]
            wy = 2.0 * (d - 1.0) * strain_ref[1, i] * mu
            wy_lo = 2.0 * (dyl[0, i] - 1.0) * dyl[1, i] * syl[r, 0, i]
            wy_hi = 2.0 * (dyh[0, i] - 1.0) * dyh[1, i] * syh[r, 0, i]
            wy_p = jnp.where(rows == Y - 1, wy_hi, pltpu.roll(wy, Y - 1, 0))
            wy_m = jnp.where(rows == 0, wy_lo, pltpu.roll(wy, 1, 0))
            wz = 2.0 * (d - 1.0) * strain_ref[2, i] * mu
            wz_p = jnp.where(lanes == Z - 1, 0.0, pltpu.roll(wz, Z - 1, 1))
            wz_m = jnp.where(lanes == 0, 0.0, pltpu.roll(wz, 1, 1))
            transfer = (
                0.5 * (wxm - wxp),
                0.5 * (wy_m - wy_p),
                0.5 * (wz_m - wz_p),
            )
            inv_mu = invs[0, i]
            inv_lam = invs[1, i]
            residual_mu = sd_ref[i] - damage_part
            new_upd = keep * upd[0, i] + gain * inv_mu * residual_mu
            new_mu = mu + new_upd
            upd[0, i] = new_upd
            lams = []
            for c in range(3):
                lam = sfr[r, 1 + c, i + 1]
                ls = sides(lam, sfr[r, 1 + c, i + 2], sfr[r, 1 + c, i],
                           syl[r, 1 + c, i], syh[r, 1 + c, i])
                disp = MASS_SHIFT * lam + STIFF_SCALE * sum(
                    fs[k] * (lam - ls[k]) for k in range(6))
                residual = sdisp_ref[c, i] - (disp + transfer[c])
                nu = keep * upd[1 + c, i] + gain * inv_lam * residual
                upd[1 + c, i] = nu
                lams.append(lam + nu)
            if not last:
                sfr[r + 1, 0, i + 1] = new_mu
                for c in range(3):
                    sfr[r + 1, 1 + c, i + 1] = lams[c]
            else:
                out_mu_ref[i] = mu
                out_step_ref[i] = new_upd
                _, ds = damage_sides(i)
                grad = [0.5 * (ds[0] - ds[1]), 0.5 * (ds[2] - ds[3]), 0.5 * (ds[4] - ds[5])]
                length = jnp.sqrt(jnp.maximum(
                    grad[0] * grad[0] + grad[1] * grad[1] + grad[2] * grad[2], NORMAL_FLOOR))
                normal = [g / length for g in grad]
                size = normal[0] * normal[0] + normal[1] * normal[1] + normal[2] * normal[2]
                along = normal[0] * lams[0] + normal[1] * lams[1] + normal[2] * lams[2]
                a = RELAX_STEP / RELAX_INNER
                factor = 1.0 - a * (1.0 + NORMAL_WEIGHT * size)
                power = factor
                for _ in range(3):
                    power = power * power
                total = power
                work = bw_ref[0, 0]
                for level in range(2, 5):
                    total = jnp.where(work >= level, total * power, total)
                pull = NORMAL_WEIGHT * (1.0 - total) / (1.0 + NORMAL_WEIGHT * size)
                for c in range(3):
                    out_disp_ref[c, i] = lams[c]
                    out_corr_ref[c, i] = (pull * along) * normal[c]
            return carry

        lax.fori_loop(1, X - 1, step, 0)
        arrive(copies, (0, 1))
        for i in (0, X - 1):
            step(i, 0)

    for copies in pending:
        sent(copies)


def body(damage, strain, seed_damage, seed_disp, brick_work, nx, ny):
    X, Y, Z = damage.shape
    f32 = jnp.float32
    vmem = pl.BlockSpec(memory_space=pltpu.VMEM)
    state = pl.pallas_call(
        functools.partial(kernel, nx, ny),
        out_shape=(
            jax.ShapeDtypeStruct((X, Y, Z), f32),
            jax.ShapeDtypeStruct((X, Y, Z), f32),
            jax.ShapeDtypeStruct((3, X, Y, Z), f32),
            jax.ShapeDtypeStruct((3, X, Y, Z), f32),
        ),
        in_specs=[pl.BlockSpec(memory_space=pltpu.SMEM), vmem, vmem, vmem, vmem],
        out_specs=(vmem, vmem, vmem, vmem),
        scratch_shapes=[
            pltpu.VMEM((2, X + 2, Y, Z), f32),
            pltpu.VMEM((2, X, 1, Z), f32),
            pltpu.VMEM((2, X, 1, Z), f32),
            pltpu.VMEM((SWEEPS, 4, X + 2, Y, Z), f32),
            pltpu.VMEM((SWEEPS, 4, X, 1, Z), f32),
            pltpu.VMEM((SWEEPS, 4, X, 1, Z), f32),
            pltpu.VMEM((6, X, Y, Z), f32),
            pltpu.VMEM((4, X, Y, Z), f32),
            pltpu.VMEM((3, X, Y, Z), f32),
            pltpu.SemaphoreType.DMA((2 + SWEEPS, 4)),
            pltpu.SemaphoreType.DMA((2 + SWEEPS, 4)),
        ],
        compiler_params=pltpu.CompilerParams(
            collective_id=0, has_side_effects=True, vmem_limit_bytes=60 * 1024 * 1024
        ),
    )(brick_work, damage, strain, seed_damage, seed_disp)
    return pl.pallas_call(
        finish_kernel,
        out_shape=(
            jax.ShapeDtypeStruct((X, Y, Z), f32),
            jax.ShapeDtypeStruct((3, X, Y, Z), f32),
        ),
        in_specs=[vmem] * 4,
        out_specs=(vmem, vmem),
    )(*state)


def finish_kernel(mu_ref, step_ref, lam_ref, corr_ref, out_mu_ref, out_disp_ref):
    out_mu_ref[...] = mu_ref[...] + step_ref[...]
    for c in range(3):
        out_disp_ref[c] = lam_ref[c] - corr_ref[c]


def solution(mesh):
    nx = mesh.shape["gx"]
    ny = mesh.shape["gy"]
    placed = (
        P("gx", "gy", None),
        P(None, "gx", "gy", None),
        P("gx", "gy", None),
        P(None, "gx", "gy", None),
        P("gx", "gy"),
    )
    return jax.shard_map(
        functools.partial(body, nx=nx, ny=ny),
        mesh=mesh,
        in_specs=placed,
        out_specs=(P("gx", "gy", None), P(None, "gx", "gy", None)),
        check_vma=False,
    )
```

```python
import functools

import jax
import jax.numpy as jnp
from jax import lax
from jax.experimental import pallas as pl
from jax.experimental.pallas import tpu as pltpu
from jax.sharding import PartitionSpec as P

SWEEPS = 3
RELAX_INNER = 8

RESIDUAL_STIFFNESS = 0.001
TOUGH_OVER_LENGTH = 0.5
TOUGH_TIMES_LENGTH = 0.25
MASS_SHIFT = 0.5
STIFF_SCALE = 0.25
CENTER_VALUE = 1.0
HALF_WIDTH = 0.75
NORMAL_WEIGHT = 1.5
RELAX_STEP = 0.5
NORMAL_FLOOR = 0.05

MESH = pl.DeviceIdType.MESH


def soft_of(d):
    return (1.0 - d) ** 2


def kernel(
    nx, ny,
    bw_ref, dmg_ref, strain_ref, sd_ref, sdisp_ref,
    out_mu_ref, out_disp_ref,
    dfr, dyl, dyh, sfr, syl, syh, faces, upd, invs, send_sem, recv_sem,
):
    X, Y, Z = dmg_ref.shape
    bx = lax.axis_index("gx")
    by = lax.axis_index("gy")
    has = (bx < nx - 1, bx > 0, by < ny - 1, by > 0)
    peers = ((bx + 1, by), (bx - 1, by), (bx, by + 1), (bx, by - 1))

    @pl.when(bx == 0)
    def _():
        dfr[:, 0] = jnp.zeros((2, Y, Z), jnp.float32)
        sfr[:, :, 0] = jnp.zeros((SWEEPS, 4, Y, Z), jnp.float32)

    @pl.when(bx == nx - 1)
    def _():
        dfr[:, X + 1] = jnp.zeros((2, Y, Z), jnp.float32)
        sfr[:, :, X + 1] = jnp.zeros((SWEEPS, 4, Y, Z), jnp.float32)

    @pl.when(by == 0)
    def _():
        dyl[...] = jnp.zeros(dyl.shape, jnp.float32)
        syl[...] = jnp.zeros(syl.shape, jnp.float32)

    @pl.when(by == ny - 1)
    def _():
        dyh[...] = jnp.zeros(dyh.shape, jnp.float32)
        syh[...] = jnp.zeros(syh.shape, jnp.float32)

    barrier = pltpu.get_barrier_semaphore()
    count = jnp.int32(0)
    for d in range(4):
        @pl.when(has[d])
        def _():
            pl.semaphore_signal(barrier, inc=1, device_id=peers[d], device_id_type=MESH)
        count = count + has[d].astype(jnp.int32)
    pl.semaphore_wait(barrier, count)

    def exchange(slot, routes):
        copies = []
        for d in range(4):
            src, dst = routes[d]
            copies.append(
                pltpu.make_async_remote_copy(
                    src_ref=src, dst_ref=dst,
                    send_sem=send_sem.at[slot, d], recv_sem=recv_sem.at[slot, d],
                    device_id=peers[d], device_id_type=MESH,
                )
            )
        for d in range(4):
            @pl.when(has[d])
            def _():
                copies[d].start()
        return copies

    def arrive(copies, dirs):
        opposite = (1, 0, 3, 2)
        for d in dirs:
            @pl.when(has[opposite[d]])
            def _():
                copies[d].wait_recv()

    def sent(copies):
        for d in range(4):
            @pl.when(has[d])
            def _():
                copies[d].wait_send()

    c_dmg = exchange(0, (
        (dmg_ref.at[X - 1:X], dfr.at[0, 0:1]),
        (dmg_ref.at[0:1], dfr.at[0, X + 1:X + 2]),
        (dmg_ref.at[:, Y - 1:Y], dyl.at[0]),
        (dmg_ref.at[:, 0:1], dyh.at[0]),
    ))
    c_str = exchange(1, (
        (strain_ref.at[0, X - 1:X], dfr.at[1, 0:1]),
        (strain_ref.at[0, 0:1], dfr.at[1, X + 1:X + 2]),
        (strain_ref.at[1, :, Y - 1:Y], dyl.at[1]),
        (strain_ref.at[1, :, 0:1], dyh.at[1]),
    ))
    dfr[0, 1:X + 1] = dmg_ref[...]
    dfr[1, 1:X + 1] = strain_ref[0]
    arrive(c_dmg, (2, 3))
    arrive(c_str, (2, 3))
    pending = [c_dmg, c_str]

    rows = lax.broadcasted_iota(jnp.int32, (Y, Z), 0)
    lanes = lax.broadcasted_iota(jnp.int32, (Y, Z), 1)

    def sides(center, nxp, nxm, lo, hi):
        yp = jnp.where(rows == Y - 1, hi, pltpu.roll(center, Y - 1, 0))
        ym = jnp.where(rows == 0, lo, pltpu.roll(center, 1, 0))
        zp = jnp.where(lanes == Z - 1, 0.0, pltpu.roll(center, Z - 1, 1))
        zm = jnp.where(lanes == 0, 0.0, pltpu.roll(center, 1, 1))
        return [nxp, nxm, yp, ym, zp, zm]

    def damage_sides(i):
        d = dfr[0, i + 1]
        return d, sides(d, dfr[0, i + 2], dfr[0, i], dyl[0, i], dyh[0, i])

    def prep(i, carry):
        d, ds = damage_sides(i)
        soft_center = soft_of(d) + RESIDUAL_STIFFNESS
        fs = [0.5 * (soft_center + soft_of(s) + RESIDUAL_STIFFNESS) for s in ds]
        total = fs[0]
        for k in range(6):
            faces[k, i] = fs[k]
            if k:
                total = total + fs[k]
        sx = strain_ref[0, i]
        sy = strain_ref[1, i]
        sz = strain_ref[2, i]
        energy = 0.5 * (sx * sx + sy * sy + sz * sz)
        inv_mu = 1.0 / (TOUGH_OVER_LENGTH + 2.0 * energy + 6.0 * TOUGH_TIMES_LENGTH)
        inv_lam = 1.0 / (MASS_SHIFT + STIFF_SCALE * total)
        invs[0, i] = inv_mu
        invs[1, i] = inv_lam
        invs[2, i] = TOUGH_OVER_LENGTH + 2.0 * energy
        mu0 = inv_mu * sd_ref[i] / CENTER_VALUE
        upd[0, i] = mu0
        sfr[0, 0, i + 1] = mu0
        for c in range(3):
            lam0 = inv_lam * sdisp_ref[c, i] / CENTER_VALUE
            upd[1 + c, i] = lam0
            sfr[0, 1 + c, i + 1] = lam0
        return carry

    lax.fori_loop(1, X - 1, prep, 0)
    arrive(c_dmg, (0, 1))
    arrive(c_str, (0, 1))
    for i in (0, X - 1):
        prep(i, 0)

    def state_routes(r):
        return (
            (sfr.at[r, :, X:X + 1], sfr.at[r, :, 0:1]),
            (sfr.at[r, :, 1:2], sfr.at[r, :, X + 1:X + 2]),
            (sfr.at[r, :, 1:X + 1, Y - 1:Y], syl.at[r]),
            (sfr.at[r, :, 1:X + 1, 0:1], syh.at[r]),
        )

    ratio = CENTER_VALUE / HALF_WIDTH
    rho = 1.0 / ratio
    for sweep in range(SWEEPS):
        r = sweep
        copies = exchange(2 + r, state_routes(r))
        pending.append(copies)
        arrive(copies, (2, 3))
        rho_next = 1.0 / (2.0 * ratio - rho)
        keep = rho_next * rho
        gain = 2.0 * rho_next / HALF_WIDTH
        rho = rho_next
        last = sweep == SWEEPS - 1

        def step(i, carry, r=r, keep=keep, gain=gain, last=last):
            mu = sfr[r, 0, i + 1]
            mus = sides(mu, sfr[r, 0, i + 2], sfr[r, 0, i], syl[r, 0, i], syh[r, 0, i])
            energy_diag = invs[2, i]
            damage_part = energy_diag * mu + TOUGH_TIMES_LENGTH * sum(mu - s for s in mus)
            fs = [faces[k, i] for k in range(6)]
            wxm = 2.0 * (dfr[0, i] - 1.0) * dfr[1, i] * mus[1]
            wxp = 2.0 * (dfr[0, i + 2] - 1.0) * dfr[1, i + 2] * mus[0]
            d = dfr[0, i + 1]
            wy = 2.0 * (d - 1.0) * strain_ref[1, i] * mu
            wy_lo = 2.0 * (dyl[0, i] - 1.0) * dyl[1, i] * syl[r, 0, i]
            wy_hi = 2.0 * (dyh[0, i] - 1.0) * dyh[1, i] * syh[r, 0, i]
            wy_p = jnp.where(rows == Y - 1, wy_hi, pltpu.roll(wy, Y - 1, 0))
            wy_m = jnp.where(rows == 0, wy_lo, pltpu.roll(wy, 1, 0))
            wz = 2.0 * (d - 1.0) * strain_ref[2, i] * mu
            wz_p = jnp.where(lanes == Z - 1, 0.0, pltpu.roll(wz, Z - 1, 1))
            wz_m = jnp.where(lanes == 0, 0.0, pltpu.roll(wz, 1, 1))
            transfer = (
                0.5 * (wxm - wxp),
                0.5 * (wy_m - wy_p),
                0.5 * (wz_m - wz_p),
            )
            inv_mu = invs[0, i]
            inv_lam = invs[1, i]
            residual_mu = sd_ref[i] - damage_part
            new_upd = keep * upd[0, i] + gain * inv_mu * residual_mu
            new_mu = mu + new_upd
            upd[0, i] = new_upd
            lams = []
            for c in range(3):
                lam = sfr[r, 1 + c, i + 1]
                ls = sides(lam, sfr[r, 1 + c, i + 2], sfr[r, 1 + c, i],
                           syl[r, 1 + c, i], syh[r, 1 + c, i])
                disp = MASS_SHIFT * lam + STIFF_SCALE * sum(
                    fs[k] * (lam - ls[k]) for k in range(6))
                residual = sdisp_ref[c, i] - (disp + transfer[c])
                nu = keep * upd[1 + c, i] + gain * inv_lam * residual
                upd[1 + c, i] = nu
                lams.append(lam + nu)
            if not last:
                sfr[r + 1, 0, i + 1] = new_mu
                for c in range(3):
                    sfr[r + 1, 1 + c, i + 1] = lams[c]
            else:
                out_mu_ref[i] = new_mu
                _, ds = damage_sides(i)
                grad = [0.5 * (ds[0] - ds[1]), 0.5 * (ds[2] - ds[3]), 0.5 * (ds[4] - ds[5])]
                length = jnp.sqrt(jnp.maximum(
                    grad[0] * grad[0] + grad[1] * grad[1] + grad[2] * grad[2], NORMAL_FLOOR))
                normal = [g / length for g in grad]
                size = normal[0] * normal[0] + normal[1] * normal[1] + normal[2] * normal[2]
                along = normal[0] * lams[0] + normal[1] * lams[1] + normal[2] * lams[2]
                a = RELAX_STEP / RELAX_INNER
                factor = 1.0 - a * (1.0 + NORMAL_WEIGHT * size)
                power = factor
                for _ in range(3):
                    power = power * power
                total = power
                work = bw_ref[0, 0]
                for level in range(2, 5):
                    total = jnp.where(work >= level, total * power, total)
                pull = NORMAL_WEIGHT * (1.0 - total) / (1.0 + NORMAL_WEIGHT * size)
                for c in range(3):
                    out_disp_ref[c, i] = lams[c] - (pull * along) * normal[c]
            return carry

        lax.fori_loop(1, X - 1, step, 0)
        arrive(copies, (0, 1))
        for i in (0, X - 1):
            step(i, 0)

    for copies in pending:
        sent(copies)


def body(damage, strain, seed_damage, seed_disp, brick_work, nx, ny):
    X, Y, Z = damage.shape
    f32 = jnp.float32
    vmem = pl.BlockSpec(memory_space=pltpu.VMEM)
    state = pl.pallas_call(
        functools.partial(kernel, nx, ny),
        out_shape=(
            jax.ShapeDtypeStruct((X, Y, Z), f32),
            jax.ShapeDtypeStruct((3, X, Y, Z), f32),
        ),
        in_specs=[pl.BlockSpec(memory_space=pltpu.SMEM), vmem, vmem, vmem, vmem],
        out_specs=(vmem, vmem),
        scratch_shapes=[
            pltpu.VMEM((2, X + 2, Y, Z), f32),
            pltpu.VMEM((2, X, 1, Z), f32),
            pltpu.VMEM((2, X, 1, Z), f32),
            pltpu.VMEM((SWEEPS, 4, X + 2, Y, Z), f32),
            pltpu.VMEM((SWEEPS, 4, X, 1, Z), f32),
            pltpu.VMEM((SWEEPS, 4, X, 1, Z), f32),
            pltpu.VMEM((6, X, Y, Z), f32),
            pltpu.VMEM((4, X, Y, Z), f32),
            pltpu.VMEM((3, X, Y, Z), f32),
            pltpu.SemaphoreType.DMA((2 + SWEEPS, 4)),
            pltpu.SemaphoreType.DMA((2 + SWEEPS, 4)),
        ],
        compiler_params=pltpu.CompilerParams(
            collective_id=0, has_side_effects=True, vmem_limit_bytes=60 * 1024 * 1024
        ),
    )(brick_work, damage, strain, seed_damage, seed_disp)
    return pl.pallas_call(
        pass_kernel,
        out_shape=(
            jax.ShapeDtypeStruct((X, Y, Z), f32),
            jax.ShapeDtypeStruct((3, X, Y, Z), f32),
        ),
        in_specs=[vmem, vmem],
        out_specs=(vmem, vmem),
    )(*state)


def pass_kernel(mu_ref, disp_ref, out_mu_ref, out_disp_ref):
    out_mu_ref[...] = mu_ref[...]
    for c in range(3):
        out_disp_ref[c] = disp_ref[c]


def solution(mesh):
    nx = mesh.shape["gx"]
    ny = mesh.shape["gy"]
    placed = (
        P("gx", "gy", None),
        P(None, "gx", "gy", None),
        P("gx", "gy", None),
        P(None, "gx", "gy", None),
        P("gx", "gy"),
    )
    return jax.shard_map(
        functools.partial(body, nx=nx, ny=ny),
        mesh=mesh,
        in_specs=placed,
        out_specs=(P("gx", "gy", None), P(None, "gx", "gy", None)),
        check_vma=False,
    )
```

```python
import functools

import jax
import jax.numpy as jnp
from jax import lax
from jax.experimental import pallas as pl
from jax.experimental.pallas import tpu as pltpu
from jax.sharding import PartitionSpec as P

SWEEPS = 3
RELAX_INNER = 8

RESIDUAL_STIFFNESS = 0.001
TOUGH_OVER_LENGTH = 0.5
TOUGH_TIMES_LENGTH = 0.25
MASS_SHIFT = 0.5
STIFF_SCALE = 0.25
CENTER_VALUE = 1.0
HALF_WIDTH = 0.75
NORMAL_WEIGHT = 1.5
RELAX_STEP = 0.5
NORMAL_FLOOR = 0.05

MESH = pl.DeviceIdType.MESH


def soft_of(d):
    return (1.0 - d) ** 2


def kernel(
    nx, ny,
    bw_ref, dmg_ref, strain_ref, sd_ref, sdisp_ref,
    out_mu_ref, out_disp_ref,
    dfr, dyl, dyh, sfr, syl, syh, faces, upd, invs, send_sem, recv_sem,
):
    X, Y, Z = dmg_ref.shape
    bx = lax.axis_index("gx")
    by = lax.axis_index("gy")
    has = (bx < nx - 1, bx > 0, by < ny - 1, by > 0)
    peers = ((bx + 1, by), (bx - 1, by), (bx, by + 1), (bx, by - 1))

    @pl.when(bx == 0)
    def _():
        dfr[:, 0] = jnp.zeros((2, Y, Z), jnp.float32)
        sfr[:, :, 0] = jnp.zeros((SWEEPS, 4, Y, Z), jnp.float32)

    @pl.when(bx == nx - 1)
    def _():
        dfr[:, X + 1] = jnp.zeros((2, Y, Z), jnp.float32)
        sfr[:, :, X + 1] = jnp.zeros((SWEEPS, 4, Y, Z), jnp.float32)

    @pl.when(by == 0)
    def _():
        dyl[...] = jnp.zeros(dyl.shape, jnp.float32)
        syl[...] = jnp.zeros(syl.shape, jnp.float32)

    @pl.when(by == ny - 1)
    def _():
        dyh[...] = jnp.zeros(dyh.shape, jnp.float32)
        syh[...] = jnp.zeros(syh.shape, jnp.float32)

    barrier = pltpu.get_barrier_semaphore()
    count = jnp.int32(0)
    for d in range(4):
        @pl.when(has[d])
        def _():
            pl.semaphore_signal(barrier, inc=1, device_id=peers[d], device_id_type=MESH)
        count = count + has[d].astype(jnp.int32)
    pl.semaphore_wait(barrier, count)

    def exchange(slot, routes):
        copies = []
        for d in range(4):
            src, dst = routes[d]
            copies.append(
                pltpu.make_async_remote_copy(
                    src_ref=src, dst_ref=dst,
                    send_sem=send_sem.at[slot, d], recv_sem=recv_sem.at[slot, d],
                    device_id=peers[d], device_id_type=MESH,
                )
            )
        for d in range(4):
            @pl.when(has[d])
            def _():
                copies[d].start()
        return copies

    def arrive(copies, dirs):
        opposite = (1, 0, 3, 2)
        for d in dirs:
            @pl.when(has[opposite[d]])
            def _():
                copies[d].wait_recv()

    def sent(copies):
        for d in range(4):
            @pl.when(has[d])
            def _():
                copies[d].wait_send()

    c_dmg = exchange(0, (
        (dmg_ref.at[X - 1:X], dfr.at[0, 0:1]),
        (dmg_ref.at[0:1], dfr.at[0, X + 1:X + 2]),
        (dmg_ref.at[:, Y - 1:Y], dyl.at[0]),
        (dmg_ref.at[:, 0:1], dyh.at[0]),
    ))
    c_str = exchange(1, (
        (strain_ref.at[0, X - 1:X], dfr.at[1, 0:1]),
        (strain_ref.at[0, 0:1], dfr.at[1, X + 1:X + 2]),
        (strain_ref.at[1, :, Y - 1:Y], dyl.at[1]),
        (strain_ref.at[1, :, 0:1], dyh.at[1]),
    ))
    dfr[0, 1:X + 1] = dmg_ref[...]
    dfr[1, 1:X + 1] = strain_ref[0]
    arrive(c_dmg, (2, 3))
    arrive(c_str, (2, 3))
    pending = [c_dmg, c_str]

    rows = lax.broadcasted_iota(jnp.int32, (Y, Z), 0)
    lanes = lax.broadcasted_iota(jnp.int32, (Y, Z), 1)

    def sides(center, nxp, nxm, lo, hi):
        yp = jnp.where(rows == Y - 1, hi, pltpu.roll(center, Y - 1, 0))
        ym = jnp.where(rows == 0, lo, pltpu.roll(center, 1, 0))
        zp = jnp.where(lanes == Z - 1, 0.0, pltpu.roll(center, Z - 1, 1))
        zm = jnp.where(lanes == 0, 0.0, pltpu.roll(center, 1, 1))
        return [nxp, nxm, yp, ym, zp, zm]

    def damage_sides(i):
        d = dfr[0, i + 1]
        return d, sides(d, dfr[0, i + 2], dfr[0, i], dyl[0, i], dyh[0, i])

    def prep(i, carry):
        d, ds = damage_sides(i)
        soft_center = soft_of(d) + RESIDUAL_STIFFNESS
        fs = [0.5 * (soft_center + soft_of(s) + RESIDUAL_STIFFNESS) for s in ds]
        total = fs[0]
        for k in range(6):
            faces[k, i] = fs[k]
            if k:
                total = total + fs[k]
        sx = strain_ref[0, i]
        sy = strain_ref[1, i]
        sz = strain_ref[2, i]
        energy = 0.5 * (sx * sx + sy * sy + sz * sz)
        inv_mu = 1.0 / (TOUGH_OVER_LENGTH + 2.0 * energy + 6.0 * TOUGH_TIMES_LENGTH)
        inv_lam = 1.0 / (MASS_SHIFT + STIFF_SCALE * total)
        invs[0, i] = inv_mu
        invs[1, i] = inv_lam
        invs[2, i] = TOUGH_OVER_LENGTH + 2.0 * energy
        mu0 = inv_mu * sd_ref[i] / CENTER_VALUE
        upd[0, i] = mu0
        sfr[0, 0, i + 1] = mu0
        for c in range(3):
            lam0 = inv_lam * sdisp_ref[c, i] / CENTER_VALUE
            upd[1 + c, i] = lam0
            sfr[0, 1 + c, i + 1] = lam0
        return carry

    lax.fori_loop(1, X - 1, prep, 0)
    arrive(c_dmg, (0, 1))
    arrive(c_str, (0, 1))
    for i in (0, X - 1):
        prep(i, 0)

    def state_routes(r):
        return (
            (sfr.at[r, :, X:X + 1], sfr.at[r, :, 0:1]),
            (sfr.at[r, :, 1:2], sfr.at[r, :, X + 1:X + 2]),
            (sfr.at[r, :, 1:X + 1, Y - 1:Y], syl.at[r]),
            (sfr.at[r, :, 1:X + 1, 0:1], syh.at[r]),
        )

    ratio = CENTER_VALUE / HALF_WIDTH
    rho = 1.0 / ratio
    for sweep in range(SWEEPS):
        r = sweep
        copies = exchange(2 + r, state_routes(r))
        pending.append(copies)
        arrive(copies, (2, 3))
        rho_next = 1.0 / (2.0 * ratio - rho)
        keep = rho_next * rho
        gain = 2.0 * rho_next / HALF_WIDTH
        rho = rho_next
        last = sweep == SWEEPS - 1

        def step(i, carry, r=r, keep=keep, gain=gain, last=last):
            mu = sfr[r, 0, i + 1]
            mus = sides(mu, sfr[r, 0, i + 2], sfr[r, 0, i], syl[r, 0, i], syh[r, 0, i])
            energy_diag = invs[2, i]
            damage_part = energy_diag * mu + TOUGH_TIMES_LENGTH * sum(mu - s for s in mus)
            fs = [faces[k, i] for k in range(6)]
            wxm = 2.0 * (dfr[0, i] - 1.0) * dfr[1, i] * mus[1]
            wxp = 2.0 * (dfr[0, i + 2] - 1.0) * dfr[1, i + 2] * mus[0]
            d = dfr[0, i + 1]
            wy = 2.0 * (d - 1.0) * strain_ref[1, i] * mu
            wy_lo = 2.0 * (dyl[0, i] - 1.0) * dyl[1, i] * syl[r, 0, i]
            wy_hi = 2.0 * (dyh[0, i] - 1.0) * dyh[1, i] * syh[r, 0, i]
            wy_p = jnp.where(rows == Y - 1, wy_hi, pltpu.roll(wy, Y - 1, 0))
            wy_m = jnp.where(rows == 0, wy_lo, pltpu.roll(wy, 1, 0))
            wz = 2.0 * (d - 1.0) * strain_ref[2, i] * mu
            wz_p = jnp.where(lanes == Z - 1, 0.0, pltpu.roll(wz, Z - 1, 1))
            wz_m = jnp.where(lanes == 0, 0.0, pltpu.roll(wz, 1, 1))
            transfer = (
                0.5 * (wxm - wxp),
                0.5 * (wy_m - wy_p),
                0.5 * (wz_m - wz_p),
            )
            inv_mu = invs[0, i]
            inv_lam = invs[1, i]
            residual_mu = sd_ref[i] - damage_part
            new_upd = keep * upd[0, i] + gain * inv_mu * residual_mu
            new_mu = mu + new_upd
            upd[0, i] = new_upd
            lams = []
            for c in range(3):
                lam = sfr[r, 1 + c, i + 1]
                ls = sides(lam, sfr[r, 1 + c, i + 2], sfr[r, 1 + c, i],
                           syl[r, 1 + c, i], syh[r, 1 + c, i])
                disp = MASS_SHIFT * lam + STIFF_SCALE * sum(
                    fs[k] * (lam - ls[k]) for k in range(6))
                residual = sdisp_ref[c, i] - (disp + transfer[c])
                nu = keep * upd[1 + c, i] + gain * inv_lam * residual
                upd[1 + c, i] = nu
                lams.append(lam + nu)
            if not last:
                sfr[r + 1, 0, i + 1] = new_mu
                for c in range(3):
                    sfr[r + 1, 1 + c, i + 1] = lams[c]
            else:
                out_mu_ref[i] = new_mu
                _, ds = damage_sides(i)
                grad = [0.5 * (ds[0] - ds[1]), 0.5 * (ds[2] - ds[3]), 0.5 * (ds[4] - ds[5])]
                length = jnp.sqrt(jnp.maximum(
                    grad[0] * grad[0] + grad[1] * grad[1] + grad[2] * grad[2], NORMAL_FLOOR))
                normal = [g / length for g in grad]
                size = normal[0] * normal[0] + normal[1] * normal[1] + normal[2] * normal[2]
                along = normal[0] * lams[0] + normal[1] * lams[1] + normal[2] * lams[2]
                a = RELAX_STEP / RELAX_INNER
                factor = 1.0 - a * (1.0 + NORMAL_WEIGHT * size)
                power = factor
                for _ in range(3):
                    power = power * power
                total = power
                work = bw_ref[0, 0]
                for level in range(2, 5):
                    total = jnp.where(work >= level, total * power, total)
                pull = NORMAL_WEIGHT * (1.0 - total) / (1.0 + NORMAL_WEIGHT * size)
                for c in range(3):
                    out_disp_ref[c, i] = lams[c] - (pull * along) * normal[c]
            return carry

        lax.fori_loop(1, X - 1, step, 0)
        arrive(copies, (0, 1))
        for i in (0, X - 1):
            step(i, 0)

    for copies in pending:
        sent(copies)


def body(damage, strain, seed_damage, seed_disp, brick_work, nx, ny):
    X, Y, Z = damage.shape
    f32 = jnp.float32
    vmem = pl.BlockSpec(memory_space=pltpu.VMEM)
    state = pl.pallas_call(
        functools.partial(kernel, nx, ny),
        out_shape=(
            jax.ShapeDtypeStruct((X, Y, Z), f32),
            jax.ShapeDtypeStruct((3, X, Y, Z), f32),
        ),
        in_specs=[pl.BlockSpec(memory_space=pltpu.SMEM), vmem, vmem, vmem, vmem],
        out_specs=(vmem, vmem),
        scratch_shapes=[
            pltpu.VMEM((2, X + 2, Y, Z), f32),
            pltpu.VMEM((2, X, 1, Z), f32),
            pltpu.VMEM((2, X, 1, Z), f32),
            pltpu.VMEM((SWEEPS, 4, X + 2, Y, Z), f32),
            pltpu.VMEM((SWEEPS, 4, X, 1, Z), f32),
            pltpu.VMEM((SWEEPS, 4, X, 1, Z), f32),
            pltpu.VMEM((6, X, Y, Z), f32),
            pltpu.VMEM((4, X, Y, Z), f32),
            pltpu.VMEM((3, X, Y, Z), f32),
            pltpu.SemaphoreType.DMA((2 + SWEEPS, 4)),
            pltpu.SemaphoreType.DMA((2 + SWEEPS, 4)),
        ],
        compiler_params=pltpu.CompilerParams(
            collective_id=0, has_side_effects=True, vmem_limit_bytes=60 * 1024 * 1024
        ),
    )(brick_work, damage, strain, seed_damage, seed_disp)
    mu_block = pl.BlockSpec((X // 4, Y, Z), lambda i: (i, 0, 0))
    disp_block = pl.BlockSpec((3, X // 4, Y, Z), lambda i: (0, i, 0, 0))
    return pl.pallas_call(
        pass_kernel,
        out_shape=(
            jax.ShapeDtypeStruct((X, Y, Z), f32),
            jax.ShapeDtypeStruct((3, X, Y, Z), f32),
        ),
        grid=(4,),
        in_specs=[mu_block, disp_block],
        out_specs=(mu_block, disp_block),
    )(*state)


def pass_kernel(mu_ref, disp_ref, out_mu_ref, out_disp_ref):
    out_mu_ref[...] = mu_ref[...]
    out_disp_ref[...] = disp_ref[...]


def solution(mesh):
    nx = mesh.shape["gx"]
    ny = mesh.shape["gy"]
    placed = (
        P("gx", "gy", None),
        P(None, "gx", "gy", None),
        P("gx", "gy", None),
        P(None, "gx", "gy", None),
        P("gx", "gy"),
    )
    return jax.shard_map(
        functools.partial(body, nx=nx, ny=ny),
        mesh=mesh,
        in_specs=placed,
        out_specs=(P("gx", "gy", None), P(None, "gx", "gy", None)),
        check_vma=False,
    )
```

```python
import functools

import jax
import jax.numpy as jnp
from jax import lax
from jax.experimental import pallas as pl
from jax.experimental.pallas import tpu as pltpu
from jax.sharding import PartitionSpec as P

SWEEPS = 3
RELAX_INNER = 8

RESIDUAL_STIFFNESS = 0.001
TOUGH_OVER_LENGTH = 0.5
TOUGH_TIMES_LENGTH = 0.25
MASS_SHIFT = 0.5
STIFF_SCALE = 0.25
CENTER_VALUE = 1.0
HALF_WIDTH = 0.75
NORMAL_WEIGHT = 1.5
RELAX_STEP = 0.5
NORMAL_FLOOR = 0.05

MESH = pl.DeviceIdType.MESH


def soft_of(d):
    return (1.0 - d) ** 2


def kernel(
    nx, ny,
    bw_ref, dmg_ref, strain_ref, sd_ref, sdisp_ref,
    out_mu_ref, out_disp_ref,
    dfr, dyl, dyh, sfr, syl, syh, faces, upd, invs, send_sem, recv_sem,
):
    X, Y, Z = dmg_ref.shape
    bx = lax.axis_index("gx")
    by = lax.axis_index("gy")
    has = (bx < nx - 1, bx > 0, by < ny - 1, by > 0)
    peers = ((bx + 1, by), (bx - 1, by), (bx, by + 1), (bx, by - 1))

    @pl.when(bx == 0)
    def _():
        dfr[:, 0] = jnp.zeros((2, Y, Z), jnp.float32)
        sfr[:, :, 0] = jnp.zeros((SWEEPS, 4, Y, Z), jnp.float32)

    @pl.when(bx == nx - 1)
    def _():
        dfr[:, X + 1] = jnp.zeros((2, Y, Z), jnp.float32)
        sfr[:, :, X + 1] = jnp.zeros((SWEEPS, 4, Y, Z), jnp.float32)

    @pl.when(by == 0)
    def _():
        dyl[...] = jnp.zeros(dyl.shape, jnp.float32)
        syl[...] = jnp.zeros(syl.shape, jnp.float32)

    @pl.when(by == ny - 1)
    def _():
        dyh[...] = jnp.zeros(dyh.shape, jnp.float32)
        syh[...] = jnp.zeros(syh.shape, jnp.float32)

    barrier = pltpu.get_barrier_semaphore()
    count = jnp.int32(0)
    for d in range(4):
        @pl.when(has[d])
        def _():
            pl.semaphore_signal(barrier, inc=1, device_id=peers[d], device_id_type=MESH)
        count = count + has[d].astype(jnp.int32)
    pl.semaphore_wait(barrier, count)

    def exchange(slot, routes):
        copies = []
        for d in range(4):
            src, dst = routes[d]
            copies.append(
                pltpu.make_async_remote_copy(
                    src_ref=src, dst_ref=dst,
                    send_sem=send_sem.at[slot, d], recv_sem=recv_sem.at[slot, d],
                    device_id=peers[d], device_id_type=MESH,
                )
            )
        for d in range(4):
            @pl.when(has[d])
            def _():
                copies[d].start()
        return copies

    def arrive(copies, dirs):
        opposite = (1, 0, 3, 2)
        for d in dirs:
            @pl.when(has[opposite[d]])
            def _():
                copies[d].wait_recv()

    def sent(copies):
        for d in range(4):
            @pl.when(has[d])
            def _():
                copies[d].wait_send()

    c_dmg = exchange(0, (
        (dmg_ref.at[X - 1:X], dfr.at[0, 0:1]),
        (dmg_ref.at[0:1], dfr.at[0, X + 1:X + 2]),
        (dmg_ref.at[:, Y - 1:Y], dyl.at[0]),
        (dmg_ref.at[:, 0:1], dyh.at[0]),
    ))
    c_str = exchange(1, (
        (strain_ref.at[0, X - 1:X], dfr.at[1, 0:1]),
        (strain_ref.at[0, 0:1], dfr.at[1, X + 1:X + 2]),
        (strain_ref.at[1, :, Y - 1:Y], dyl.at[1]),
        (strain_ref.at[1, :, 0:1], dyh.at[1]),
    ))
    dfr[0, 1:X + 1] = dmg_ref[...]
    dfr[1, 1:X + 1] = strain_ref[0]
    arrive(c_dmg, (2, 3))
    arrive(c_str, (2, 3))
    pending = [c_dmg, c_str]

    rows = lax.broadcasted_iota(jnp.int32, (Y, Z), 0)
    lanes = lax.broadcasted_iota(jnp.int32, (Y, Z), 1)

    def sides(center, nxp, nxm, lo, hi):
        yp = jnp.where(rows == Y - 1, hi, pltpu.roll(center, Y - 1, 0))
        ym = jnp.where(rows == 0, lo, pltpu.roll(center, 1, 0))
        zp = jnp.where(lanes == Z - 1, 0.0, pltpu.roll(center, Z - 1, 1))
        zm = jnp.where(lanes == 0, 0.0, pltpu.roll(center, 1, 1))
        return [nxp, nxm, yp, ym, zp, zm]

    def damage_sides(i):
        d = dfr[0, i + 1]
        return d, sides(d, dfr[0, i + 2], dfr[0, i], dyl[0, i], dyh[0, i])

    def prep(i, carry):
        d, ds = damage_sides(i)
        soft_center = soft_of(d) + RESIDUAL_STIFFNESS
        fs = [0.5 * (soft_center + soft_of(s) + RESIDUAL_STIFFNESS) for s in ds]
        total = fs[0]
        for k in range(6):
            faces[k, i] = fs[k]
            if k:
                total = total + fs[k]
        sx = strain_ref[0, i]
        sy = strain_ref[1, i]
        sz = strain_ref[2, i]
        energy = 0.5 * (sx * sx + sy * sy + sz * sz)
        inv_mu = 1.0 / (TOUGH_OVER_LENGTH + 2.0 * energy + 6.0 * TOUGH_TIMES_LENGTH)
        inv_lam = 1.0 / (MASS_SHIFT + STIFF_SCALE * total)
        invs[0, i] = inv_mu
        invs[1, i] = inv_lam
        invs[2, i] = TOUGH_OVER_LENGTH + 2.0 * energy
        mu0 = inv_mu * sd_ref[i] / CENTER_VALUE
        upd[0, i] = mu0
        sfr[0, 0, i + 1] = mu0
        for c in range(3):
            lam0 = inv_lam * sdisp_ref[c, i] / CENTER_VALUE
            upd[1 + c, i] = lam0
            sfr[0, 1 + c, i + 1] = lam0
        return carry

    lax.fori_loop(1, X - 1, prep, 0)
    arrive(c_dmg, (0, 1))
    arrive(c_str, (0, 1))
    for i in (0, X - 1):
        prep(i, 0)

    def state_routes(r):
        return (
            (sfr.at[r, :, X:X + 1], sfr.at[r, :, 0:1]),
            (sfr.at[r, :, 1:2], sfr.at[r, :, X + 1:X + 2]),
            (sfr.at[r, :, 1:X + 1, Y - 1:Y], syl.at[r]),
            (sfr.at[r, :, 1:X + 1, 0:1], syh.at[r]),
        )

    ratio = CENTER_VALUE / HALF_WIDTH
    rho = 1.0 / ratio
    for sweep in range(SWEEPS):
        r = sweep
        copies = exchange(2 + r, state_routes(r))
        pending.append(copies)
        arrive(copies, (2, 3))
        rho_next = 1.0 / (2.0 * ratio - rho)
        keep = rho_next * rho
        gain = 2.0 * rho_next / HALF_WIDTH
        rho = rho_next
        last = sweep == SWEEPS - 1

        def step(i, carry, r=r, keep=keep, gain=gain, last=last):
            mu = sfr[r, 0, i + 1]
            mus = sides(mu, sfr[r, 0, i + 2], sfr[r, 0, i], syl[r, 0, i], syh[r, 0, i])
            energy_diag = invs[2, i]
            damage_part = energy_diag * mu + TOUGH_TIMES_LENGTH * sum(mu - s for s in mus)
            fs = [faces[k, i] for k in range(6)]
            wxm = 2.0 * (dfr[0, i] - 1.0) * dfr[1, i] * mus[1]
            wxp = 2.0 * (dfr[0, i + 2] - 1.0) * dfr[1, i + 2] * mus[0]
            d = dfr[0, i + 1]
            wy = 2.0 * (d - 1.0) * strain_ref[1, i] * mu
            wy_lo = 2.0 * (dyl[0, i] - 1.0) * dyl[1, i] * syl[r, 0, i]
            wy_hi = 2.0 * (dyh[0, i] - 1.0) * dyh[1, i] * syh[r, 0, i]
            wy_p = jnp.where(rows == Y - 1, wy_hi, pltpu.roll(wy, Y - 1, 0))
            wy_m = jnp.where(rows == 0, wy_lo, pltpu.roll(wy, 1, 0))
            wz = 2.0 * (d - 1.0) * strain_ref[2, i] * mu
            wz_p = jnp.where(lanes == Z - 1, 0.0, pltpu.roll(wz, Z - 1, 1))
            wz_m = jnp.where(lanes == 0, 0.0, pltpu.roll(wz, 1, 1))
            transfer = (
                0.5 * (wxm - wxp),
                0.5 * (wy_m - wy_p),
                0.5 * (wz_m - wz_p),
            )
            inv_mu = invs[0, i]
            inv_lam = invs[1, i]
            residual_mu = sd_ref[i] - damage_part
            new_upd = keep * upd[0, i] + gain * inv_mu * residual_mu
            new_mu = mu + new_upd
            upd[0, i] = new_upd
            lams = []
            for c in range(3):
                lam = sfr[r, 1 + c, i + 1]
                ls = sides(lam, sfr[r, 1 + c, i + 2], sfr[r, 1 + c, i],
                           syl[r, 1 + c, i], syh[r, 1 + c, i])
                disp = MASS_SHIFT * lam + STIFF_SCALE * sum(
                    fs[k] * (lam - ls[k]) for k in range(6))
                residual = sdisp_ref[c, i] - (disp + transfer[c])
                nu = keep * upd[1 + c, i] + gain * inv_lam * residual
                upd[1 + c, i] = nu
                lams.append(lam + nu)
            if not last:
                sfr[r + 1, 0, i + 1] = new_mu
                for c in range(3):
                    sfr[r + 1, 1 + c, i + 1] = lams[c]
            else:
                out_mu_ref[i] = new_mu
                _, ds = damage_sides(i)
                grad = [0.5 * (ds[0] - ds[1]), 0.5 * (ds[2] - ds[3]), 0.5 * (ds[4] - ds[5])]
                length = jnp.sqrt(jnp.maximum(
                    grad[0] * grad[0] + grad[1] * grad[1] + grad[2] * grad[2], NORMAL_FLOOR))
                normal = [g / length for g in grad]
                size = normal[0] * normal[0] + normal[1] * normal[1] + normal[2] * normal[2]
                along = normal[0] * lams[0] + normal[1] * lams[1] + normal[2] * lams[2]
                a = RELAX_STEP / RELAX_INNER
                factor = 1.0 - a * (1.0 + NORMAL_WEIGHT * size)
                power = factor
                for _ in range(3):
                    power = power * power
                total = power
                work = bw_ref[0, 0]
                for level in range(2, 5):
                    total = jnp.where(work >= level, total * power, total)
                pull = NORMAL_WEIGHT * (1.0 - total) / (1.0 + NORMAL_WEIGHT * size)
                for c in range(3):
                    out_disp_ref[c, i] = lams[c] - (pull * along) * normal[c]
            return carry

        lax.fori_loop(1, X - 1, step, 0)
        arrive(copies, (0, 1))
        for i in (0, X - 1):
            step(i, 0)

    for copies in pending:
        sent(copies)


def body(damage, strain, seed_damage, seed_disp, brick_work, nx, ny):
    X, Y, Z = damage.shape
    f32 = jnp.float32
    vmem = pl.BlockSpec(memory_space=pltpu.VMEM)
    state = pl.pallas_call(
        functools.partial(kernel, nx, ny),
        out_shape=(
            jax.ShapeDtypeStruct((X, Y, Z), f32),
            jax.ShapeDtypeStruct((3, X, Y, Z), f32),
        ),
        in_specs=[pl.BlockSpec(memory_space=pltpu.SMEM), vmem, vmem, vmem, vmem],
        out_specs=(vmem, vmem),
        scratch_shapes=[
            pltpu.VMEM((2, X + 2, Y, Z), f32),
            pltpu.VMEM((2, X, 1, Z), f32),
            pltpu.VMEM((2, X, 1, Z), f32),
            pltpu.VMEM((SWEEPS, 4, X + 2, Y, Z), f32),
            pltpu.VMEM((SWEEPS, 4, X, 1, Z), f32),
            pltpu.VMEM((SWEEPS, 4, X, 1, Z), f32),
            pltpu.VMEM((6, X, Y, Z), f32),
            pltpu.VMEM((4, X, Y, Z), f32),
            pltpu.VMEM((3, X, Y, Z), f32),
            pltpu.SemaphoreType.DMA((2 + SWEEPS, 4)),
            pltpu.SemaphoreType.DMA((2 + SWEEPS, 4)),
        ],
        compiler_params=pltpu.CompilerParams(
            collective_id=0, has_side_effects=True, vmem_limit_bytes=60 * 1024 * 1024
        ),
    )(brick_work, damage, strain, seed_damage, seed_disp)
    hbm = pl.BlockSpec(memory_space=pl.ANY)
    return pl.pallas_call(
        pass_kernel,
        out_shape=(
            jax.ShapeDtypeStruct((X, Y, Z), f32),
            jax.ShapeDtypeStruct((3, X, Y, Z), f32),
        ),
        in_specs=[hbm, hbm],
        out_specs=(hbm, hbm),
        scratch_shapes=[pltpu.SemaphoreType.DMA((2,))],
    )(*state)


def pass_kernel(mu_ref, disp_ref, out_mu_ref, out_disp_ref, sems):
    first = pltpu.make_async_copy(mu_ref, out_mu_ref, sems.at[0])
    second = pltpu.make_async_copy(disp_ref, out_disp_ref, sems.at[1])
    first.start()
    second.start()
    first.wait()
    second.wait()


def solution(mesh):
    nx = mesh.shape["gx"]
    ny = mesh.shape["gy"]
    placed = (
        P("gx", "gy", None),
        P(None, "gx", "gy", None),
        P("gx", "gy", None),
        P(None, "gx", "gy", None),
        P("gx", "gy"),
    )
    return jax.shard_map(
        functools.partial(body, nx=nx, ny=ny),
        mesh=mesh,
        in_specs=placed,
        out_specs=(P("gx", "gy", None), P(None, "gx", "gy", None)),
        check_vma=False,
    )
```

```python
import functools

import jax
import jax.numpy as jnp
from jax import lax
from jax.experimental import pallas as pl
from jax.experimental.pallas import tpu as pltpu
from jax.sharding import PartitionSpec as P

SWEEPS = 3
RELAX_INNER = 8

RESIDUAL_STIFFNESS = 0.001
TOUGH_OVER_LENGTH = 0.5
TOUGH_TIMES_LENGTH = 0.25
MASS_SHIFT = 0.5
STIFF_SCALE = 0.25
CENTER_VALUE = 1.0
HALF_WIDTH = 0.75
NORMAL_WEIGHT = 1.5
RELAX_STEP = 0.5
NORMAL_FLOOR = 0.05

MESH = pl.DeviceIdType.MESH


def soft_of(d):
    return (1.0 - d) ** 2


def kernel(
    nx, ny,
    bw_ref, dmg_hbm, strain_hbm, sd_hbm, sdisp_hbm,
    out_mu_ref, out_disp_ref,
    dfr, dyl, dyh, sfr, syl, syh, faces, upd, invs, send_sem, recv_sem,
    dmg_ref, strain_ref, sd_ref, sdisp_ref, load_sem,
):
    X, Y, Z = dmg_ref.shape
    bx = lax.axis_index("gx")
    by = lax.axis_index("gy")
    has = (bx < nx - 1, bx > 0, by < ny - 1, by > 0)
    peers = ((bx + 1, by), (bx - 1, by), (bx, by + 1), (bx, by - 1))

    @pl.when(bx == 0)
    def _():
        dfr[:, 0] = jnp.zeros((2, Y, Z), jnp.float32)
        sfr[:, :, 0] = jnp.zeros((SWEEPS, 4, Y, Z), jnp.float32)

    @pl.when(bx == nx - 1)
    def _():
        dfr[:, X + 1] = jnp.zeros((2, Y, Z), jnp.float32)
        sfr[:, :, X + 1] = jnp.zeros((SWEEPS, 4, Y, Z), jnp.float32)

    @pl.when(by == 0)
    def _():
        dyl[...] = jnp.zeros(dyl.shape, jnp.float32)
        syl[...] = jnp.zeros(syl.shape, jnp.float32)

    @pl.when(by == ny - 1)
    def _():
        dyh[...] = jnp.zeros(dyh.shape, jnp.float32)
        syh[...] = jnp.zeros(syh.shape, jnp.float32)

    barrier = pltpu.get_barrier_semaphore()
    count = jnp.int32(0)
    for d in range(4):
        @pl.when(has[d])
        def _():
            pl.semaphore_signal(barrier, inc=1, device_id=peers[d], device_id_type=MESH)
        count = count + has[d].astype(jnp.int32)
    loads = [
        pltpu.make_async_copy(src, dst, load_sem.at[k])
        for k, (src, dst) in enumerate(((dmg_hbm, dmg_ref), (strain_hbm, strain_ref),
                                        (sd_hbm, sd_ref), (sdisp_hbm, sdisp_ref)))
    ]
    for copy in loads:
        copy.start()
    for copy in loads:
        copy.wait()
    pl.semaphore_wait(barrier, count)

    def exchange(slot, routes):
        copies = []
        for d in range(4):
            src, dst = routes[d]
            copies.append(
                pltpu.make_async_remote_copy(
                    src_ref=src, dst_ref=dst,
                    send_sem=send_sem.at[slot, d], recv_sem=recv_sem.at[slot, d],
                    device_id=peers[d], device_id_type=MESH,
                )
            )
        for d in range(4):
            @pl.when(has[d])
            def _():
                copies[d].start()
        return copies

    def arrive(copies, dirs):
        opposite = (1, 0, 3, 2)
        for d in dirs:
            @pl.when(has[opposite[d]])
            def _():
                copies[d].wait_recv()

    def sent(copies):
        for d in range(4):
            @pl.when(has[d])
            def _():
                copies[d].wait_send()

    c_dmg = exchange(0, (
        (dmg_ref.at[X - 1:X], dfr.at[0, 0:1]),
        (dmg_ref.at[0:1], dfr.at[0, X + 1:X + 2]),
        (dmg_ref.at[:, Y - 1:Y], dyl.at[0]),
        (dmg_ref.at[:, 0:1], dyh.at[0]),
    ))
    c_str = exchange(1, (
        (strain_ref.at[0, X - 1:X], dfr.at[1, 0:1]),
        (strain_ref.at[0, 0:1], dfr.at[1, X + 1:X + 2]),
        (strain_ref.at[1, :, Y - 1:Y], dyl.at[1]),
        (strain_ref.at[1, :, 0:1], dyh.at[1]),
    ))
    dfr[0, 1:X + 1] = dmg_ref[...]
    dfr[1, 1:X + 1] = strain_ref[0]
    arrive(c_dmg, (2, 3))
    arrive(c_str, (2, 3))
    pending = [c_dmg, c_str]

    rows = lax.broadcasted_iota(jnp.int32, (Y, Z), 0)
    lanes = lax.broadcasted_iota(jnp.int32, (Y, Z), 1)

    def sides(center, nxp, nxm, lo, hi):
        yp = jnp.where(rows == Y - 1, hi, pltpu.roll(center, Y - 1, 0))
        ym = jnp.where(rows == 0, lo, pltpu.roll(center, 1, 0))
        zp = jnp.where(lanes == Z - 1, 0.0, pltpu.roll(center, Z - 1, 1))
        zm = jnp.where(lanes == 0, 0.0, pltpu.roll(center, 1, 1))
        return [nxp, nxm, yp, ym, zp, zm]

    def damage_sides(i):
        d = dfr[0, i + 1]
        return d, sides(d, dfr[0, i + 2], dfr[0, i], dyl[0, i], dyh[0, i])

    def prep(i, carry):
        d, ds = damage_sides(i)
        soft_center = soft_of(d) + RESIDUAL_STIFFNESS
        fs = [0.5 * (soft_center + soft_of(s) + RESIDUAL_STIFFNESS) for s in ds]
        total = fs[0]
        for k in range(6):
            faces[k, i] = fs[k]
            if k:
                total = total + fs[k]
        sx = strain_ref[0, i]
        sy = strain_ref[1, i]
        sz = strain_ref[2, i]
        energy = 0.5 * (sx * sx + sy * sy + sz * sz)
        inv_mu = 1.0 / (TOUGH_OVER_LENGTH + 2.0 * energy + 6.0 * TOUGH_TIMES_LENGTH)
        inv_lam = 1.0 / (MASS_SHIFT + STIFF_SCALE * total)
        invs[0, i] = inv_mu
        invs[1, i] = inv_lam
        invs[2, i] = TOUGH_OVER_LENGTH + 2.0 * energy
        mu0 = inv_mu * sd_ref[i] / CENTER_VALUE
        upd[0, i] = mu0
        sfr[0, 0, i + 1] = mu0
        for c in range(3):
            lam0 = inv_lam * sdisp_ref[c, i] / CENTER_VALUE
            upd[1 + c, i] = lam0
            sfr[0, 1 + c, i + 1] = lam0
        return carry

    lax.fori_loop(1, X - 1, prep, 0)
    arrive(c_dmg, (0, 1))
    arrive(c_str, (0, 1))
    for i in (0, X - 1):
        prep(i, 0)

    def state_routes(r):
        return (
            (sfr.at[r, :, X:X + 1], sfr.at[r, :, 0:1]),
            (sfr.at[r, :, 1:2], sfr.at[r, :, X + 1:X + 2]),
            (sfr.at[r, :, 1:X + 1, Y - 1:Y], syl.at[r]),
            (sfr.at[r, :, 1:X + 1, 0:1], syh.at[r]),
        )

    ratio = CENTER_VALUE / HALF_WIDTH
    rho = 1.0 / ratio
    for sweep in range(SWEEPS):
        r = sweep
        copies = exchange(2 + r, state_routes(r))
        pending.append(copies)
        arrive(copies, (2, 3))
        rho_next = 1.0 / (2.0 * ratio - rho)
        keep = rho_next * rho
        gain = 2.0 * rho_next / HALF_WIDTH
        rho = rho_next
        last = sweep == SWEEPS - 1

        def step(i, carry, r=r, keep=keep, gain=gain, last=last):
            mu = sfr[r, 0, i + 1]
            mus = sides(mu, sfr[r, 0, i + 2], sfr[r, 0, i], syl[r, 0, i], syh[r, 0, i])
            energy_diag = invs[2, i]
            damage_part = energy_diag * mu + TOUGH_TIMES_LENGTH * sum(mu - s for s in mus)
            fs = [faces[k, i] for k in range(6)]
            wxm = 2.0 * (dfr[0, i] - 1.0) * dfr[1, i] * mus[1]
            wxp = 2.0 * (dfr[0, i + 2] - 1.0) * dfr[1, i + 2] * mus[0]
            d = dfr[0, i + 1]
            wy = 2.0 * (d - 1.0) * strain_ref[1, i] * mu
            wy_lo = 2.0 * (dyl[0, i] - 1.0) * dyl[1, i] * syl[r, 0, i]
            wy_hi = 2.0 * (dyh[0, i] - 1.0) * dyh[1, i] * syh[r, 0, i]
            wy_p = jnp.where(rows == Y - 1, wy_hi, pltpu.roll(wy, Y - 1, 0))
            wy_m = jnp.where(rows == 0, wy_lo, pltpu.roll(wy, 1, 0))
            wz = 2.0 * (d - 1.0) * strain_ref[2, i] * mu
            wz_p = jnp.where(lanes == Z - 1, 0.0, pltpu.roll(wz, Z - 1, 1))
            wz_m = jnp.where(lanes == 0, 0.0, pltpu.roll(wz, 1, 1))
            transfer = (
                0.5 * (wxm - wxp),
                0.5 * (wy_m - wy_p),
                0.5 * (wz_m - wz_p),
            )
            inv_mu = invs[0, i]
            inv_lam = invs[1, i]
            residual_mu = sd_ref[i] - damage_part
            new_upd = keep * upd[0, i] + gain * inv_mu * residual_mu
            new_mu = mu + new_upd
            upd[0, i] = new_upd
            lams = []
            for c in range(3):
                lam = sfr[r, 1 + c, i + 1]
                ls = sides(lam, sfr[r, 1 + c, i + 2], sfr[r, 1 + c, i],
                           syl[r, 1 + c, i], syh[r, 1 + c, i])
                disp = MASS_SHIFT * lam + STIFF_SCALE * sum(
                    fs[k] * (lam - ls[k]) for k in range(6))
                residual = sdisp_ref[c, i] - (disp + transfer[c])
                nu = keep * upd[1 + c, i] + gain * inv_lam * residual
                upd[1 + c, i] = nu
                lams.append(lam + nu)
            if not last:
                sfr[r + 1, 0, i + 1] = new_mu
                for c in range(3):
                    sfr[r + 1, 1 + c, i + 1] = lams[c]
            else:
                out_mu_ref[i] = new_mu
                _, ds = damage_sides(i)
                grad = [0.5 * (ds[0] - ds[1]), 0.5 * (ds[2] - ds[3]), 0.5 * (ds[4] - ds[5])]
                length = jnp.sqrt(jnp.maximum(
                    grad[0] * grad[0] + grad[1] * grad[1] + grad[2] * grad[2], NORMAL_FLOOR))
                normal = [g / length for g in grad]
                size = normal[0] * normal[0] + normal[1] * normal[1] + normal[2] * normal[2]
                along = normal[0] * lams[0] + normal[1] * lams[1] + normal[2] * lams[2]
                a = RELAX_STEP / RELAX_INNER
                factor = 1.0 - a * (1.0 + NORMAL_WEIGHT * size)
                power = factor
                for _ in range(3):
                    power = power * power
                total = power
                work = bw_ref[0, 0]
                for level in range(2, 5):
                    total = jnp.where(work >= level, total * power, total)
                pull = NORMAL_WEIGHT * (1.0 - total) / (1.0 + NORMAL_WEIGHT * size)
                for c in range(3):
                    out_disp_ref[c, i] = lams[c] - (pull * along) * normal[c]
            return carry

        lax.fori_loop(1, X - 1, step, 0)
        arrive(copies, (0, 1))
        for i in (0, X - 1):
            step(i, 0)

    for copies in pending:
        sent(copies)


def body(damage, strain, seed_damage, seed_disp, brick_work, nx, ny):
    X, Y, Z = damage.shape
    f32 = jnp.float32
    vmem = pl.BlockSpec(memory_space=pltpu.VMEM)
    state = pl.pallas_call(
        functools.partial(kernel, nx, ny),
        out_shape=(
            jax.ShapeDtypeStruct((X, Y, Z), f32),
            jax.ShapeDtypeStruct((3, X, Y, Z), f32),
        ),
        in_specs=[pl.BlockSpec(memory_space=pltpu.SMEM)] + [pl.BlockSpec(memory_space=pl.ANY)] * 4,
        out_specs=(vmem, vmem),
        scratch_shapes=[
            pltpu.VMEM((2, X + 2, Y, Z), f32),
            pltpu.VMEM((2, X, 1, Z), f32),
            pltpu.VMEM((2, X, 1, Z), f32),
            pltpu.VMEM((SWEEPS, 4, X + 2, Y, Z), f32),
            pltpu.VMEM((SWEEPS, 4, X, 1, Z), f32),
            pltpu.VMEM((SWEEPS, 4, X, 1, Z), f32),
            pltpu.VMEM((6, X, Y, Z), f32),
            pltpu.VMEM((4, X, Y, Z), f32),
            pltpu.VMEM((3, X, Y, Z), f32),
            pltpu.SemaphoreType.DMA((2 + SWEEPS, 4)),
            pltpu.SemaphoreType.DMA((2 + SWEEPS, 4)),
            pltpu.VMEM((X, Y, Z), f32),
            pltpu.VMEM((3, X, Y, Z), f32),
            pltpu.VMEM((X, Y, Z), f32),
            pltpu.VMEM((3, X, Y, Z), f32),
            pltpu.SemaphoreType.DMA((4,)),
        ],
        compiler_params=pltpu.CompilerParams(
            collective_id=0, has_side_effects=True, vmem_limit_bytes=60 * 1024 * 1024
        ),
    )(brick_work, damage, strain, seed_damage, seed_disp)
    return pl.pallas_call(
        pass_kernel,
        out_shape=(
            jax.ShapeDtypeStruct((X, Y, Z), f32),
            jax.ShapeDtypeStruct((3, X, Y, Z), f32),
        ),
        in_specs=[vmem, vmem],
        out_specs=(vmem, vmem),
    )(*state)


def pass_kernel(mu_ref, disp_ref, out_mu_ref, out_disp_ref):
    out_mu_ref[...] = mu_ref[...]
    for c in range(3):
        out_disp_ref[c] = disp_ref[c]


def solution(mesh):
    nx = mesh.shape["gx"]
    ny = mesh.shape["gy"]
    placed = (
        P("gx", "gy", None),
        P(None, "gx", "gy", None),
        P("gx", "gy", None),
        P(None, "gx", "gy", None),
        P("gx", "gy"),
    )
    return jax.shard_map(
        functools.partial(body, nx=nx, ny=ny),
        mesh=mesh,
        in_specs=placed,
        out_specs=(P("gx", "gy", None), P(None, "gx", "gy", None)),
        check_vma=False,
    )
```

```python
import functools

import jax
import jax.numpy as jnp
from jax import lax
from jax.experimental import pallas as pl
from jax.experimental.pallas import tpu as pltpu
from jax.sharding import PartitionSpec as P

SWEEPS = 3
RELAX_INNER = 8

RESIDUAL_STIFFNESS = 0.001
TOUGH_OVER_LENGTH = 0.5
TOUGH_TIMES_LENGTH = 0.25
MASS_SHIFT = 0.5
STIFF_SCALE = 0.25
CENTER_VALUE = 1.0
HALF_WIDTH = 0.75
NORMAL_WEIGHT = 1.5
RELAX_STEP = 0.5
NORMAL_FLOOR = 0.05

MESH = pl.DeviceIdType.MESH


def soft_of(d):
    return (1.0 - d) ** 2


def kernel(
    nx, ny,
    bw_ref, dmg_hbm, strain_hbm, sd_hbm, sdisp_hbm,
    out_mu_hbm, out_disp_hbm,
    dfr, dyl, dyh, sfr, syl, syh, faces, upd, invs, send_sem, recv_sem,
    dmg_ref, strain_ref, sd_ref, sdisp_ref, load_sem, out_mu_ref, out_disp_ref, out_sem,
):
    X, Y, Z = dmg_ref.shape
    bx = lax.axis_index("gx")
    by = lax.axis_index("gy")
    has = (bx < nx - 1, bx > 0, by < ny - 1, by > 0)
    peers = ((bx + 1, by), (bx - 1, by), (bx, by + 1), (bx, by - 1))

    @pl.when(bx == 0)
    def _():
        dfr[:, 0] = jnp.zeros((2, Y, Z), jnp.float32)
        sfr[:, :, 0] = jnp.zeros((SWEEPS, 4, Y, Z), jnp.float32)

    @pl.when(bx == nx - 1)
    def _():
        dfr[:, X + 1] = jnp.zeros((2, Y, Z), jnp.float32)
        sfr[:, :, X + 1] = jnp.zeros((SWEEPS, 4, Y, Z), jnp.float32)

    @pl.when(by == 0)
    def _():
        dyl[...] = jnp.zeros(dyl.shape, jnp.float32)
        syl[...] = jnp.zeros(syl.shape, jnp.float32)

    @pl.when(by == ny - 1)
    def _():
        dyh[...] = jnp.zeros(dyh.shape, jnp.float32)
        syh[...] = jnp.zeros(syh.shape, jnp.float32)

    barrier = pltpu.get_barrier_semaphore()
    count = jnp.int32(0)
    for d in range(4):
        @pl.when(has[d])
        def _():
            pl.semaphore_signal(barrier, inc=1, device_id=peers[d], device_id_type=MESH)
        count = count + has[d].astype(jnp.int32)
    loads = [
        pltpu.make_async_copy(src, dst, load_sem.at[k])
        for k, (src, dst) in enumerate(((dmg_hbm, dmg_ref), (strain_hbm, strain_ref),
                                        (sd_hbm, sd_ref), (sdisp_hbm, sdisp_ref)))
    ]
    for copy in loads:
        copy.start()
    for copy in loads:
        copy.wait()
    pl.semaphore_wait(barrier, count)

    def exchange(slot, routes):
        copies = []
        for d in range(4):
            src, dst = routes[d]
            copies.append(
                pltpu.make_async_remote_copy(
                    src_ref=src, dst_ref=dst,
                    send_sem=send_sem.at[slot, d], recv_sem=recv_sem.at[slot, d],
                    device_id=peers[d], device_id_type=MESH,
                )
            )
        for d in range(4):
            @pl.when(has[d])
            def _():
                copies[d].start()
        return copies

    def arrive(copies, dirs):
        opposite = (1, 0, 3, 2)
        for d in dirs:
            @pl.when(has[opposite[d]])
            def _():
                copies[d].wait_recv()

    def sent(copies):
        for d in range(4):
            @pl.when(has[d])
            def _():
                copies[d].wait_send()

    c_dmg = exchange(0, (
        (dmg_ref.at[X - 1:X], dfr.at[0, 0:1]),
        (dmg_ref.at[0:1], dfr.at[0, X + 1:X + 2]),
        (dmg_ref.at[:, Y - 1:Y], dyl.at[0]),
        (dmg_ref.at[:, 0:1], dyh.at[0]),
    ))
    c_str = exchange(1, (
        (strain_ref.at[0, X - 1:X], dfr.at[1, 0:1]),
        (strain_ref.at[0, 0:1], dfr.at[1, X + 1:X + 2]),
        (strain_ref.at[1, :, Y - 1:Y], dyl.at[1]),
        (strain_ref.at[1, :, 0:1], dyh.at[1]),
    ))
    dfr[0, 1:X + 1] = dmg_ref[...]
    dfr[1, 1:X + 1] = strain_ref[0]
    arrive(c_dmg, (2, 3))
    arrive(c_str, (2, 3))
    pending = [c_dmg, c_str]

    rows = lax.broadcasted_iota(jnp.int32, (Y, Z), 0)
    lanes = lax.broadcasted_iota(jnp.int32, (Y, Z), 1)

    def sides(center, nxp, nxm, lo, hi):
        yp = jnp.where(rows == Y - 1, hi, pltpu.roll(center, Y - 1, 0))
        ym = jnp.where(rows == 0, lo, pltpu.roll(center, 1, 0))
        zp = jnp.where(lanes == Z - 1, 0.0, pltpu.roll(center, Z - 1, 1))
        zm = jnp.where(lanes == 0, 0.0, pltpu.roll(center, 1, 1))
        return [nxp, nxm, yp, ym, zp, zm]

    def damage_sides(i):
        d = dfr[0, i + 1]
        return d, sides(d, dfr[0, i + 2], dfr[0, i], dyl[0, i], dyh[0, i])

    def prep(i, carry):
        d, ds = damage_sides(i)
        soft_center = soft_of(d) + RESIDUAL_STIFFNESS
        fs = [0.5 * (soft_center + soft_of(s) + RESIDUAL_STIFFNESS) for s in ds]
        total = fs[0]
        for k in range(6):
            faces[k, i] = fs[k]
            if k:
                total = total + fs[k]
        sx = strain_ref[0, i]
        sy = strain_ref[1, i]
        sz = strain_ref[2, i]
        energy = 0.5 * (sx * sx + sy * sy + sz * sz)
        inv_mu = 1.0 / (TOUGH_OVER_LENGTH + 2.0 * energy + 6.0 * TOUGH_TIMES_LENGTH)
        inv_lam = 1.0 / (MASS_SHIFT + STIFF_SCALE * total)
        invs[0, i] = inv_mu
        invs[1, i] = inv_lam
        invs[2, i] = TOUGH_OVER_LENGTH + 2.0 * energy
        mu0 = inv_mu * sd_ref[i] / CENTER_VALUE
        upd[0, i] = mu0
        sfr[0, 0, i + 1] = mu0
        for c in range(3):
            lam0 = inv_lam * sdisp_ref[c, i] / CENTER_VALUE
            upd[1 + c, i] = lam0
            sfr[0, 1 + c, i + 1] = lam0
        return carry

    lax.fori_loop(1, X - 1, prep, 0)
    arrive(c_dmg, (0, 1))
    arrive(c_str, (0, 1))
    for i in (0, X - 1):
        prep(i, 0)

    def state_routes(r):
        return (
            (sfr.at[r, :, X:X + 1], sfr.at[r, :, 0:1]),
            (sfr.at[r, :, 1:2], sfr.at[r, :, X + 1:X + 2]),
            (sfr.at[r, :, 1:X + 1, Y - 1:Y], syl.at[r]),
            (sfr.at[r, :, 1:X + 1, 0:1], syh.at[r]),
        )

    ratio = CENTER_VALUE / HALF_WIDTH
    rho = 1.0 / ratio
    for sweep in range(SWEEPS):
        r = sweep
        copies = exchange(2 + r, state_routes(r))
        pending.append(copies)
        arrive(copies, (2, 3))
        rho_next = 1.0 / (2.0 * ratio - rho)
        keep = rho_next * rho
        gain = 2.0 * rho_next / HALF_WIDTH
        rho = rho_next
        last = sweep == SWEEPS - 1

        def step(i, carry, r=r, keep=keep, gain=gain, last=last):
            mu = sfr[r, 0, i + 1]
            mus = sides(mu, sfr[r, 0, i + 2], sfr[r, 0, i], syl[r, 0, i], syh[r, 0, i])
            energy_diag = invs[2, i]
            damage_part = energy_diag * mu + TOUGH_TIMES_LENGTH * sum(mu - s for s in mus)
            fs = [faces[k, i] for k in range(6)]
            wxm = 2.0 * (dfr[0, i] - 1.0) * dfr[1, i] * mus[1]
            wxp = 2.0 * (dfr[0, i + 2] - 1.0) * dfr[1, i + 2] * mus[0]
            d = dfr[0, i + 1]
            wy = 2.0 * (d - 1.0) * strain_ref[1, i] * mu
            wy_lo = 2.0 * (dyl[0, i] - 1.0) * dyl[1, i] * syl[r, 0, i]
            wy_hi = 2.0 * (dyh[0, i] - 1.0) * dyh[1, i] * syh[r, 0, i]
            wy_p = jnp.where(rows == Y - 1, wy_hi, pltpu.roll(wy, Y - 1, 0))
            wy_m = jnp.where(rows == 0, wy_lo, pltpu.roll(wy, 1, 0))
            wz = 2.0 * (d - 1.0) * strain_ref[2, i] * mu
            wz_p = jnp.where(lanes == Z - 1, 0.0, pltpu.roll(wz, Z - 1, 1))
            wz_m = jnp.where(lanes == 0, 0.0, pltpu.roll(wz, 1, 1))
            transfer = (
                0.5 * (wxm - wxp),
                0.5 * (wy_m - wy_p),
                0.5 * (wz_m - wz_p),
            )
            inv_mu = invs[0, i]
            inv_lam = invs[1, i]
            residual_mu = sd_ref[i] - damage_part
            new_upd = keep * upd[0, i] + gain * inv_mu * residual_mu
            new_mu = mu + new_upd
            upd[0, i] = new_upd
            lams = []
            for c in range(3):
                lam = sfr[r, 1 + c, i + 1]
                ls = sides(lam, sfr[r, 1 + c, i + 2], sfr[r, 1 + c, i],
                           syl[r, 1 + c, i], syh[r, 1 + c, i])
                disp = MASS_SHIFT * lam + STIFF_SCALE * sum(
                    fs[k] * (lam - ls[k]) for k in range(6))
                residual = sdisp_ref[c, i] - (disp + transfer[c])
                nu = keep * upd[1 + c, i] + gain * inv_lam * residual
                upd[1 + c, i] = nu
                lams.append(lam + nu)
            if not last:
                sfr[r + 1, 0, i + 1] = new_mu
                for c in range(3):
                    sfr[r + 1, 1 + c, i + 1] = lams[c]
            else:
                out_mu_ref[i] = new_mu
                _, ds = damage_sides(i)
                grad = [0.5 * (ds[0] - ds[1]), 0.5 * (ds[2] - ds[3]), 0.5 * (ds[4] - ds[5])]
                length = jnp.sqrt(jnp.maximum(
                    grad[0] * grad[0] + grad[1] * grad[1] + grad[2] * grad[2], NORMAL_FLOOR))
                normal = [g / length for g in grad]
                size = normal[0] * normal[0] + normal[1] * normal[1] + normal[2] * normal[2]
                along = normal[0] * lams[0] + normal[1] * lams[1] + normal[2] * lams[2]
                a = RELAX_STEP / RELAX_INNER
                factor = 1.0 - a * (1.0 + NORMAL_WEIGHT * size)
                power = factor
                for _ in range(3):
                    power = power * power
                total = power
                work = bw_ref[0, 0]
                for level in range(2, 5):
                    total = jnp.where(work >= level, total * power, total)
                pull = NORMAL_WEIGHT * (1.0 - total) / (1.0 + NORMAL_WEIGHT * size)
                for c in range(3):
                    out_disp_ref[c, i] = lams[c] - (pull * along) * normal[c]
            return carry

        lax.fori_loop(1, X - 1, step, 0)
        if last:
            outs = [
                pltpu.make_async_copy(out_mu_ref.at[1:X - 1], out_mu_hbm.at[1:X - 1], out_sem.at[0]),
                pltpu.make_async_copy(out_disp_ref.at[:, 1:X - 1], out_disp_hbm.at[:, 1:X - 1], out_sem.at[1]),
            ]
            for copy in outs:
                copy.start()
        arrive(copies, (0, 1))
        for i in (0, X - 1):
            step(i, 0)
        if last:
            for k, i in enumerate((0, X - 1)):
                outs.append(pltpu.make_async_copy(
                    out_mu_ref.at[i:i + 1], out_mu_hbm.at[i:i + 1], out_sem.at[2 + 2 * k]))
                outs.append(pltpu.make_async_copy(
                    out_disp_ref.at[:, i:i + 1], out_disp_hbm.at[:, i:i + 1], out_sem.at[3 + 2 * k]))
                outs[-2].start()
                outs[-1].start()
            for copy in outs:
                copy.wait()

    for copies in pending:
        sent(copies)


def body(damage, strain, seed_damage, seed_disp, brick_work, nx, ny):
    X, Y, Z = damage.shape
    f32 = jnp.float32
    vmem = pl.BlockSpec(memory_space=pltpu.VMEM)
    state = pl.pallas_call(
        functools.partial(kernel, nx, ny),
        out_shape=(
            jax.ShapeDtypeStruct((X, Y, Z), f32),
            jax.ShapeDtypeStruct((3, X, Y, Z), f32),
        ),
        in_specs=[pl.BlockSpec(memory_space=pltpu.SMEM)] + [pl.BlockSpec(memory_space=pl.ANY)] * 4,
        out_specs=(pl.BlockSpec(memory_space=pl.ANY),) * 2,
        scratch_shapes=[
            pltpu.VMEM((2, X + 2, Y, Z), f32),
            pltpu.VMEM((2, X, 1, Z), f32),
            pltpu.VMEM((2, X, 1, Z), f32),
            pltpu.VMEM((SWEEPS, 4, X + 2, Y, Z), f32),
            pltpu.VMEM((SWEEPS, 4, X, 1, Z), f32),
            pltpu.VMEM((SWEEPS, 4, X, 1, Z), f32),
            pltpu.VMEM((6, X, Y, Z), f32),
            pltpu.VMEM((4, X, Y, Z), f32),
            pltpu.VMEM((3, X, Y, Z), f32),
            pltpu.SemaphoreType.DMA((2 + SWEEPS, 4)),
            pltpu.SemaphoreType.DMA((2 + SWEEPS, 4)),
            pltpu.VMEM((X, Y, Z), f32),
            pltpu.VMEM((3, X, Y, Z), f32),
            pltpu.VMEM((X, Y, Z), f32),
            pltpu.VMEM((3, X, Y, Z), f32),
            pltpu.SemaphoreType.DMA((4,)),
            pltpu.VMEM((X, Y, Z), f32),
            pltpu.VMEM((3, X, Y, Z), f32),
            pltpu.SemaphoreType.DMA((6,)),
        ],
        compiler_params=pltpu.CompilerParams(
            collective_id=0, has_side_effects=True, vmem_limit_bytes=60 * 1024 * 1024
        ),
    )(brick_work, damage, strain, seed_damage, seed_disp)
    return pl.pallas_call(
        pass_kernel,
        out_shape=(
            jax.ShapeDtypeStruct((X, Y, Z), f32),
            jax.ShapeDtypeStruct((3, X, Y, Z), f32),
        ),
        in_specs=[vmem, vmem],
        out_specs=(vmem, vmem),
    )(*state)


def pass_kernel(mu_ref, disp_ref, out_mu_ref, out_disp_ref):
    out_mu_ref[...] = mu_ref[...]
    for c in range(3):
        out_disp_ref[c] = disp_ref[c]


def solution(mesh):
    nx = mesh.shape["gx"]
    ny = mesh.shape["gy"]
    placed = (
        P("gx", "gy", None),
        P(None, "gx", "gy", None),
        P("gx", "gy", None),
        P(None, "gx", "gy", None),
        P("gx", "gy"),
    )
    return jax.shard_map(
        functools.partial(body, nx=nx, ny=ny),
        mesh=mesh,
        in_specs=placed,
        out_specs=(P("gx", "gy", None), P(None, "gx", "gy", None)),
        check_vma=False,
    )
```

```python
import functools

import jax
import jax.numpy as jnp
from jax import lax
from jax.experimental import pallas as pl
from jax.experimental.pallas import tpu as pltpu
from jax.sharding import PartitionSpec as P

SWEEPS = 3
RELAX_INNER = 8

RESIDUAL_STIFFNESS = 0.001
TOUGH_OVER_LENGTH = 0.5
TOUGH_TIMES_LENGTH = 0.25
MASS_SHIFT = 0.5
STIFF_SCALE = 0.25
CENTER_VALUE = 1.0
HALF_WIDTH = 0.75
NORMAL_WEIGHT = 1.5
RELAX_STEP = 0.5
NORMAL_FLOOR = 0.05

MESH = pl.DeviceIdType.MESH


def soft_of(d):
    return (1.0 - d) ** 2


def kernel(
    nx, ny,
    bw_ref, dmg_hbm, strain_hbm, sd_hbm, sdisp_hbm,
    out_mu_ref, out_disp_ref,
    dfr, dyl, dyh, sfr, syl, syh, faces, upd, invs, send_sem, recv_sem,
    dmg_ref, strain_ref, sd_ref, sdisp_ref, load_sem,
):
    X, Y, Z = dmg_ref.shape
    bx = lax.axis_index("gx")
    by = lax.axis_index("gy")
    has = (bx < nx - 1, bx > 0, by < ny - 1, by > 0)
    peers = ((bx + 1, by), (bx - 1, by), (bx, by + 1), (bx, by - 1))

    @pl.when(bx == 0)
    def _():
        dfr[:, 0] = jnp.zeros((2, Y, Z), jnp.float32)
        sfr[:, :, 0] = jnp.zeros((SWEEPS, 4, Y, Z), jnp.float32)

    @pl.when(bx == nx - 1)
    def _():
        dfr[:, X + 1] = jnp.zeros((2, Y, Z), jnp.float32)
        sfr[:, :, X + 1] = jnp.zeros((SWEEPS, 4, Y, Z), jnp.float32)

    @pl.when(by == 0)
    def _():
        dyl[...] = jnp.zeros(dyl.shape, jnp.float32)
        syl[...] = jnp.zeros(syl.shape, jnp.float32)

    @pl.when(by == ny - 1)
    def _():
        dyh[...] = jnp.zeros(dyh.shape, jnp.float32)
        syh[...] = jnp.zeros(syh.shape, jnp.float32)

    barrier = pltpu.get_barrier_semaphore()
    count = jnp.int32(0)
    for d in range(4):
        @pl.when(has[d])
        def _():
            pl.semaphore_signal(barrier, inc=1, device_id=peers[d], device_id_type=MESH)
        count = count + has[d].astype(jnp.int32)
    loads = [
        pltpu.make_async_copy(src, dst, load_sem.at[k])
        for k, (src, dst) in enumerate(((dmg_hbm, dmg_ref), (strain_hbm, strain_ref),
                                        (sd_hbm, sd_ref), (sdisp_hbm, sdisp_ref)))
    ]
    for copy in loads:
        copy.start()
    for copy in loads:
        copy.wait()
    pl.semaphore_wait(barrier, count)

    def exchange(slot, routes):
        copies = []
        for d in range(4):
            src, dst = routes[d]
            copies.append(
                pltpu.make_async_remote_copy(
                    src_ref=src, dst_ref=dst,
                    send_sem=send_sem.at[slot, d], recv_sem=recv_sem.at[slot, d],
                    device_id=peers[d], device_id_type=MESH,
                )
            )
        for d in range(4):
            @pl.when(has[d])
            def _():
                copies[d].start()
        return copies

    def arrive(copies, dirs):
        opposite = (1, 0, 3, 2)
        for d in dirs:
            @pl.when(has[opposite[d]])
            def _():
                copies[d].wait_recv()

    def sent(copies):
        for d in range(4):
            @pl.when(has[d])
            def _():
                copies[d].wait_send()

    c_dmg = exchange(0, (
        (dmg_ref.at[X - 1:X], dfr.at[0, 0:1]),
        (dmg_ref.at[0:1], dfr.at[0, X + 1:X + 2]),
        (dmg_ref.at[:, Y - 1:Y], dyl.at[0]),
        (dmg_ref.at[:, 0:1], dyh.at[0]),
    ))
    c_str = exchange(1, (
        (strain_ref.at[0, X - 1:X], dfr.at[1, 0:1]),
        (strain_ref.at[0, 0:1], dfr.at[1, X + 1:X + 2]),
        (strain_ref.at[1, :, Y - 1:Y], dyl.at[1]),
        (strain_ref.at[1, :, 0:1], dyh.at[1]),
    ))
    dfr[0, 1:X + 1] = dmg_ref[...]
    dfr[1, 1:X + 1] = strain_ref[0]
    arrive(c_dmg, (2, 3))
    arrive(c_str, (2, 3))
    pending = [c_dmg, c_str]

    rows = lax.broadcasted_iota(jnp.int32, (Y, Z), 0)
    lanes = lax.broadcasted_iota(jnp.int32, (Y, Z), 1)

    def sides(center, nxp, nxm, lo, hi):
        yp = jnp.where(rows == Y - 1, hi, pltpu.roll(center, Y - 1, 0))
        ym = jnp.where(rows == 0, lo, pltpu.roll(center, 1, 0))
        zp = jnp.where(lanes == Z - 1, 0.0, pltpu.roll(center, Z - 1, 1))
        zm = jnp.where(lanes == 0, 0.0, pltpu.roll(center, 1, 1))
        return [nxp, nxm, yp, ym, zp, zm]

    def damage_sides(i):
        d = dfr[0, i + 1]
        return d, sides(d, dfr[0, i + 2], dfr[0, i], dyl[0, i], dyh[0, i])

    def prep(i, carry):
        d, ds = damage_sides(i)
        soft_center = soft_of(d) + RESIDUAL_STIFFNESS
        fs = [0.5 * (soft_center + soft_of(s) + RESIDUAL_STIFFNESS) for s in ds]
        total = fs[0]
        for k in range(6):
            faces[k, i] = fs[k]
            if k:
                total = total + fs[k]
        sx = strain_ref[0, i]
        sy = strain_ref[1, i]
        sz = strain_ref[2, i]
        energy = 0.5 * (sx * sx + sy * sy + sz * sz)
        inv_mu = 1.0 / (TOUGH_OVER_LENGTH + 2.0 * energy + 6.0 * TOUGH_TIMES_LENGTH)
        inv_lam = 1.0 / (MASS_SHIFT + STIFF_SCALE * total)
        invs[0, i] = inv_mu
        invs[1, i] = inv_lam
        invs[2, i] = TOUGH_OVER_LENGTH + 2.0 * energy
        mu0 = inv_mu * sd_ref[i] / CENTER_VALUE
        upd[0, i] = mu0
        sfr[0, 0, i + 1] = mu0
        for c in range(3):
            lam0 = inv_lam * sdisp_ref[c, i] / CENTER_VALUE
            upd[1 + c, i] = lam0
            sfr[0, 1 + c, i + 1] = lam0
        return carry

    lax.fori_loop(1, X - 1, prep, 0)
    arrive(c_dmg, (0, 1))
    arrive(c_str, (0, 1))
    for i in (0, X - 1):
        prep(i, 0)

    def state_routes(r):
        return (
            (sfr.at[r, :, X:X + 1], sfr.at[r, :, 0:1]),
            (sfr.at[r, :, 1:2], sfr.at[r, :, X + 1:X + 2]),
            (sfr.at[r, :, 1:X + 1, Y - 1:Y], syl.at[r]),
            (sfr.at[r, :, 1:X + 1, 0:1], syh.at[r]),
        )

    ratio = CENTER_VALUE / HALF_WIDTH
    rho = 1.0 / ratio
    for sweep in range(SWEEPS):
        r = sweep
        copies = exchange(2 + r, state_routes(r))
        pending.append(copies)
        arrive(copies, (2, 3))
        rho_next = 1.0 / (2.0 * ratio - rho)
        keep = rho_next * rho
        gain = 2.0 * rho_next / HALF_WIDTH
        rho = rho_next
        last = sweep == SWEEPS - 1

        def step(i, carry, r=r, keep=keep, gain=gain, last=last):
            mu = sfr[r, 0, i + 1]
            mus = sides(mu, sfr[r, 0, i + 2], sfr[r, 0, i], syl[r, 0, i], syh[r, 0, i])
            energy_diag = invs[2, i]
            damage_part = energy_diag * mu + TOUGH_TIMES_LENGTH * sum(mu - s for s in mus)
            fs = [faces[k, i] for k in range(6)]
            wxm = 2.0 * (dfr[0, i] - 1.0) * dfr[1, i] * mus[1]
            wxp = 2.0 * (dfr[0, i + 2] - 1.0) * dfr[1, i + 2] * mus[0]
            d = dfr[0, i + 1]
            wy = 2.0 * (d - 1.0) * strain_ref[1, i] * mu
            wy_lo = 2.0 * (dyl[0, i] - 1.0) * dyl[1, i] * syl[r, 0, i]
            wy_hi = 2.0 * (dyh[0, i] - 1.0) * dyh[1, i] * syh[r, 0, i]
            wy_p = jnp.where(rows == Y - 1, wy_hi, pltpu.roll(wy, Y - 1, 0))
            wy_m = jnp.where(rows == 0, wy_lo, pltpu.roll(wy, 1, 0))
            wz = 2.0 * (d - 1.0) * strain_ref[2, i] * mu
            wz_p = jnp.where(lanes == Z - 1, 0.0, pltpu.roll(wz, Z - 1, 1))
            wz_m = jnp.where(lanes == 0, 0.0, pltpu.roll(wz, 1, 1))
            transfer = (
                0.5 * (wxm - wxp),
                0.5 * (wy_m - wy_p),
                0.5 * (wz_m - wz_p),
            )
            inv_mu = invs[0, i]
            inv_lam = invs[1, i]
            residual_mu = sd_ref[i] - damage_part
            new_upd = keep * upd[0, i] + gain * inv_mu * residual_mu
            new_mu = mu + new_upd
            upd[0, i] = new_upd
            lams = []
            for c in range(3):
                lam = sfr[r, 1 + c, i + 1]
                ls = sides(lam, sfr[r, 1 + c, i + 2], sfr[r, 1 + c, i],
                           syl[r, 1 + c, i], syh[r, 1 + c, i])
                disp = MASS_SHIFT * lam + STIFF_SCALE * sum(
                    fs[k] * (lam - ls[k]) for k in range(6))
                residual = sdisp_ref[c, i] - (disp + transfer[c])
                nu = keep * upd[1 + c, i] + gain * inv_lam * residual
                upd[1 + c, i] = nu
                lams.append(lam + nu)
            if not last:
                sfr[r + 1, 0, i + 1] = new_mu
                for c in range(3):
                    sfr[r + 1, 1 + c, i + 1] = lams[c]
            else:
                out_mu_ref[i] = new_mu
                _, ds = damage_sides(i)
                grad = [0.5 * (ds[0] - ds[1]), 0.5 * (ds[2] - ds[3]), 0.5 * (ds[4] - ds[5])]
                length = jnp.sqrt(jnp.maximum(
                    grad[0] * grad[0] + grad[1] * grad[1] + grad[2] * grad[2], NORMAL_FLOOR))
                normal = [g / length for g in grad]
                size = normal[0] * normal[0] + normal[1] * normal[1] + normal[2] * normal[2]
                along = normal[0] * lams[0] + normal[1] * lams[1] + normal[2] * lams[2]
                a = RELAX_STEP / RELAX_INNER
                factor = 1.0 - a * (1.0 + NORMAL_WEIGHT * size)
                power = factor
                for _ in range(3):
                    power = power * power
                total = power
                work = bw_ref[0, 0]
                for level in range(2, 5):
                    total = jnp.where(work >= level, total * power, total)
                pull = NORMAL_WEIGHT * (1.0 - total) / (1.0 + NORMAL_WEIGHT * size)
                for c in range(3):
                    out_disp_ref[c, i] = lams[c] - (pull * along) * normal[c]
            return carry

        lax.fori_loop(1, X - 1, step, 0)
        arrive(copies, (0, 1))
        for i in (0, X - 1):
            step(i, 0)

    for copies in pending:
        sent(copies)


def body(damage, strain, seed_damage, seed_disp, brick_work, nx, ny):
    X, Y, Z = damage.shape
    f32 = jnp.float32
    vmem = pl.BlockSpec(memory_space=pltpu.VMEM)
    state = pl.pallas_call(
        functools.partial(kernel, nx, ny),
        out_shape=(
            jax.ShapeDtypeStruct((X, Y, Z), f32),
            jax.ShapeDtypeStruct((3, X, Y, Z), f32),
        ),
        in_specs=[pl.BlockSpec(memory_space=pltpu.SMEM)] + [pl.BlockSpec(memory_space=pl.ANY)] * 4,
        out_specs=(vmem, vmem),
        scratch_shapes=[
            pltpu.VMEM((2, X + 2, Y, Z), f32),
            pltpu.VMEM((2, X, 1, Z), f32),
            pltpu.VMEM((2, X, 1, Z), f32),
            pltpu.VMEM((SWEEPS, 4, X + 2, Y, Z), f32),
            pltpu.VMEM((SWEEPS, 4, X, 1, Z), f32),
            pltpu.VMEM((SWEEPS, 4, X, 1, Z), f32),
            pltpu.VMEM((6, X, Y, Z), f32),
            pltpu.VMEM((4, X, Y, Z), f32),
            pltpu.VMEM((3, X, Y, Z), f32),
            pltpu.SemaphoreType.DMA((2 + SWEEPS, 4)),
            pltpu.SemaphoreType.DMA((2 + SWEEPS, 4)),
            pltpu.VMEM((X, Y, Z), f32),
            pltpu.VMEM((3, X, Y, Z), f32),
            pltpu.VMEM((X, Y, Z), f32),
            pltpu.VMEM((3, X, Y, Z), f32),
            pltpu.SemaphoreType.DMA((4,)),
        ],
        compiler_params=pltpu.CompilerParams(
            collective_id=0, has_side_effects=True, vmem_limit_bytes=60 * 1024 * 1024
        ),
    )(brick_work, damage, strain, seed_damage, seed_disp)
    return pl.pallas_call(
        pass_kernel,
        out_shape=(
            jax.ShapeDtypeStruct((X, Y, Z), f32),
            jax.ShapeDtypeStruct((3, X, Y, Z), f32),
        ),
        in_specs=[pl.BlockSpec(memory_space=pl.ANY)] * 2,
        out_specs=(vmem, vmem),
        scratch_shapes=[pltpu.SemaphoreType.DMA((2,))],
    )(*state)


def pass_kernel(mu_ref, disp_ref, out_mu_ref, out_disp_ref, sems):
    copies = [
        pltpu.make_async_copy(mu_ref, out_mu_ref, sems.at[0]),
        pltpu.make_async_copy(disp_ref, out_disp_ref, sems.at[1]),
    ]
    for copy in copies:
        copy.start()
    for copy in copies:
        copy.wait()


def solution(mesh):
    nx = mesh.shape["gx"]
    ny = mesh.shape["gy"]
    placed = (
        P("gx", "gy", None),
        P(None, "gx", "gy", None),
        P("gx", "gy", None),
        P(None, "gx", "gy", None),
        P("gx", "gy"),
    )
    return jax.shard_map(
        functools.partial(body, nx=nx, ny=ny),
        mesh=mesh,
        in_specs=placed,
        out_specs=(P("gx", "gy", None), P(None, "gx", "gy", None)),
        check_vma=False,
    )
```

```python
import functools

import jax
import jax.numpy as jnp
from jax import lax
from jax.experimental import pallas as pl
from jax.experimental.pallas import tpu as pltpu
from jax.sharding import PartitionSpec as P

SWEEPS = 3
RELAX_INNER = 8

RESIDUAL_STIFFNESS = 0.001
TOUGH_OVER_LENGTH = 0.5
TOUGH_TIMES_LENGTH = 0.25
MASS_SHIFT = 0.5
STIFF_SCALE = 0.25
CENTER_VALUE = 1.0
HALF_WIDTH = 0.75
NORMAL_WEIGHT = 1.5
RELAX_STEP = 0.5
NORMAL_FLOOR = 0.05

MESH = pl.DeviceIdType.MESH


def soft_of(d):
    return (1.0 - d) ** 2


def kernel(
    nx, ny,
    bw_ref, dmg_hbm, strain_hbm, sd_hbm, sdisp_hbm,
    out_mu_ref, out_disp_ref,
    dfr, dyl, dyh, sfr, syl, syh, faces, upd, invs, send_sem, recv_sem,
    dmg_ref, strain_ref, sd_ref, sdisp_ref, load_sem,
):
    X, Y, Z = dmg_ref.shape
    bx = lax.axis_index("gx")
    by = lax.axis_index("gy")
    has = (bx < nx - 1, bx > 0, by < ny - 1, by > 0)
    peers = ((bx + 1, by), (bx - 1, by), (bx, by + 1), (bx, by - 1))

    @pl.when(bx == 0)
    def _():
        dfr[:, 0] = jnp.zeros((2, Y, Z), jnp.float32)
        sfr[:, :, 0] = jnp.zeros((SWEEPS, 4, Y, Z), jnp.float32)

    @pl.when(bx == nx - 1)
    def _():
        dfr[:, X + 1] = jnp.zeros((2, Y, Z), jnp.float32)
        sfr[:, :, X + 1] = jnp.zeros((SWEEPS, 4, Y, Z), jnp.float32)

    @pl.when(by == 0)
    def _():
        dyl[...] = jnp.zeros(dyl.shape, jnp.float32)
        syl[...] = jnp.zeros(syl.shape, jnp.float32)

    @pl.when(by == ny - 1)
    def _():
        dyh[...] = jnp.zeros(dyh.shape, jnp.float32)
        syh[...] = jnp.zeros(syh.shape, jnp.float32)

    barrier = pltpu.get_barrier_semaphore()
    count = jnp.int32(0)
    for d in range(4):
        @pl.when(has[d])
        def _():
            pl.semaphore_signal(barrier, inc=1, device_id=peers[d], device_id_type=MESH)
        count = count + has[d].astype(jnp.int32)
    loads = [
        pltpu.make_async_copy(src, dst, load_sem.at[k])
        for k, (src, dst) in enumerate(((dmg_hbm, dmg_ref), (strain_hbm, strain_ref),
                                        (sd_hbm, sd_ref), (sdisp_hbm, sdisp_ref)))
    ]
    for copy in loads:
        copy.start()
    for copy in loads:
        copy.wait()
    dfr[0, 1:X + 1] = dmg_ref[...]
    dfr[1, 1:X + 1] = strain_ref[0]

    def local(i, carry):
        sx = strain_ref[0, i]
        sy = strain_ref[1, i]
        sz = strain_ref[2, i]
        energy = 0.5 * (sx * sx + sy * sy + sz * sz)
        inv_mu = 1.0 / (TOUGH_OVER_LENGTH + 2.0 * energy + 6.0 * TOUGH_TIMES_LENGTH)
        invs[0, i] = inv_mu
        invs[2, i] = TOUGH_OVER_LENGTH + 2.0 * energy
        mu0 = inv_mu * sd_ref[i] / CENTER_VALUE
        upd[0, i] = mu0
        sfr[0, 0, i + 1] = mu0
        return carry

    lax.fori_loop(0, X, local, 0)
    pl.semaphore_wait(barrier, count)

    def exchange(slot, routes):
        copies = []
        for d in range(4):
            src, dst = routes[d]
            copies.append(
                pltpu.make_async_remote_copy(
                    src_ref=src, dst_ref=dst,
                    send_sem=send_sem.at[slot, d], recv_sem=recv_sem.at[slot, d],
                    device_id=peers[d], device_id_type=MESH,
                )
            )
        for d in range(4):
            @pl.when(has[d])
            def _():
                copies[d].start()
        return copies

    def arrive(copies, dirs):
        opposite = (1, 0, 3, 2)
        for d in dirs:
            @pl.when(has[opposite[d]])
            def _():
                copies[d].wait_recv()

    def sent(copies):
        for d in range(4):
            @pl.when(has[d])
            def _():
                copies[d].wait_send()

    c_dmg = exchange(0, (
        (dmg_ref.at[X - 1:X], dfr.at[0, 0:1]),
        (dmg_ref.at[0:1], dfr.at[0, X + 1:X + 2]),
        (dmg_ref.at[:, Y - 1:Y], dyl.at[0]),
        (dmg_ref.at[:, 0:1], dyh.at[0]),
    ))
    c_str = exchange(1, (
        (strain_ref.at[0, X - 1:X], dfr.at[1, 0:1]),
        (strain_ref.at[0, 0:1], dfr.at[1, X + 1:X + 2]),
        (strain_ref.at[1, :, Y - 1:Y], dyl.at[1]),
        (strain_ref.at[1, :, 0:1], dyh.at[1]),
    ))
    arrive(c_dmg, (2, 3))
    arrive(c_str, (2, 3))
    pending = [c_dmg, c_str]

    rows = lax.broadcasted_iota(jnp.int32, (Y, Z), 0)
    lanes = lax.broadcasted_iota(jnp.int32, (Y, Z), 1)

    def sides(center, nxp, nxm, lo, hi):
        yp = jnp.where(rows == Y - 1, hi, pltpu.roll(center, Y - 1, 0))
        ym = jnp.where(rows == 0, lo, pltpu.roll(center, 1, 0))
        zp = jnp.where(lanes == Z - 1, 0.0, pltpu.roll(center, Z - 1, 1))
        zm = jnp.where(lanes == 0, 0.0, pltpu.roll(center, 1, 1))
        return [nxp, nxm, yp, ym, zp, zm]

    def damage_sides(i):
        d = dfr[0, i + 1]
        return d, sides(d, dfr[0, i + 2], dfr[0, i], dyl[0, i], dyh[0, i])

    def prep(i, carry):
        d, ds = damage_sides(i)
        soft_center = soft_of(d) + RESIDUAL_STIFFNESS
        fs = [0.5 * (soft_center + soft_of(s) + RESIDUAL_STIFFNESS) for s in ds]
        total = fs[0]
        for k in range(6):
            faces[k, i] = fs[k]
            if k:
                total = total + fs[k]
        inv_lam = 1.0 / (MASS_SHIFT + STIFF_SCALE * total)
        invs[1, i] = inv_lam
        for c in range(3):
            lam0 = inv_lam * sdisp_ref[c, i] / CENTER_VALUE
            upd[1 + c, i] = lam0
            sfr[0, 1 + c, i + 1] = lam0
        return carry

    lax.fori_loop(1, X - 1, prep, 0)
    arrive(c_dmg, (0, 1))
    arrive(c_str, (0, 1))
    for i in (0, X - 1):
        prep(i, 0)

    def state_routes(r):
        return (
            (sfr.at[r, :, X:X + 1], sfr.at[r, :, 0:1]),
            (sfr.at[r, :, 1:2], sfr.at[r, :, X + 1:X + 2]),
            (sfr.at[r, :, 1:X + 1, Y - 1:Y], syl.at[r]),
            (sfr.at[r, :, 1:X + 1, 0:1], syh.at[r]),
        )

    ratio = CENTER_VALUE / HALF_WIDTH
    rho = 1.0 / ratio
    for sweep in range(SWEEPS):
        r = sweep
        copies = exchange(2 + r, state_routes(r))
        pending.append(copies)
        arrive(copies, (2, 3))
        rho_next = 1.0 / (2.0 * ratio - rho)
        keep = rho_next * rho
        gain = 2.0 * rho_next / HALF_WIDTH
        rho = rho_next
        last = sweep == SWEEPS - 1

        def step(i, carry, r=r, keep=keep, gain=gain, last=last):
            mu = sfr[r, 0, i + 1]
            mus = sides(mu, sfr[r, 0, i + 2], sfr[r, 0, i], syl[r, 0, i], syh[r, 0, i])
            energy_diag = invs[2, i]
            damage_part = energy_diag * mu + TOUGH_TIMES_LENGTH * sum(mu - s for s in mus)
            fs = [faces[k, i] for k in range(6)]
            wxm = 2.0 * (dfr[0, i] - 1.0) * dfr[1, i] * mus[1]
            wxp = 2.0 * (dfr[0, i + 2] - 1.0) * dfr[1, i + 2] * mus[0]
            d = dfr[0, i + 1]
            wy = 2.0 * (d - 1.0) * strain_ref[1, i] * mu
            wy_lo = 2.0 * (dyl[0, i] - 1.0) * dyl[1, i] * syl[r, 0, i]
            wy_hi = 2.0 * (dyh[0, i] - 1.0) * dyh[1, i] * syh[r, 0, i]
            wy_p = jnp.where(rows == Y - 1, wy_hi, pltpu.roll(wy, Y - 1, 0))
            wy_m = jnp.where(rows == 0, wy_lo, pltpu.roll(wy, 1, 0))
            wz = 2.0 * (d - 1.0) * strain_ref[2, i] * mu
            wz_p = jnp.where(lanes == Z - 1, 0.0, pltpu.roll(wz, Z - 1, 1))
            wz_m = jnp.where(lanes == 0, 0.0, pltpu.roll(wz, 1, 1))
            transfer = (
                0.5 * (wxm - wxp),
                0.5 * (wy_m - wy_p),
                0.5 * (wz_m - wz_p),
            )
            inv_mu = invs[0, i]
            inv_lam = invs[1, i]
            residual_mu = sd_ref[i] - damage_part
            new_upd = keep * upd[0, i] + gain * inv_mu * residual_mu
            new_mu = mu + new_upd
            upd[0, i] = new_upd
            lams = []
            for c in range(3):
                lam = sfr[r, 1 + c, i + 1]
                ls = sides(lam, sfr[r, 1 + c, i + 2], sfr[r, 1 + c, i],
                           syl[r, 1 + c, i], syh[r, 1 + c, i])
                disp = MASS_SHIFT * lam + STIFF_SCALE * sum(
                    fs[k] * (lam - ls[k]) for k in range(6))
                residual = sdisp_ref[c, i] - (disp + transfer[c])
                nu = keep * upd[1 + c, i] + gain * inv_lam * residual
                upd[1 + c, i] = nu
                lams.append(lam + nu)
            if not last:
                sfr[r + 1, 0, i + 1] = new_mu
                for c in range(3):
                    sfr[r + 1, 1 + c, i + 1] = lams[c]
            else:
                out_mu_ref[i] = new_mu
                _, ds = damage_sides(i)
                grad = [0.5 * (ds[0] - ds[1]), 0.5 * (ds[2] - ds[3]), 0.5 * (ds[4] - ds[5])]
                length = jnp.sqrt(jnp.maximum(
                    grad[0] * grad[0] + grad[1] * grad[1] + grad[2] * grad[2], NORMAL_FLOOR))
                normal = [g / length for g in grad]
                size = normal[0] * normal[0] + normal[1] * normal[1] + normal[2] * normal[2]
                along = normal[0] * lams[0] + normal[1] * lams[1] + normal[2] * lams[2]
                a = RELAX_STEP / RELAX_INNER
                factor = 1.0 - a * (1.0 + NORMAL_WEIGHT * size)
                power = factor
                for _ in range(3):
                    power = power * power
                total = power
                work = bw_ref[0, 0]
                for level in range(2, 5):
                    total = jnp.where(work >= level, total * power, total)
                pull = NORMAL_WEIGHT * (1.0 - total) / (1.0 + NORMAL_WEIGHT * size)
                for c in range(3):
                    out_disp_ref[c, i] = lams[c] - (pull * along) * normal[c]
            return carry

        lax.fori_loop(1, X - 1, step, 0)
        arrive(copies, (0, 1))
        for i in (0, X - 1):
            step(i, 0)

    for copies in pending:
        sent(copies)


def body(damage, strain, seed_damage, seed_disp, brick_work, nx, ny):
    X, Y, Z = damage.shape
    f32 = jnp.float32
    vmem = pl.BlockSpec(memory_space=pltpu.VMEM)
    state = pl.pallas_call(
        functools.partial(kernel, nx, ny),
        out_shape=(
            jax.ShapeDtypeStruct((X, Y, Z), f32),
            jax.ShapeDtypeStruct((3, X, Y, Z), f32),
        ),
        in_specs=[pl.BlockSpec(memory_space=pltpu.SMEM)] + [pl.BlockSpec(memory_space=pl.ANY)] * 4,
        out_specs=(vmem, vmem),
        scratch_shapes=[
            pltpu.VMEM((2, X + 2, Y, Z), f32),
            pltpu.VMEM((2, X, 1, Z), f32),
            pltpu.VMEM((2, X, 1, Z), f32),
            pltpu.VMEM((SWEEPS, 4, X + 2, Y, Z), f32),
            pltpu.VMEM((SWEEPS, 4, X, 1, Z), f32),
            pltpu.VMEM((SWEEPS, 4, X, 1, Z), f32),
            pltpu.VMEM((6, X, Y, Z), f32),
            pltpu.VMEM((4, X, Y, Z), f32),
            pltpu.VMEM((3, X, Y, Z), f32),
            pltpu.SemaphoreType.DMA((2 + SWEEPS, 4)),
            pltpu.SemaphoreType.DMA((2 + SWEEPS, 4)),
            pltpu.VMEM((X, Y, Z), f32),
            pltpu.VMEM((3, X, Y, Z), f32),
            pltpu.VMEM((X, Y, Z), f32),
            pltpu.VMEM((3, X, Y, Z), f32),
            pltpu.SemaphoreType.DMA((4,)),
        ],
        compiler_params=pltpu.CompilerParams(
            collective_id=0, has_side_effects=True, vmem_limit_bytes=60 * 1024 * 1024
        ),
    )(brick_work, damage, strain, seed_damage, seed_disp)
    return pl.pallas_call(
        pass_kernel,
        out_shape=(
            jax.ShapeDtypeStruct((X, Y, Z), f32),
            jax.ShapeDtypeStruct((3, X, Y, Z), f32),
        ),
        in_specs=[pl.BlockSpec(memory_space=pl.ANY)] * 2,
        out_specs=(vmem, vmem),
        scratch_shapes=[pltpu.SemaphoreType.DMA((2,))],
    )(*state)


def pass_kernel(mu_ref, disp_ref, out_mu_ref, out_disp_ref, sems):
    copies = [
        pltpu.make_async_copy(mu_ref, out_mu_ref, sems.at[0]),
        pltpu.make_async_copy(disp_ref, out_disp_ref, sems.at[1]),
    ]
    for copy in copies:
        copy.start()
    for copy in copies:
        copy.wait()


def solution(mesh):
    nx = mesh.shape["gx"]
    ny = mesh.shape["gy"]
    placed = (
        P("gx", "gy", None),
        P(None, "gx", "gy", None),
        P("gx", "gy", None),
        P(None, "gx", "gy", None),
        P("gx", "gy"),
    )
    return jax.shard_map(
        functools.partial(body, nx=nx, ny=ny),
        mesh=mesh,
        in_specs=placed,
        out_specs=(P("gx", "gy", None), P(None, "gx", "gy", None)),
        check_vma=False,
    )
```

```python
import functools

import jax
import jax.numpy as jnp
from jax import lax
from jax.experimental import pallas as pl
from jax.experimental.pallas import tpu as pltpu
from jax.sharding import PartitionSpec as P

SWEEPS = 3
RELAX_INNER = 8

RESIDUAL_STIFFNESS = 0.001
TOUGH_OVER_LENGTH = 0.5
TOUGH_TIMES_LENGTH = 0.25
MASS_SHIFT = 0.5
STIFF_SCALE = 0.25
CENTER_VALUE = 1.0
HALF_WIDTH = 0.75
NORMAL_WEIGHT = 1.5
RELAX_STEP = 0.5
NORMAL_FLOOR = 0.05

MESH = pl.DeviceIdType.MESH


def soft_of(d):
    return (1.0 - d) ** 2


def kernel(
    nx, ny,
    bw_ref, dmg_hbm, strain_hbm, sd_hbm, sdisp_hbm,
    out_mu_ref, out_disp_ref,
    dfr, dyl, dyh, sfr, syl, syh, faces, upd, invs, send_sem, recv_sem,
    dmg_ref, strain_ref, sd_ref, sdisp_ref, load_sem,
):
    X, Y, Z = dmg_ref.shape
    bx = lax.axis_index("gx")
    by = lax.axis_index("gy")
    has = (bx < nx - 1, bx > 0, by < ny - 1, by > 0)
    peers = ((bx + 1, by), (bx - 1, by), (bx, by + 1), (bx, by - 1))

    @pl.when(bx == 0)
    def _():
        dfr[:, 0] = jnp.zeros((2, Y, Z), jnp.float32)
        sfr[:, :, 0] = jnp.zeros((SWEEPS, 4, Y, Z), jnp.float32)

    @pl.when(bx == nx - 1)
    def _():
        dfr[:, X + 1] = jnp.zeros((2, Y, Z), jnp.float32)
        sfr[:, :, X + 1] = jnp.zeros((SWEEPS, 4, Y, Z), jnp.float32)

    @pl.when(by == 0)
    def _():
        dyl[...] = jnp.zeros(dyl.shape, jnp.float32)
        syl[...] = jnp.zeros(syl.shape, jnp.float32)

    @pl.when(by == ny - 1)
    def _():
        dyh[...] = jnp.zeros(dyh.shape, jnp.float32)
        syh[...] = jnp.zeros(syh.shape, jnp.float32)

    barrier = pltpu.get_barrier_semaphore()
    count = jnp.int32(0)
    for d in range(4):
        @pl.when(has[d])
        def _():
            pl.semaphore_signal(barrier, inc=1, device_id=peers[d], device_id_type=MESH)
        count = count + has[d].astype(jnp.int32)
    loads = [
        pltpu.make_async_copy(src, dst, load_sem.at[k])
        for k, (src, dst) in enumerate(((dmg_hbm, dmg_ref), (strain_hbm, strain_ref),
                                        (sd_hbm, sd_ref), (sdisp_hbm, sdisp_ref)))
    ]
    for copy in loads:
        copy.start()
    for copy in loads:
        copy.wait()
    pl.semaphore_wait(barrier, count)

    def exchange(slot, routes, dirs=range(4)):
        copies = []
        for d in range(4):
            src, dst = routes[d]
            copies.append(
                pltpu.make_async_remote_copy(
                    src_ref=src, dst_ref=dst,
                    send_sem=send_sem.at[slot, d], recv_sem=recv_sem.at[slot, d],
                    device_id=peers[d], device_id_type=MESH,
                )
            )
        start(copies, dirs)
        return copies

    def start(copies, dirs):
        for d in dirs:
            @pl.when(has[d])
            def _():
                copies[d].start()

    def arrive(copies, dirs):
        opposite = (1, 0, 3, 2)
        for d in dirs:
            @pl.when(has[opposite[d]])
            def _():
                copies[d].wait_recv()

    def sent(copies):
        for d in range(4):
            @pl.when(has[d])
            def _():
                copies[d].wait_send()

    c_dmg = exchange(0, (
        (dmg_ref.at[X - 1:X], dfr.at[0, 0:1]),
        (dmg_ref.at[0:1], dfr.at[0, X + 1:X + 2]),
        (dmg_ref.at[:, Y - 1:Y], dyl.at[0]),
        (dmg_ref.at[:, 0:1], dyh.at[0]),
    ), ())
    c_str = exchange(1, (
        (strain_ref.at[0, X - 1:X], dfr.at[1, 0:1]),
        (strain_ref.at[0, 0:1], dfr.at[1, X + 1:X + 2]),
        (strain_ref.at[1, :, Y - 1:Y], dyl.at[1]),
        (strain_ref.at[1, :, 0:1], dyh.at[1]),
    ), ())
    for dirs in ((0, 1), (2, 3)):
        start(c_dmg, dirs)
        start(c_str, dirs)
    dfr[0, 1:X + 1] = dmg_ref[...]
    dfr[1, 1:X + 1] = strain_ref[0]
    arrive(c_dmg, (2, 3))
    arrive(c_str, (2, 3))
    pending = [c_dmg, c_str]

    rows = lax.broadcasted_iota(jnp.int32, (Y, Z), 0)
    lanes = lax.broadcasted_iota(jnp.int32, (Y, Z), 1)

    def sides(center, nxp, nxm, lo, hi):
        yp = jnp.where(rows == Y - 1, hi, pltpu.roll(center, Y - 1, 0))
        ym = jnp.where(rows == 0, lo, pltpu.roll(center, 1, 0))
        zp = jnp.where(lanes == Z - 1, 0.0, pltpu.roll(center, Z - 1, 1))
        zm = jnp.where(lanes == 0, 0.0, pltpu.roll(center, 1, 1))
        return [nxp, nxm, yp, ym, zp, zm]

    def damage_sides(i):
        d = dfr[0, i + 1]
        return d, sides(d, dfr[0, i + 2], dfr[0, i], dyl[0, i], dyh[0, i])

    def prep(i, carry):
        d, ds = damage_sides(i)
        soft_center = soft_of(d) + RESIDUAL_STIFFNESS
        fs = [0.5 * (soft_center + soft_of(s) + RESIDUAL_STIFFNESS) for s in ds]
        total = fs[0]
        for k in range(6):
            faces[k, i] = fs[k]
            if k:
                total = total + fs[k]
        sx = strain_ref[0, i]
        sy = strain_ref[1, i]
        sz = strain_ref[2, i]
        energy = 0.5 * (sx * sx + sy * sy + sz * sz)
        inv_mu = 1.0 / (TOUGH_OVER_LENGTH + 2.0 * energy + 6.0 * TOUGH_TIMES_LENGTH)
        inv_lam = 1.0 / (MASS_SHIFT + STIFF_SCALE * total)
        invs[0, i] = inv_mu
        invs[1, i] = inv_lam
        invs[2, i] = TOUGH_OVER_LENGTH + 2.0 * energy
        mu0 = inv_mu * sd_ref[i] / CENTER_VALUE
        upd[0, i] = mu0
        sfr[0, 0, i + 1] = mu0
        for c in range(3):
            lam0 = inv_lam * sdisp_ref[c, i] / CENTER_VALUE
            upd[1 + c, i] = lam0
            sfr[0, 1 + c, i + 1] = lam0
        return carry

    lax.fori_loop(1, X - 1, prep, 0)
    arrive(c_dmg, (0, 1))
    arrive(c_str, (0, 1))
    for i in (0, X - 1):
        prep(i, 0)

    def state_routes(r):
        return (
            (sfr.at[r, :, X:X + 1], sfr.at[r, :, 0:1]),
            (sfr.at[r, :, 1:2], sfr.at[r, :, X + 1:X + 2]),
            (sfr.at[r, :, 1:X + 1, Y - 1:Y], syl.at[r]),
            (sfr.at[r, :, 1:X + 1, 0:1], syh.at[r]),
        )

    ratio = CENTER_VALUE / HALF_WIDTH
    rho = 1.0 / ratio
    for sweep in range(SWEEPS):
        r = sweep
        copies = exchange(2 + r, state_routes(r))
        pending.append(copies)
        arrive(copies, (2, 3))
        rho_next = 1.0 / (2.0 * ratio - rho)
        keep = rho_next * rho
        gain = 2.0 * rho_next / HALF_WIDTH
        rho = rho_next
        last = sweep == SWEEPS - 1

        def step(i, carry, r=r, keep=keep, gain=gain, last=last):
            mu = sfr[r, 0, i + 1]
            mus = sides(mu, sfr[r, 0, i + 2], sfr[r, 0, i], syl[r, 0, i], syh[r, 0, i])
            energy_diag = invs[2, i]
            damage_part = energy_diag * mu + TOUGH_TIMES_LENGTH * sum(mu - s for s in mus)
            fs = [faces[k, i] for k in range(6)]
            wxm = 2.0 * (dfr[0, i] - 1.0) * dfr[1, i] * mus[1]
            wxp = 2.0 * (dfr[0, i + 2] - 1.0) * dfr[1, i + 2] * mus[0]
            d = dfr[0, i + 1]
            wy = 2.0 * (d - 1.0) * strain_ref[1, i] * mu
            wy_lo = 2.0 * (dyl[0, i] - 1.0) * dyl[1, i] * syl[r, 0, i]
            wy_hi = 2.0 * (dyh[0, i] - 1.0) * dyh[1, i] * syh[r, 0, i]
            wy_p = jnp.where(rows == Y - 1, wy_hi, pltpu.roll(wy, Y - 1, 0))
            wy_m = jnp.where(rows == 0, wy_lo, pltpu.roll(wy, 1, 0))
            wz = 2.0 * (d - 1.0) * strain_ref[2, i] * mu
            wz_p = jnp.where(lanes == Z - 1, 0.0, pltpu.roll(wz, Z - 1, 1))
            wz_m = jnp.where(lanes == 0, 0.0, pltpu.roll(wz, 1, 1))
            transfer = (
                0.5 * (wxm - wxp),
                0.5 * (wy_m - wy_p),
                0.5 * (wz_m - wz_p),
            )
            inv_mu = invs[0, i]
            inv_lam = invs[1, i]
            residual_mu = sd_ref[i] - damage_part
            new_upd = keep * upd[0, i] + gain * inv_mu * residual_mu
            new_mu = mu + new_upd
            upd[0, i] = new_upd
            lams = []
            for c in range(3):
                lam = sfr[r, 1 + c, i + 1]
                ls = sides(lam, sfr[r, 1 + c, i + 2], sfr[r, 1 + c, i],
                           syl[r, 1 + c, i], syh[r, 1 + c, i])
                disp = MASS_SHIFT * lam + STIFF_SCALE * sum(
                    fs[k] * (lam - ls[k]) for k in range(6))
                residual = sdisp_ref[c, i] - (disp + transfer[c])
                nu = keep * upd[1 + c, i] + gain * inv_lam * residual
                upd[1 + c, i] = nu
                lams.append(lam + nu)
            if not last:
                sfr[r + 1, 0, i + 1] = new_mu
                for c in range(3):
                    sfr[r + 1, 1 + c, i + 1] = lams[c]
            else:
                out_mu_ref[i] = new_mu
                _, ds = damage_sides(i)
                grad = [0.5 * (ds[0] - ds[1]), 0.5 * (ds[2] - ds[3]), 0.5 * (ds[4] - ds[5])]
                length = jnp.sqrt(jnp.maximum(
                    grad[0] * grad[0] + grad[1] * grad[1] + grad[2] * grad[2], NORMAL_FLOOR))
                normal = [g / length for g in grad]
                size = normal[0] * normal[0] + normal[1] * normal[1] + normal[2] * normal[2]
                along = normal[0] * lams[0] + normal[1] * lams[1] + normal[2] * lams[2]
                a = RELAX_STEP / RELAX_INNER
                factor = 1.0 - a * (1.0 + NORMAL_WEIGHT * size)
                power = factor
                for _ in range(3):
                    power = power * power
                total = power
                work = bw_ref[0, 0]
                for level in range(2, 5):
                    total = jnp.where(work >= level, total * power, total)
                pull = NORMAL_WEIGHT * (1.0 - total) / (1.0 + NORMAL_WEIGHT * size)
                for c in range(3):
                    out_disp_ref[c, i] = lams[c] - (pull * along) * normal[c]
            return carry

        lax.fori_loop(1, X - 1, step, 0)
        arrive(copies, (0, 1))
        for i in (0, X - 1):
            step(i, 0)

    for copies in pending:
        sent(copies)


def body(damage, strain, seed_damage, seed_disp, brick_work, nx, ny):
    X, Y, Z = damage.shape
    f32 = jnp.float32
    vmem = pl.BlockSpec(memory_space=pltpu.VMEM)
    state = pl.pallas_call(
        functools.partial(kernel, nx, ny),
        out_shape=(
            jax.ShapeDtypeStruct((X, Y, Z), f32),
            jax.ShapeDtypeStruct((3, X, Y, Z), f32),
        ),
        in_specs=[pl.BlockSpec(memory_space=pltpu.SMEM)] + [pl.BlockSpec(memory_space=pl.ANY)] * 4,
        out_specs=(vmem, vmem),
        scratch_shapes=[
            pltpu.VMEM((2, X + 2, Y, Z), f32),
            pltpu.VMEM((2, X, 1, Z), f32),
            pltpu.VMEM((2, X, 1, Z), f32),
            pltpu.VMEM((SWEEPS, 4, X + 2, Y, Z), f32),
            pltpu.VMEM((SWEEPS, 4, X, 1, Z), f32),
            pltpu.VMEM((SWEEPS, 4, X, 1, Z), f32),
            pltpu.VMEM((6, X, Y, Z), f32),
            pltpu.VMEM((4, X, Y, Z), f32),
            pltpu.VMEM((3, X, Y, Z), f32),
            pltpu.SemaphoreType.DMA((2 + SWEEPS, 4)),
            pltpu.SemaphoreType.DMA((2 + SWEEPS, 4)),
            pltpu.VMEM((X, Y, Z), f32),
            pltpu.VMEM((3, X, Y, Z), f32),
            pltpu.VMEM((X, Y, Z), f32),
            pltpu.VMEM((3, X, Y, Z), f32),
            pltpu.SemaphoreType.DMA((4,)),
        ],
        compiler_params=pltpu.CompilerParams(
            collective_id=0, has_side_effects=True, vmem_limit_bytes=60 * 1024 * 1024
        ),
    )(brick_work, damage, strain, seed_damage, seed_disp)
    return pl.pallas_call(
        pass_kernel,
        out_shape=(
            jax.ShapeDtypeStruct((X, Y, Z), f32),
            jax.ShapeDtypeStruct((3, X, Y, Z), f32),
        ),
        in_specs=[pl.BlockSpec(memory_space=pl.ANY)] * 2,
        out_specs=(vmem, vmem),
        scratch_shapes=[pltpu.SemaphoreType.DMA((2,))],
    )(*state)


def pass_kernel(mu_ref, disp_ref, out_mu_ref, out_disp_ref, sems):
    copies = [
        pltpu.make_async_copy(mu_ref, out_mu_ref, sems.at[0]),
        pltpu.make_async_copy(disp_ref, out_disp_ref, sems.at[1]),
    ]
    for copy in copies:
        copy.start()
    for copy in copies:
        copy.wait()


def solution(mesh):
    nx = mesh.shape["gx"]
    ny = mesh.shape["gy"]
    placed = (
        P("gx", "gy", None),
        P(None, "gx", "gy", None),
        P("gx", "gy", None),
        P(None, "gx", "gy", None),
        P("gx", "gy"),
    )
    return jax.shard_map(
        functools.partial(body, nx=nx, ny=ny),
        mesh=mesh,
        in_specs=placed,
        out_specs=(P("gx", "gy", None), P(None, "gx", "gy", None)),
        check_vma=False,
    )
```

```python
import functools

import jax
import jax.numpy as jnp
from jax import lax
from jax.experimental import pallas as pl
from jax.experimental.pallas import tpu as pltpu
from jax.sharding import PartitionSpec as P

SWEEPS = 3
RELAX_INNER = 8

RESIDUAL_STIFFNESS = 0.001
TOUGH_OVER_LENGTH = 0.5
TOUGH_TIMES_LENGTH = 0.25
MASS_SHIFT = 0.5
STIFF_SCALE = 0.25
CENTER_VALUE = 1.0
HALF_WIDTH = 0.75
NORMAL_WEIGHT = 1.5
RELAX_STEP = 0.5
NORMAL_FLOOR = 0.05

MESH = pl.DeviceIdType.MESH


def soft_of(d):
    return (1.0 - d) ** 2


def kernel(
    nx, ny,
    bw_ref, dmg_hbm, strain_hbm, sd_hbm, sdisp_hbm,
    out_mu_ref, out_disp_ref,
    dfr, dyl, dyh, sfr, syl, syh, faces, upd, invs, send_sem, recv_sem,
    dmg_ref, strain_ref, sd_ref, sdisp_ref, load_sem,
):
    X, Y, Z = dmg_ref.shape
    bx = lax.axis_index("gx")
    by = lax.axis_index("gy")
    has = (bx < nx - 1, bx > 0, by < ny - 1, by > 0)
    peers = ((bx + 1, by), (bx - 1, by), (bx, by + 1), (bx, by - 1))

    @pl.when(bx == 0)
    def _():
        dfr[:, 0] = jnp.zeros((2, Y, Z), jnp.float32)
        sfr[:, :, 0] = jnp.zeros((SWEEPS, 4, Y, Z), jnp.float32)

    @pl.when(bx == nx - 1)
    def _():
        dfr[:, X + 1] = jnp.zeros((2, Y, Z), jnp.float32)
        sfr[:, :, X + 1] = jnp.zeros((SWEEPS, 4, Y, Z), jnp.float32)

    @pl.when(by == 0)
    def _():
        dyl[...] = jnp.zeros(dyl.shape, jnp.float32)
        syl[...] = jnp.zeros(syl.shape, jnp.float32)

    @pl.when(by == ny - 1)
    def _():
        dyh[...] = jnp.zeros(dyh.shape, jnp.float32)
        syh[...] = jnp.zeros(syh.shape, jnp.float32)

    barrier = pltpu.get_barrier_semaphore()
    count = jnp.int32(0)
    for d in range(4):
        @pl.when(has[d])
        def _():
            pl.semaphore_signal(barrier, inc=1, device_id=peers[d], device_id_type=MESH)
        count = count + has[d].astype(jnp.int32)
    loads = [
        pltpu.make_async_copy(src, dst, load_sem.at[k])
        for k, (src, dst) in enumerate(((dmg_hbm, dmg_ref), (strain_hbm, strain_ref),
                                        (sd_hbm, sd_ref), (sdisp_hbm, sdisp_ref)))
    ]
    for copy in loads:
        copy.start()
    for copy in loads:
        copy.wait()
    pl.semaphore_wait(barrier, count)

    def exchange(slot, routes):
        copies = []
        for d in range(4):
            src, dst = routes[d]
            copies.append(
                pltpu.make_async_remote_copy(
                    src_ref=src, dst_ref=dst,
                    send_sem=send_sem.at[slot, d], recv_sem=recv_sem.at[slot, d],
                    device_id=peers[d], device_id_type=MESH,
                )
            )
        for d in range(4):
            @pl.when(has[d])
            def _():
                copies[d].start()
        return copies

    def arrive(copies, dirs):
        opposite = (1, 0, 3, 2)
        for d in dirs:
            @pl.when(has[opposite[d]])
            def _():
                copies[d].wait_recv()

    def sent(copies):
        for d in range(4):
            @pl.when(has[d])
            def _():
                copies[d].wait_send()

    c_dmg = exchange(0, (
        (dmg_ref.at[X - 1:X], dfr.at[0, 0:1]),
        (dmg_ref.at[0:1], dfr.at[0, X + 1:X + 2]),
        (dmg_ref.at[:, Y - 1:Y], dyl.at[0]),
        (dmg_ref.at[:, 0:1], dyh.at[0]),
    ))
    c_str = exchange(1, (
        (strain_ref.at[0, X - 1:X], dfr.at[1, 0:1]),
        (strain_ref.at[0, 0:1], dfr.at[1, X + 1:X + 2]),
        (strain_ref.at[1, :, Y - 1:Y], dyl.at[1]),
        (strain_ref.at[1, :, 0:1], dyh.at[1]),
    ))
    dfr[0, 1:X + 1] = dmg_ref[...]
    dfr[1, 1:X + 1] = strain_ref[0]
    arrive(c_dmg, (2, 3))
    arrive(c_str, (2, 3))
    pending = [c_dmg, c_str]

    rows = lax.broadcasted_iota(jnp.int32, (Y, Z), 0)
    lanes = lax.broadcasted_iota(jnp.int32, (Y, Z), 1)

    def sides(center, nxp, nxm, lo, hi):
        yp = jnp.where(rows == Y - 1, hi, pltpu.roll(center, Y - 1, 0))
        ym = jnp.where(rows == 0, lo, pltpu.roll(center, 1, 0))
        zp = jnp.where(lanes == Z - 1, 0.0, pltpu.roll(center, Z - 1, 1))
        zm = jnp.where(lanes == 0, 0.0, pltpu.roll(center, 1, 1))
        return [nxp, nxm, yp, ym, zp, zm]

    def damage_sides(i):
        d = dfr[0, i + 1]
        return d, sides(d, dfr[0, i + 2], dfr[0, i], dyl[0, i], dyh[0, i])

    def prep(i, carry):
        d, ds = damage_sides(i)
        soft_center = soft_of(d) + RESIDUAL_STIFFNESS
        fs = [0.5 * (soft_center + soft_of(s) + RESIDUAL_STIFFNESS) for s in ds]
        total = fs[0]
        for k in range(6):
            faces[k, i] = fs[k]
            if k:
                total = total + fs[k]
        sx = strain_ref[0, i]
        sy = strain_ref[1, i]
        sz = strain_ref[2, i]
        energy = 0.5 * (sx * sx + sy * sy + sz * sz)
        inv_mu = 1.0 / (TOUGH_OVER_LENGTH + 2.0 * energy + 6.0 * TOUGH_TIMES_LENGTH)
        inv_lam = 1.0 / (MASS_SHIFT + STIFF_SCALE * total)
        invs[0, i] = inv_mu
        invs[1, i] = inv_lam
        invs[2, i] = TOUGH_OVER_LENGTH + 2.0 * energy
        mu0 = inv_mu * sd_ref[i] / CENTER_VALUE
        upd[0, i] = mu0
        sfr[0, 0, i + 1] = mu0
        for c in range(3):
            lam0 = inv_lam * sdisp_ref[c, i] / CENTER_VALUE
            upd[1 + c, i] = lam0
            sfr[0, 1 + c, i + 1] = lam0
        return carry

    lax.fori_loop(1, X - 1, prep, 0)
    arrive(c_dmg, (0, 1))
    arrive(c_str, (0, 1))
    for i in (0, X - 1):
        prep(i, 0)

    def state_routes(r):
        return (
            (sfr.at[r, :, X:X + 1], sfr.at[r, :, 0:1]),
            (sfr.at[r, :, 1:2], sfr.at[r, :, X + 1:X + 2]),
            (sfr.at[r, :, 1:X + 1, Y - 1:Y], syl.at[r]),
            (sfr.at[r, :, 1:X + 1, 0:1], syh.at[r]),
        )

    ratio = CENTER_VALUE / HALF_WIDTH
    rho = 1.0 / ratio
    for sweep in range(SWEEPS):
        r = sweep
        copies = exchange(2 + r, state_routes(r))
        pending.append(copies)
        arrive(copies, (2, 3))
        rho_next = 1.0 / (2.0 * ratio - rho)
        keep = rho_next * rho
        gain = 2.0 * rho_next / HALF_WIDTH
        rho = rho_next
        last = sweep == SWEEPS - 1

        def step(i, carry, r=r, keep=keep, gain=gain, last=last):
            mu = sfr[r, 0, i + 1]
            mus = sides(mu, sfr[r, 0, i + 2], sfr[r, 0, i], syl[r, 0, i], syh[r, 0, i])
            energy_diag = invs[2, i]
            damage_part = energy_diag * mu + TOUGH_TIMES_LENGTH * sum(mu - s for s in mus)
            fs = [faces[k, i] for k in range(6)]
            wxm = 2.0 * (dfr[0, i] - 1.0) * dfr[1, i] * mus[1]
            wxp = 2.0 * (dfr[0, i + 2] - 1.0) * dfr[1, i + 2] * mus[0]
            d = dfr[0, i + 1]
            wy = 2.0 * (d - 1.0) * strain_ref[1, i] * mu
            wy_lo = 2.0 * (dyl[0, i] - 1.0) * dyl[1, i] * syl[r, 0, i]
            wy_hi = 2.0 * (dyh[0, i] - 1.0) * dyh[1, i] * syh[r, 0, i]
            wy_p = jnp.where(rows == Y - 1, wy_hi, pltpu.roll(wy, Y - 1, 0))
            wy_m = jnp.where(rows == 0, wy_lo, pltpu.roll(wy, 1, 0))
            wz = 2.0 * (d - 1.0) * strain_ref[2, i] * mu
            wz_p = jnp.where(lanes == Z - 1, 0.0, pltpu.roll(wz, Z - 1, 1))
            wz_m = jnp.where(lanes == 0, 0.0, pltpu.roll(wz, 1, 1))
            transfer = (
                0.5 * (wxm - wxp),
                0.5 * (wy_m - wy_p),
                0.5 * (wz_m - wz_p),
            )
            inv_mu = invs[0, i]
            inv_lam = invs[1, i]
            residual_mu = sd_ref[i] - damage_part
            new_upd = keep * upd[0, i] + gain * inv_mu * residual_mu
            new_mu = mu + new_upd
            upd[0, i] = new_upd
            lams = []
            for c in range(3):
                lam = sfr[r, 1 + c, i + 1]
                ls = sides(lam, sfr[r, 1 + c, i + 2], sfr[r, 1 + c, i],
                           syl[r, 1 + c, i], syh[r, 1 + c, i])
                disp = MASS_SHIFT * lam + STIFF_SCALE * sum(
                    fs[k] * (lam - ls[k]) for k in range(6))
                residual = sdisp_ref[c, i] - (disp + transfer[c])
                nu = keep * upd[1 + c, i] + gain * inv_lam * residual
                upd[1 + c, i] = nu
                lams.append(lam + nu)
            if not last:
                sfr[r + 1, 0, i + 1] = new_mu
                for c in range(3):
                    sfr[r + 1, 1 + c, i + 1] = lams[c]
            else:
                out_mu_ref[i] = new_mu
                _, ds = damage_sides(i)
                grad = [0.5 * (ds[0] - ds[1]), 0.5 * (ds[2] - ds[3]), 0.5 * (ds[4] - ds[5])]
                length = jnp.sqrt(jnp.maximum(
                    grad[0] * grad[0] + grad[1] * grad[1] + grad[2] * grad[2], NORMAL_FLOOR))
                normal = [g / length for g in grad]
                size = normal[0] * normal[0] + normal[1] * normal[1] + normal[2] * normal[2]
                along = normal[0] * lams[0] + normal[1] * lams[1] + normal[2] * lams[2]
                a = RELAX_STEP / RELAX_INNER
                factor = 1.0 - a * (1.0 + NORMAL_WEIGHT * size)
                power = factor
                for _ in range(3):
                    power = power * power
                total = power
                work = bw_ref[0, 0]
                for level in range(2, 5):
                    total = jnp.where(work >= level, total * power, total)
                pull = NORMAL_WEIGHT * (1.0 - total) / (1.0 + NORMAL_WEIGHT * size)
                for c in range(3):
                    out_disp_ref[c, i] = lams[c] - (pull * along) * normal[c]
            return carry

        lax.fori_loop(1, X - 1, step, 0)
        arrive(copies, (0, 1))
        for i in (0, X - 1):
            step(i, 0)

    for copies in pending:
        sent(copies)


def body(damage, strain, seed_damage, seed_disp, brick_work, nx, ny):
    X, Y, Z = damage.shape
    f32 = jnp.float32
    vmem = pl.BlockSpec(memory_space=pltpu.VMEM)
    state = pl.pallas_call(
        functools.partial(kernel, nx, ny),
        out_shape=(
            jax.ShapeDtypeStruct((X, Y, Z), f32),
            jax.ShapeDtypeStruct((3, X, Y, Z), f32),
        ),
        in_specs=[pl.BlockSpec(memory_space=pltpu.SMEM)] + [pl.BlockSpec(memory_space=pl.ANY)] * 4,
        out_specs=(vmem, vmem),
        scratch_shapes=[
            pltpu.VMEM((2, X + 2, Y, Z), f32),
            pltpu.VMEM((2, X, 1, Z), f32),
            pltpu.VMEM((2, X, 1, Z), f32),
            pltpu.VMEM((SWEEPS, 4, X + 2, Y, Z), f32),
            pltpu.VMEM((SWEEPS, 4, X, 1, Z), f32),
            pltpu.VMEM((SWEEPS, 4, X, 1, Z), f32),
            pltpu.VMEM((6, X, Y, Z), f32),
            pltpu.VMEM((4, X, Y, Z), f32),
            pltpu.VMEM((3, X, Y, Z), f32),
            pltpu.SemaphoreType.DMA((2 + SWEEPS, 4)),
            pltpu.SemaphoreType.DMA((2 + SWEEPS, 4)),
            pltpu.VMEM((X, Y, Z), f32),
            pltpu.VMEM((3, X, Y, Z), f32),
            pltpu.VMEM((X, Y, Z), f32),
            pltpu.VMEM((3, X, Y, Z), f32),
            pltpu.SemaphoreType.DMA((4,)),
        ],
        compiler_params=pltpu.CompilerParams(
            collective_id=0, has_side_effects=True, vmem_limit_bytes=60 * 1024 * 1024
        ),
    )(brick_work, damage, strain, seed_damage, seed_disp)
    return pl.pallas_call(
        pass_kernel,
        out_shape=(
            jax.ShapeDtypeStruct((X, Y, Z), f32),
            jax.ShapeDtypeStruct((3, X, Y, Z), f32),
        ),
        in_specs=[pl.BlockSpec(memory_space=pl.ANY)] * 2,
        out_specs=(vmem, vmem),
        scratch_shapes=[pltpu.SemaphoreType.DMA((4,))],
    )(*state)


def pass_kernel(mu_ref, disp_ref, out_mu_ref, out_disp_ref, sems):
    copies = [pltpu.make_async_copy(mu_ref, out_mu_ref, sems.at[0])] + [
        pltpu.make_async_copy(disp_ref.at[c], out_disp_ref.at[c], sems.at[1 + c]) for c in range(3)
    ]
    for copy in copies:
        copy.start()
    for copy in copies:
        copy.wait()


def solution(mesh):
    nx = mesh.shape["gx"]
    ny = mesh.shape["gy"]
    placed = (
        P("gx", "gy", None),
        P(None, "gx", "gy", None),
        P("gx", "gy", None),
        P(None, "gx", "gy", None),
        P("gx", "gy"),
    )
    return jax.shard_map(
        functools.partial(body, nx=nx, ny=ny),
        mesh=mesh,
        in_specs=placed,
        out_specs=(P("gx", "gy", None), P(None, "gx", "gy", None)),
        check_vma=False,
    )
```
